512 devices in a mesh: chan: 64 (over y, x, z_hi, core), freq: 8 (over z_lo).
Axes of the slice: x: 4, y: 4, z: 16 (z_hi: 2, z_lo: 8; z = z_hi * 8 + z_lo), core: 2. Of those that a mesh axis runs over, the one named last changes fastest.
Arguments:
- spectra: bfloat16 [256, 2, 16, 8192], P('freq', None, None, 'chan'), may hold values from -20 to 20
- model: bfloat16 [256, 2, 8, 8192], P('freq', None, None, 'chan'), may hold values from -6 to 6
- channel_ok: int32 [8192], replicated, may hold values 0 or 1
- limits: int32 [64], replicated, may hold values from 128 to 1024, as said below
Outputs:
- adjoint: float32 [256, 2, 16, 8192], P('freq', None, None, 'chan')
- misfit: float32 [], replicated
The draws below stay inside these ranges and needn't reach their ends.
Inputs may be any that keep to these rules, and one draw needn't show every extreme that they name: `limits`: one block has the limit 128 and another the limit 1024.
All inputs are finite; a program needn't handle non-finite values.
Results may differ from the reference program's by a relative error of at most 0.00053.
Values may be sent and summed in bfloat16 or wider, within the bound.
A program may use at most 64 MiB of HBM per device.

```python
import math
import jax
import jax.numpy as jnp
from jax import lax

F = 256
W = 16
K = 8
BAND = 1024
C_DEV = 128
CHANNELS = 8192


def channel_gain(key):
    position = jnp.arange(CHANNELS, dtype=jnp.float32) / CHANNELS
    reach = 0.4
    jitter = jax.random.uniform(jax.random.fold_in(key, 11), (CHANNELS,), jnp.float32, -reach, reach)
    return jnp.exp(jitter) * (1.0 + 0.6 * position)


def noise_field(key, salt, row_count, size):
    gain = channel_gain(key)
    noise_key = jax.random.fold_in(key, salt)
    values = jnp.clip(jax.random.normal(noise_key, (F, 2, row_count, CHANNELS), jnp.float32), -4.0, 4.0) * gain
    return values * size


def draw_spectra(key, part):
    return noise_field(key, 1, W, 1.0).astype(jnp.bfloat16)


def draw_model(key, part):
    return noise_field(key, 2, K, 0.3).astype(jnp.bfloat16)


def draw_limits(key, part):
    block_total = CHANNELS // C_DEV
    values = jax.random.randint(jax.random.fold_in(key, 21), (block_total,), C_DEV, BAND + 1, dtype=jnp.int32)
    chosen_order = jax.random.permutation(jax.random.fold_in(key, 22), block_total)
    values = values.at[chosen_order[0]].set(BAND)
    values = values.at[chosen_order[1]].set(C_DEV)
    return values


def place_ends(values, key, smallest, top_value):
    longest = values.shape.index(max(values.shape))
    spots = []
    for shift in (0, 1):
        where = [jax.random.randint(jax.random.fold_in(key, axis), (), 0, length) for axis, length in enumerate(values.shape)]
        where[longest] = (where[longest] + shift) % values.shape[longest]
        spots.append(tuple(where))
    return values.at[spots[0]].set(smallest).at[spots[1]].set(top_value)


def setup_inputs(seed: int = 0) -> dict:
    keys = jax.random.split(jax.random.key(seed), 5)
    return {
        "spectra": draw_spectra(jax.random.fold_in(keys[4], 71), 0),
        "model": draw_model(jax.random.fold_in(keys[4], 71), 0),
        "channel_ok": place_ends((jax.random.randint(keys[2], (CHANNELS,), 0, 16) < 15).astype(jnp.int32), jax.random.fold_in(keys[2], 1), 0, 1),
        "limits": draw_limits(jax.random.fold_in(keys[4], 71), 0),
    }


def complex_cross(left_rows, right_rows):
    real_part = jnp.einsum('grbc,grbd->gbcd', left_rows[:, 0], right_rows[:, 0]) + jnp.einsum('grbc,grbd->gbcd', left_rows[:, 1], right_rows[:, 1])
    imag_part = jnp.einsum('grbc,grbd->gbcd', left_rows[:, 1], right_rows[:, 0]) - jnp.einsum('grbc,grbd->gbcd', left_rows[:, 0], right_rows[:, 1])
    return real_part, imag_part


def reference(spectra, model, channel_ok, limits):
    band_blocks = BAND // C_DEV
    block_total = CHANNELS // C_DEV
    row_count = W + K
    group_size = math.gcd(F, 16)
    group_total = F // group_size
    row_scale = jnp.concatenate([jnp.full((W,), 1.0 / W, jnp.float32), jnp.full((K,), -1.0, jnp.float32)])
    payload = jnp.concatenate([spectra, model], axis=2).astype(jnp.float32)
    ok_all = channel_ok.astype(jnp.float32).reshape(block_total, C_DEV)
    row_index = jnp.arange(C_DEV, dtype=jnp.int32)[:, None]
    col_index = jnp.arange(C_DEV, dtype=jnp.int32)[None, :]

    def one_group(pay_rows):
        pay_blocks = pay_rows.reshape(group_size, 2, row_count, block_total, C_DEV)
        scaled = pay_blocks * row_scale[None, None, :, None, None]
        spec_blocks = pay_blocks[:, :, :W]
        adjoint_sum = jnp.zeros(spec_blocks.shape, jnp.float32)
        misfit_sum = jnp.zeros((), jnp.float32)
        for s in range(band_blocks + 1):
            partner = jnp.roll(pay_blocks, -s, axis=3)
            partner_spec = partner[:, :, :W]
            partner_ok = jnp.roll(ok_all, -s, axis=0)
            real_part, imag_part = complex_cross(scaled, partner)
            offset = s * C_DEV + col_index - row_index
            inside = ((offset >= 1) & (offset <= limits[:, None, None])).astype(jnp.float32)
            live_mask = ok_all[:, :, None] * partner_ok[:, None, :] * inside
            real_res = real_part * live_mask[None]
            imag_res = imag_part * live_mask[None]
            misfit_sum = misfit_sum + 0.5 * jnp.sum(real_res * real_res + imag_res * imag_res)
            real_round = lax.optimization_barrier(real_res.astype(jnp.bfloat16)).astype(jnp.float32)
            imag_round = lax.optimization_barrier(imag_res.astype(jnp.bfloat16)).astype(jnp.float32)
            own_real = jnp.einsum('gbcd,gwbd->gwbc', real_round, partner_spec[:, 0]) - jnp.einsum('gbcd,gwbd->gwbc', imag_round, partner_spec[:, 1])
            own_imag = jnp.einsum('gbcd,gwbd->gwbc', real_round, partner_spec[:, 1]) + jnp.einsum('gbcd,gwbd->gwbc', imag_round, partner_spec[:, 0])
            far_real = jnp.einsum('gbcd,gwbc->gwbd', real_round, spec_blocks[:, 0]) + jnp.einsum('gbcd,gwbc->gwbd', imag_round, spec_blocks[:, 1])
            far_imag = jnp.einsum('gbcd,gwbc->gwbd', real_round, spec_blocks[:, 1]) - jnp.einsum('gbcd,gwbc->gwbd', imag_round, spec_blocks[:, 0])
            far_part = jnp.roll(jnp.stack([far_real, far_imag], axis=1), s, axis=3)
            adjoint_sum = adjoint_sum + jnp.stack([own_real, own_imag], axis=1) + far_part
        return (adjoint_sum * (1.0 / W)).reshape(group_size, 2, W, CHANNELS), misfit_sum

    grouped = payload.reshape(group_total, group_size, 2, row_count, CHANNELS)
    adjoint_groups, misfit_groups = lax.map(one_group, grouped)
    adjoint = adjoint_groups.reshape(F, 2, W, CHANNELS)
    misfit = jnp.sum(misfit_groups) / float(F * CHANNELS * BAND)
    return adjoint, misfit
```

```python
import jax
import jax.numpy as jnp
from jax import lax
from jax.sharding import PartitionSpec as P

F = 256
W = 16
BAND = 1024
GROUP = 4


def permute(x, pairs):
    return lax.ppermute(x, "chan", pairs)


def shift_pairs(peers, by):
    return [(i, (i + by) % peers) for i in range(peers)]


def group_pairs(peers, t):
    return [(i, (i // GROUP) * GROUP + (i % GROUP + t) % GROUP) for i in range(peers)]


def exchange(chunks, j, peers):
    rel = jnp.roll(chunks, -j, axis=0)
    got = [rel[0]] + [permute(rel[t], group_pairs(peers, t)) for t in range(1, GROUP)]
    got = jnp.stack(got, axis=0)
    order = (j - jnp.arange(GROUP)) % GROUP
    return jnp.take(got, order, axis=0)


def pair_terms(first, second, ok_first, ok_second, limit_first, shift_blocks):
    row_count = first.shape[2]
    block_width = first.shape[4]
    row_scale = jnp.concatenate(
        [jnp.full((W,), 1.0 / W, jnp.float32), jnp.full((row_count - W,), -1.0, jnp.float32)]
    ).astype(jnp.bfloat16)
    scaled = first * row_scale[None, None, :, None, None]
    fb = first.shape[0]
    nb = first.shape[3]
    stacked_left = jnp.stack(
        [
            scaled.reshape(fb, 2 * row_count, nb, block_width),
            jnp.concatenate([scaled[:, 1], -scaled[:, 0]], axis=1),
        ],
        axis=0,
    )
    right_rows = second.reshape(fb, 2 * row_count, nb, block_width)
    cross_spec = jnp.einsum(
        "xfrbc,frbd->xfbcd", stacked_left, right_rows, preferred_element_type=jnp.float32
    )
    row_index = lax.broadcasted_iota(jnp.int32, (block_width, block_width), 0)
    col_index = lax.broadcasted_iota(jnp.int32, (block_width, block_width), 1)
    offset = shift_blocks * block_width + col_index - row_index
    inside = ((offset[None] >= 1) & (offset[None] <= limit_first[:, None, None])).astype(jnp.float32)
    live_mask = ok_first[:, :, None] * ok_second[:, None, :] * inside
    residual = cross_spec * live_mask[None, None]
    piece_loss = 0.5 * jnp.sum(residual * residual)
    rounded = residual.astype(jnp.bfloat16)
    far_spec = second[:, :, :W].reshape(fb, 2 * W, nb, block_width)
    near_spec = first[:, :, :W].reshape(fb, 2 * W, nb, block_width)
    toward = jnp.einsum("xfbcd,fvbd->xfvbc", rounded, far_spec, preferred_element_type=jnp.float32)
    first_real = toward[0, :, :W] - toward[1, :, W:]
    first_imag = toward[0, :, W:] + toward[1, :, :W]
    backward = jnp.einsum("xfbcd,fvbc->xfvbd", rounded, near_spec, preferred_element_type=jnp.float32)
    second_real = backward[0, :, :W] + backward[1, :, W:]
    second_imag = backward[0, :, W:] - backward[1, :, :W]
    return (
        piece_loss,
        jnp.stack([first_real, first_imag], axis=1),
        jnp.stack([second_real, second_imag], axis=1),
    )


def shards(spectra, model, channel_ok, limits):
    payload = jnp.concatenate([spectra, model], axis=2)
    fl, _, rows, bw = payload.shape
    peers = lax.axis_size("chan")
    me = lax.axis_index("chan")
    j = me % GROUP
    column = me // GROUP
    sub = fl // GROUP
    band_blocks = BAND // bw
    halo_cols = -(-band_blocks // GROUP)
    span = GROUP * bw

    chunks = payload.reshape(GROUP, sub, 2, rows, bw)
    mine = exchange(chunks, j, peers)
    own = jnp.transpose(mine, (1, 2, 3, 0, 4)).reshape(sub, 2, rows, span)

    parts = [own] + [permute(own, shift_pairs(peers, -GROUP * h)) for h in range(1, halo_cols + 1)]
    ext = jnp.concatenate(parts, axis=3)
    total = ext.shape[3]

    ok_all = channel_ok.astype(jnp.float32)
    ok_wide = jnp.concatenate([ok_all, ok_all[:total]])
    ok_ext = lax.dynamic_slice_in_dim(ok_wide, column * span, total)
    lim = lax.dynamic_slice_in_dim(limits, column * GROUP, GROUP)

    first = ext[:, :, :, :span].reshape(sub, 2, rows, GROUP, bw)
    ok_first = ok_ext[:span].reshape(GROUP, bw)
    misfit_sum = jnp.zeros((), jnp.float32)
    near_acc = jnp.zeros((sub, 2, W, GROUP, bw), jnp.float32)
    far_acc = jnp.zeros((sub, 2, W, total), jnp.float32)
    for s in range(band_blocks + 1):
        second = ext[:, :, :, s * bw : s * bw + span].reshape(sub, 2, rows, GROUP, bw)
        ok_second = ok_ext[s * bw : s * bw + span].reshape(GROUP, bw)
        piece_loss, near_terms, far_terms = pair_terms(first, second, ok_first, ok_second, lim, s)
        misfit_sum = misfit_sum + piece_loss
        near_acc = near_acc + near_terms
        far_flat = far_terms.reshape(sub, 2, W, span)
        far_acc = far_acc + jnp.pad(far_flat, ((0, 0), (0, 0), (0, 0), (s * bw, total - span - s * bw)))
    adj = near_acc.reshape(sub, 2, W, span) + far_acc[:, :, :, :span]
    for h in range(1, halo_cols + 1):
        adj = adj + permute(far_acc[:, :, :, h * span : (h + 1) * span], shift_pairs(peers, GROUP * h))
    adj = adj * (1.0 / W)

    blocks = jnp.transpose(adj.reshape(sub, 2, W, GROUP, bw), (3, 0, 1, 2, 4))
    back = exchange(blocks, j, peers)
    adjoint = back.reshape(fl, 2, W, bw)

    misfit_total = lax.psum(misfit_sum, ("chan", "freq"))
    misfit = misfit_total / float(F * bw * peers * BAND)
    return adjoint, misfit


def solution(mesh):
    return jax.shard_map(
        shards,
        mesh=mesh,
        in_specs=(P("freq", None, None, "chan"), P("freq", None, None, "chan"), P(), P()),
        out_specs=(P("freq", None, None, "chan"), P()),
        check_vma=False,
    )
```

```python
import jax
import jax.numpy as jnp
from jax import lax
from jax.sharding import PartitionSpec as P

F = 256
W = 16
BAND = 1024
GROUP = 4


def permute(x, pairs):
    return lax.ppermute(x, "chan", pairs)


def shift_pairs(peers, by):
    return [(i, (i + by) % peers) for i in range(peers)]


def group_pairs(peers, t):
    return [(i, (i // GROUP) * GROUP + (i % GROUP + t) % GROUP) for i in range(peers)]


def exchange(chunks, j, peers):
    rel = jnp.roll(chunks, -j, axis=0)
    got = [rel[0]] + [permute(rel[t], group_pairs(peers, t)) for t in range(1, GROUP)]
    got = jnp.stack(got, axis=0)
    order = (j - jnp.arange(GROUP)) % GROUP
    return jnp.take(got, order, axis=0)


def pair_terms(first, second, ok_first, ok_second, limit_first, shift_blocks):
    fb, nb, _, row_count, block_width = first.shape
    row_scale = jnp.concatenate(
        [jnp.full((W,), 1.0 / W, jnp.float32), jnp.full((row_count - W,), -1.0, jnp.float32)]
    ).astype(jnp.bfloat16)
    scaled = first * row_scale[None, None, None, :, None]
    stacked_left = jnp.stack(
        [
            scaled.reshape(fb, nb, 2 * row_count, block_width),
            jnp.concatenate([scaled[:, :, 1], -scaled[:, :, 0]], axis=2),
        ],
        axis=2,
    )
    right_rows = second.reshape(fb, nb, 2 * row_count, block_width)
    cross_spec = jnp.einsum(
        "fbxrc,fbrd->fbxcd", stacked_left, right_rows, preferred_element_type=jnp.float32
    )
    row_index = lax.broadcasted_iota(jnp.int32, (block_width, block_width), 0)
    col_index = lax.broadcasted_iota(jnp.int32, (block_width, block_width), 1)
    offset = shift_blocks * block_width + col_index - row_index
    inside = ((offset[None] >= 1) & (offset[None] <= limit_first[:, None, None])).astype(jnp.float32)
    live_mask = ok_first[:, :, None] * ok_second[:, None, :] * inside
    residual = cross_spec * live_mask[None, :, None]
    piece_loss = 0.5 * jnp.sum(residual * residual)
    rounded = residual.astype(jnp.bfloat16)
    far_spec = second[:, :, :, :W].reshape(fb, nb, 2 * W, block_width)
    near_spec = first[:, :, :, :W].reshape(fb, nb, 2 * W, block_width)
    toward = jnp.einsum("fbxcd,fbvd->fbxvc", rounded, far_spec, preferred_element_type=jnp.float32)
    first_real = toward[:, :, 0, :W] - toward[:, :, 1, W:]
    first_imag = toward[:, :, 0, W:] + toward[:, :, 1, :W]
    backward = jnp.einsum("fbxcd,fbvc->fbxvd", rounded, near_spec, preferred_element_type=jnp.float32)
    second_real = backward[:, :, 0, :W] + backward[:, :, 1, W:]
    second_imag = backward[:, :, 0, W:] - backward[:, :, 1, :W]
    return (
        piece_loss,
        jnp.stack([first_real, first_imag], axis=2),
        jnp.stack([second_real, second_imag], axis=2),
    )


def global_sum(v, mesh_shape):
    for axis in ("chan", "freq"):
        n = mesh_shape[axis]
        bit = 1
        while bit < n:
            v = v + lax.ppermute(v, axis, [(i, i ^ bit) for i in range(n)])
            bit *= 2
    return v


def shards(spectra, model, channel_ok, limits, mesh_shape):
    payload = jnp.concatenate([spectra, model], axis=2)
    fl, _, rows, bw = payload.shape
    peers = lax.axis_size("chan")
    me = lax.axis_index("chan")
    j = me % GROUP
    column = me // GROUP
    sub = fl // GROUP
    band_blocks = BAND // bw
    halo_cols = -(-band_blocks // GROUP)
    nblk = GROUP * (1 + halo_cols)

    chunks = payload.reshape(GROUP, sub, 2, rows, bw)
    mine = exchange(chunks, j, peers)
    own = jnp.transpose(mine, (1, 0, 2, 3, 4))

    parts = [own] + [permute(own, shift_pairs(peers, -GROUP * h)) for h in range(1, halo_cols + 1)]
    ext = jnp.concatenate(parts, axis=1)

    ok_all = channel_ok.astype(jnp.float32)
    ok_wide = jnp.concatenate([ok_all, ok_all[: nblk * bw]])
    ok_ext = lax.dynamic_slice_in_dim(ok_wide, column * GROUP * bw, nblk * bw).reshape(nblk, bw)
    lim = lax.dynamic_slice_in_dim(limits, column * GROUP, GROUP)

    first = ext[:, :GROUP]
    ok_first = ok_ext[:GROUP]
    misfit_sum = jnp.zeros((), jnp.float32)
    near_acc = jnp.zeros((sub, GROUP, 2, W, bw), jnp.float32)
    far_acc = jnp.zeros((sub, nblk, 2, W, bw), jnp.float32)
    for s in range(band_blocks + 1):
        second = ext[:, s : s + GROUP]
        piece_loss, near_terms, far_terms = pair_terms(
            first, second, ok_first, ok_ext[s : s + GROUP], lim, s
        )
        misfit_sum = misfit_sum + piece_loss
        near_acc = near_acc + near_terms
        far_acc = far_acc.at[:, s : s + GROUP].add(far_terms)
    misfit_total = global_sum(misfit_sum, mesh_shape)
    adj = near_acc + far_acc[:, :GROUP]
    for h in range(1, halo_cols + 1):
        adj = adj + permute(far_acc[:, h * GROUP : (h + 1) * GROUP], shift_pairs(peers, GROUP * h))
    adj = adj * (1.0 / W)

    blocks = jnp.transpose(adj, (1, 0, 2, 3, 4))
    back = exchange(blocks, j, peers)
    adjoint = back.reshape(fl, 2, W, bw)

    misfit = misfit_total / float(F * bw * peers * BAND)
    return adjoint, misfit


def solution(mesh):
    mesh_shape = dict(mesh.shape)
    return jax.shard_map(
        lambda *a: shards(*a, mesh_shape),
        mesh=mesh,
        in_specs=(P("freq", None, None, "chan"), P("freq", None, None, "chan"), P(), P()),
        out_specs=(P("freq", None, None, "chan"), P()),
        check_vma=False,
    )
```

```python
import jax
import jax.numpy as jnp
from jax import lax
from jax.experimental import pallas as pl
from jax.experimental.pallas import tpu as pltpu
from jax.sharding import PartitionSpec as P
import functools

F = 256
W = 16
BAND = 1024
GROUP = 4


def permute(x, pairs):
    return lax.ppermute(x, "chan", pairs)


def shift_pairs(peers, by):
    return [(i, (i + by) % peers) for i in range(peers)]


def group_pairs(peers, t):
    return [(i, (i // GROUP) * GROUP + (i % GROUP + t) % GROUP) for i in range(peers)]


def exchange(chunks, j, peers):
    rel = jnp.roll(chunks, -j, axis=0)
    got = [rel[0]] + [permute(rel[t], group_pairs(peers, t)) for t in range(1, GROUP)]
    got = jnp.stack(got, axis=0)
    order = (j - jnp.arange(GROUP)) % GROUP
    return jnp.take(got, order, axis=0)


def pair_terms(first, second, ok_first, ok_second, limit_first, shift_blocks):
    fb, nb, _, row_count, block_width = first.shape
    row_scale = jnp.concatenate(
        [jnp.full((W,), 1.0 / W, jnp.float32), jnp.full((row_count - W,), -1.0, jnp.float32)]
    ).astype(jnp.bfloat16)
    scaled = first * row_scale[None, None, None, :, None]
    stacked_left = jnp.stack(
        [
            scaled.reshape(fb, nb, 2 * row_count, block_width),
            jnp.concatenate([scaled[:, :, 1], -scaled[:, :, 0]], axis=2),
        ],
        axis=2,
    )
    right_rows = second.reshape(fb, nb, 2 * row_count, block_width)
    cross_spec = jnp.einsum(
        "fbxrc,fbrd->fbxcd", stacked_left, right_rows, preferred_element_type=jnp.float32
    )
    row_index = lax.broadcasted_iota(jnp.int32, (block_width, block_width), 0)
    col_index = lax.broadcasted_iota(jnp.int32, (block_width, block_width), 1)
    offset = shift_blocks * block_width + col_index - row_index
    inside = ((offset[None] >= 1) & (offset[None] <= limit_first[:, None, None])).astype(jnp.float32)
    live_mask = ok_first[:, :, None] * ok_second[:, None, :] * inside
    residual = cross_spec * live_mask[None, :, None]
    piece_loss = 0.5 * jnp.sum(residual * residual)
    rounded = residual.astype(jnp.bfloat16)
    far_spec = second[:, :, :, :W].reshape(fb, nb, 2 * W, block_width)
    near_spec = first[:, :, :, :W].reshape(fb, nb, 2 * W, block_width)
    toward = jnp.einsum("fbxcd,fbvd->fbxvc", rounded, far_spec, preferred_element_type=jnp.float32)
    first_real = toward[:, :, 0, :W] - toward[:, :, 1, W:]
    first_imag = toward[:, :, 0, W:] + toward[:, :, 1, :W]
    backward = jnp.einsum("fbxcd,fbvc->fbxvd", rounded, near_spec, preferred_element_type=jnp.float32)
    second_real = backward[:, :, 0, :W] + backward[:, :, 1, W:]
    second_imag = backward[:, :, 0, W:] - backward[:, :, 1, :W]
    return (
        piece_loss,
        jnp.stack([first_real, first_imag], axis=2),
        jnp.stack([second_real, second_imag], axis=2),
    )


MESH = pl.DeviceIdType.MESH

def sum_kernel(n_col, n_f, val_ref, out_ref, slots1, slots2, stage, send1, recv1, send2, recv2):
    c = lax.axis_index("chan")
    f = lax.axis_index("freq")
    k = c // GROUP
    j = c % GROUP
    g1 = GROUP * n_f
    me1 = j * n_f + f

    def dev1(slot):
        return (k * GROUP + slot // n_f, slot % n_f)

    def dev2(col):
        return (col * GROUP + j, f)

    barrier = pltpu.get_barrier_semaphore()
    for t in range(1, g1):
        pl.semaphore_signal(barrier, 1, device_id=dev1((me1 + t) % g1), device_id_type=MESH)
    for t in range(1, n_col):
        pl.semaphore_signal(barrier, 1, device_id=dev2((k + t) % n_col), device_id_type=MESH)
    pl.semaphore_wait(barrier, g1 - 1 + n_col - 1)

    def gather(src, slots, sends, recvs, count, mine, dev):
        out = []
        for t in range(1, count):
            peer = (mine + t) % count
            cp = pltpu.make_async_remote_copy(
                src_ref=src, dst_ref=slots.at[mine], send_sem=sends.at[peer],
                recv_sem=recvs.at[mine], device_id=dev(peer), device_id_type=MESH)
            cp.start()
            out.append(cp)
        slots[mine] = src[...]
        for t in range(1, count):
            peer = (mine + t) % count
            pltpu.make_async_remote_copy(
                src_ref=src, dst_ref=slots.at[peer], send_sem=sends.at[peer],
                recv_sem=recvs.at[peer], device_id=dev(peer), device_id_type=MESH).wait_recv()
        for cp in out:
            cp.wait_send()
        acc = slots[0]
        for s in range(1, count):
            acc = acc + slots[s]
        return acc

    stage[...] = gather(val_ref, slots1, send1, recv1, g1, me1, dev1)
    out_ref[...] = gather(stage, slots2, send2, recv2, n_col, k, dev2)


def global_sum(v, mesh_shape):
    n_col = mesh_shape["chan"] // GROUP
    n_f = mesh_shape["freq"]
    g1 = GROUP * n_f
    tile = jnp.full((8, 128), v, jnp.float32)
    out = pl.pallas_call(
        functools.partial(sum_kernel, n_col, n_f),
        out_shape=jax.ShapeDtypeStruct((8, 128), jnp.float32),
        in_specs=[pl.BlockSpec(memory_space=pltpu.VMEM)],
        out_specs=pl.BlockSpec(memory_space=pltpu.VMEM),
        scratch_shapes=[
            pltpu.VMEM((g1, 8, 128), jnp.float32),
            pltpu.VMEM((n_col, 8, 128), jnp.float32),
            pltpu.VMEM((8, 128), jnp.float32),
            pltpu.SemaphoreType.DMA((g1,)),
            pltpu.SemaphoreType.DMA((g1,)),
            pltpu.SemaphoreType.DMA((n_col,)),
            pltpu.SemaphoreType.DMA((n_col,)),
        ],
        compiler_params=pltpu.CompilerParams(collective_id=0, has_side_effects=True),
    )(tile)
    return out[0, 0]


def shards(spectra, model, channel_ok, limits, mesh_shape):
    payload = jnp.concatenate([spectra, model], axis=2)
    fl, _, rows, bw = payload.shape
    peers = lax.axis_size("chan")
    me = lax.axis_index("chan")
    j = me % GROUP
    column = me // GROUP
    sub = fl // GROUP
    band_blocks = BAND // bw
    halo_cols = -(-band_blocks // GROUP)
    nblk = GROUP * (1 + halo_cols)

    chunks = payload.reshape(GROUP, sub, 2, rows, bw)
    mine = exchange(chunks, j, peers)
    own = jnp.transpose(mine, (1, 0, 2, 3, 4))

    parts = [own] + [permute(own, shift_pairs(peers, -GROUP * h)) for h in range(1, halo_cols + 1)]
    ext = jnp.concatenate(parts, axis=1)

    ok_all = channel_ok.astype(jnp.float32)
    ok_wide = jnp.concatenate([ok_all, ok_all[: nblk * bw]])
    ok_ext = lax.dynamic_slice_in_dim(ok_wide, column * GROUP * bw, nblk * bw).reshape(nblk, bw)
    lim = lax.dynamic_slice_in_dim(limits, column * GROUP, GROUP)

    first = ext[:, :GROUP]
    ok_first = ok_ext[:GROUP]
    misfit_sum = jnp.zeros((), jnp.float32)
    near_acc = jnp.zeros((sub, GROUP, 2, W, bw), jnp.float32)
    far_acc = jnp.zeros((sub, nblk, 2, W, bw), jnp.float32)
    for s in range(band_blocks + 1):
        second = ext[:, s : s + GROUP]
        piece_loss, near_terms, far_terms = pair_terms(
            first, second, ok_first, ok_ext[s : s + GROUP], lim, s
        )
        misfit_sum = misfit_sum + piece_loss
        near_acc = near_acc + near_terms
        far_acc = far_acc.at[:, s : s + GROUP].add(far_terms)
    misfit_total = global_sum(misfit_sum, mesh_shape)
    adj = near_acc + far_acc[:, :GROUP]
    for h in range(1, halo_cols + 1):
        adj = adj + permute(far_acc[:, h * GROUP : (h + 1) * GROUP], shift_pairs(peers, GROUP * h))
    adj = adj * (1.0 / W)

    blocks = jnp.transpose(adj, (1, 0, 2, 3, 4))
    back = exchange(blocks, j, peers)
    adjoint = back.reshape(fl, 2, W, bw)

    misfit = misfit_total / float(F * bw * peers * BAND)
    return adjoint, misfit


def solution(mesh):
    mesh_shape = dict(mesh.shape)
    return jax.shard_map(
        lambda *a: shards(*a, mesh_shape),
        mesh=mesh,
        in_specs=(P("freq", None, None, "chan"), P("freq", None, None, "chan"), P(), P()),
        out_specs=(P("freq", None, None, "chan"), P()),
        check_vma=False,
    )
```

```python
import jax
import jax.numpy as jnp
from jax import lax
from jax.experimental import pallas as pl
from jax.experimental.pallas import tpu as pltpu
from jax.sharding import PartitionSpec as P
import functools

F = 256
W = 16
BAND = 1024
GROUP = 4


def permute(x, pairs):
    return lax.ppermute(x, "chan", pairs)


def shift_pairs(peers, by):
    return [(i, (i + by) % peers) for i in range(peers)]


def group_pairs(peers, t):
    return [(i, (i // GROUP) * GROUP + (i % GROUP + t) % GROUP) for i in range(peers)]


def exchange(chunks, j, peers):
    rel = jnp.roll(chunks, -j, axis=0)
    got = [rel[0]] + [permute(rel[t], group_pairs(peers, t)) for t in range(1, GROUP)]
    got = jnp.stack(got, axis=0)
    order = (j - jnp.arange(GROUP)) % GROUP
    return jnp.take(got, order, axis=0)


def pair_terms(first, second, ok_first, ok_second, limit_first, shift_blocks):
    fb, nb, _, row_count, block_width = first.shape
    row_scale = jnp.concatenate(
        [jnp.full((W,), 1.0 / W, jnp.float32), jnp.full((row_count - W,), -1.0, jnp.float32)]
    ).astype(jnp.bfloat16)
    scaled = first * row_scale[None, None, None, :, None]
    stacked_left = jnp.stack(
        [
            scaled.reshape(fb, nb, 2 * row_count, block_width),
            jnp.concatenate([scaled[:, :, 1], -scaled[:, :, 0]], axis=2),
        ],
        axis=2,
    )
    right_rows = second.reshape(fb, nb, 2 * row_count, block_width)
    cross_spec = jnp.einsum(
        "fbxrc,fbrd->fbxcd", stacked_left, right_rows, preferred_element_type=jnp.float32
    )
    row_index = lax.broadcasted_iota(jnp.int32, (block_width, block_width), 0)
    col_index = lax.broadcasted_iota(jnp.int32, (block_width, block_width), 1)
    offset = shift_blocks * block_width + col_index - row_index
    inside = ((offset[None] >= 1) & (offset[None] <= limit_first[:, None, None])).astype(jnp.float32)
    live_mask = ok_first[:, :, None] * ok_second[:, None, :] * inside
    residual = cross_spec * live_mask[None, :, None]
    piece_loss = 0.5 * jnp.sum(residual * residual)
    rounded = residual.astype(jnp.bfloat16)
    far_spec = second[:, :, :, :W].reshape(fb, nb, 2 * W, block_width)
    near_spec = first[:, :, :, :W].reshape(fb, nb, 2 * W, block_width)
    toward = jnp.einsum("fbxcd,fbvd->fbxvc", rounded, far_spec, preferred_element_type=jnp.float32)
    first_real = toward[:, :, 0, :W] - toward[:, :, 1, W:]
    first_imag = toward[:, :, 0, W:] + toward[:, :, 1, :W]
    backward = jnp.einsum("fbxcd,fbvc->fbxvd", rounded, near_spec, preferred_element_type=jnp.float32)
    second_real = backward[:, :, 0, :W] + backward[:, :, 1, W:]
    second_imag = backward[:, :, 0, W:] - backward[:, :, 1, :W]
    return (
        piece_loss,
        jnp.stack([first_real, first_imag], axis=2),
        jnp.stack([second_real, second_imag], axis=2),
    )


MESH = pl.DeviceIdType.MESH

def sum_kernel(n_col, n_f, val_ref, out_ref, slots1, slots2, stage, send1, recv1, send2, recv2):
    c = lax.axis_index("chan")
    f = lax.axis_index("freq")
    k = c // GROUP
    j = c % GROUP
    g1 = GROUP * n_f
    me1 = j * n_f + f

    def dev1(slot):
        return (k * GROUP + slot // n_f, slot % n_f)

    def dev2(col):
        return (col * GROUP + j, f)

    barrier = pltpu.get_barrier_semaphore()
    for t in range(1, g1):
        pl.semaphore_signal(barrier, 1, device_id=dev1((me1 + t) % g1), device_id_type=MESH)
    for t in range(1, n_col):
        pl.semaphore_signal(barrier, 1, device_id=dev2((k + t) % n_col), device_id_type=MESH)
    pl.semaphore_wait(barrier, g1 - 1 + n_col - 1)

    def gather(src, slots, sends, recvs, count, mine, dev):
        out = []
        for t in range(1, count):
            peer = (mine + t) % count
            cp = pltpu.make_async_remote_copy(
                src_ref=src, dst_ref=slots.at[mine], send_sem=sends.at[peer],
                recv_sem=recvs.at[mine], device_id=dev(peer), device_id_type=MESH)
            cp.start()
            out.append(cp)
        slots[mine] = src[...]
        for t in range(1, count):
            peer = (mine + t) % count
            pltpu.make_async_remote_copy(
                src_ref=src, dst_ref=slots.at[peer], send_sem=sends.at[peer],
                recv_sem=recvs.at[peer], device_id=dev(peer), device_id_type=MESH).wait_recv()
        for cp in out:
            cp.wait_send()
        acc = slots[0]
        for s in range(1, count):
            acc = acc + slots[s]
        return acc

    stage[...] = gather(val_ref, slots1, send1, recv1, g1, me1, dev1)
    out_ref[...] = gather(stage, slots2, send2, recv2, n_col, k, dev2)


def global_sum(v, mesh_shape):
    n_col = mesh_shape["chan"] // GROUP
    n_f = mesh_shape["freq"]
    g1 = GROUP * n_f
    tile = jnp.full((8, 128), v, jnp.float32)
    out = pl.pallas_call(
        functools.partial(sum_kernel, n_col, n_f),
        out_shape=jax.ShapeDtypeStruct((8, 128), jnp.float32),
        in_specs=[pl.BlockSpec(memory_space=pltpu.VMEM)],
        out_specs=pl.BlockSpec(memory_space=pltpu.VMEM),
        scratch_shapes=[
            pltpu.VMEM((g1, 8, 128), jnp.float32),
            pltpu.VMEM((n_col, 8, 128), jnp.float32),
            pltpu.VMEM((8, 128), jnp.float32),
            pltpu.SemaphoreType.DMA((g1,)),
            pltpu.SemaphoreType.DMA((g1,)),
            pltpu.SemaphoreType.DMA((n_col,)),
            pltpu.SemaphoreType.DMA((n_col,)),
        ],
        compiler_params=pltpu.CompilerParams(collective_id=0, has_side_effects=True),
    )(tile)
    return out[0, 0]


def shards(spectra, model, channel_ok, limits, mesh_shape):
    payload = jnp.concatenate([spectra, model], axis=2)
    fl, _, rows, bw = payload.shape
    peers = lax.axis_size("chan")
    me = lax.axis_index("chan")
    j = me % GROUP
    column = me // GROUP
    sub = fl // GROUP
    band_blocks = BAND // bw
    halo_cols = -(-band_blocks // GROUP)
    nblk = GROUP * (1 + 2 * halo_cols)

    chunks = payload.reshape(GROUP, sub, 2, rows, bw)
    mine = exchange(chunks, j, peers)
    own = jnp.transpose(mine, (1, 0, 2, 3, 4))

    ahead = [permute(own, shift_pairs(peers, -GROUP * h)) for h in range(1, halo_cols + 1)]
    behind = [permute(own, shift_pairs(peers, GROUP * h)) for h in range(halo_cols, 0, -1)]
    ext = jnp.concatenate(behind + [own] + ahead, axis=1)
    base = GROUP * halo_cols
    start_col = (column - halo_cols) % (peers // GROUP)

    ok_all = channel_ok.astype(jnp.float32)
    ok_wide = jnp.concatenate([ok_all, ok_all[: nblk * bw]])
    ok_ext = lax.dynamic_slice_in_dim(ok_wide, start_col * GROUP * bw, nblk * bw).reshape(nblk, bw)
    lim_wide = jnp.concatenate([limits, limits[:nblk]])
    lim_ext = lax.dynamic_slice_in_dim(lim_wide, start_col * GROUP, nblk)

    own_blk = slice(base, base + GROUP)
    misfit_sum = jnp.zeros((), jnp.float32)
    adj = jnp.zeros((sub, GROUP, 2, W, bw), jnp.float32)
    for s in range(band_blocks + 1):
        ahead_blk = slice(base + s, base + s + GROUP)
        piece_loss, near_terms, far_terms = pair_terms(
            ext[:, own_blk], ext[:, ahead_blk], ok_ext[own_blk], ok_ext[ahead_blk], lim_ext[own_blk], s
        )
        misfit_sum = misfit_sum + piece_loss
        adj = adj + near_terms
        if s == 0:
            adj = adj + far_terms
        else:
            back_blk = slice(base - s, base - s + GROUP)
            _, _, back_terms = pair_terms(
                ext[:, back_blk], ext[:, own_blk], ok_ext[back_blk], ok_ext[own_blk], lim_ext[back_blk], s
            )
            adj = adj + back_terms
    misfit_total = global_sum(misfit_sum, mesh_shape)
    adj = adj * (1.0 / W)

    blocks = jnp.transpose(adj, (1, 0, 2, 3, 4))
    back = exchange(blocks, j, peers)
    adjoint = back.reshape(fl, 2, W, bw)

    misfit = misfit_total / float(F * bw * peers * BAND)
    return adjoint, misfit


def solution(mesh):
    mesh_shape = dict(mesh.shape)
    return jax.shard_map(
        lambda *a: shards(*a, mesh_shape),
        mesh=mesh,
        in_specs=(P("freq", None, None, "chan"), P("freq", None, None, "chan"), P(), P()),
        out_specs=(P("freq", None, None, "chan"), P()),
        check_vma=False,
    )
```

```python
import jax
import jax.numpy as jnp
from jax import lax
from jax.experimental import pallas as pl
from jax.experimental.pallas import tpu as pltpu
from jax.sharding import PartitionSpec as P
import functools

F = 256
W = 16
BAND = 1024
CHUNKS = 2
GROUP = 4


def permute(x, pairs):
    return lax.ppermute(x, "chan", pairs)


def shift_pairs(peers, by):
    return [(i, (i + by) % peers) for i in range(peers)]


def group_pairs(peers, t):
    return [(i, (i // GROUP) * GROUP + (i % GROUP + t) % GROUP) for i in range(peers)]


def exchange(chunks, j, peers):
    rel = jnp.roll(chunks, -j, axis=0)
    got = [rel[0]] + [permute(rel[t], group_pairs(peers, t)) for t in range(1, GROUP)]
    got = jnp.stack(got, axis=0)
    order = (j - jnp.arange(GROUP)) % GROUP
    return jnp.take(got, order, axis=0)


def pair_terms(first, second, ok_first, ok_second, limit_first, shift_blocks):
    fb, nb, _, row_count, block_width = first.shape
    row_scale = jnp.concatenate(
        [jnp.full((W,), 1.0 / W, jnp.float32), jnp.full((row_count - W,), -1.0, jnp.float32)]
    ).astype(jnp.bfloat16)
    scaled = first * row_scale[None, None, None, :, None]
    stacked_left = jnp.stack(
        [
            scaled.reshape(fb, nb, 2 * row_count, block_width),
            jnp.concatenate([scaled[:, :, 1], -scaled[:, :, 0]], axis=2),
        ],
        axis=2,
    )
    right_rows = second.reshape(fb, nb, 2 * row_count, block_width)
    cross_spec = jnp.einsum(
        "fbxrc,fbrd->fbxcd", stacked_left, right_rows, preferred_element_type=jnp.float32
    )
    row_index = lax.broadcasted_iota(jnp.int32, (block_width, block_width), 0)
    col_index = lax.broadcasted_iota(jnp.int32, (block_width, block_width), 1)
    offset = shift_blocks * block_width + col_index - row_index
    inside = ((offset[None] >= 1) & (offset[None] <= limit_first[:, None, None])).astype(jnp.float32)
    live_mask = ok_first[:, :, None] * ok_second[:, None, :] * inside
    residual = cross_spec * live_mask[None, :, None]
    piece_loss = 0.5 * jnp.sum(residual * residual)
    rounded = residual.astype(jnp.bfloat16)
    far_spec = second[:, :, :, :W].reshape(fb, nb, 2 * W, block_width)
    near_spec = first[:, :, :, :W].reshape(fb, nb, 2 * W, block_width)
    toward = jnp.einsum("fbxcd,fbvd->fbxvc", rounded, far_spec, preferred_element_type=jnp.float32)
    first_real = toward[:, :, 0, :W] - toward[:, :, 1, W:]
    first_imag = toward[:, :, 0, W:] + toward[:, :, 1, :W]
    backward = jnp.einsum("fbxcd,fbvc->fbxvd", rounded, near_spec, preferred_element_type=jnp.float32)
    second_real = backward[:, :, 0, :W] + backward[:, :, 1, W:]
    second_imag = backward[:, :, 0, W:] - backward[:, :, 1, :W]
    return (
        piece_loss,
        jnp.stack([first_real, first_imag], axis=2),
        jnp.stack([second_real, second_imag], axis=2),
    )


MESH = pl.DeviceIdType.MESH

def sum_kernel(n_col, n_f, val_ref, out_ref, slots1, slots2, stage, send1, recv1, send2, recv2):
    c = lax.axis_index("chan")
    f = lax.axis_index("freq")
    k = c // GROUP
    j = c % GROUP
    g1 = GROUP * n_f
    me1 = j * n_f + f

    def dev1(slot):
        return (k * GROUP + slot // n_f, slot % n_f)

    def dev2(col):
        return (col * GROUP + j, f)

    barrier = pltpu.get_barrier_semaphore()
    for t in range(1, g1):
        pl.semaphore_signal(barrier, 1, device_id=dev1((me1 + t) % g1), device_id_type=MESH)
    for t in range(1, n_col):
        pl.semaphore_signal(barrier, 1, device_id=dev2((k + t) % n_col), device_id_type=MESH)
    pl.semaphore_wait(barrier, g1 - 1 + n_col - 1)

    def gather(src, slots, sends, recvs, count, mine, dev):
        out = []
        for t in range(1, count):
            peer = (mine + t) % count
            cp = pltpu.make_async_remote_copy(
                src_ref=src, dst_ref=slots.at[mine], send_sem=sends.at[peer],
                recv_sem=recvs.at[mine], device_id=dev(peer), device_id_type=MESH)
            cp.start()
            out.append(cp)
        slots[mine] = src[...]
        for t in range(1, count):
            peer = (mine + t) % count
            pltpu.make_async_remote_copy(
                src_ref=src, dst_ref=slots.at[peer], send_sem=sends.at[peer],
                recv_sem=recvs.at[peer], device_id=dev(peer), device_id_type=MESH).wait_recv()
        for cp in out:
            cp.wait_send()
        acc = slots[0]
        for s in range(1, count):
            acc = acc + slots[s]
        return acc

    stage[...] = gather(val_ref, slots1, send1, recv1, g1, me1, dev1)
    out_ref[...] = gather(stage, slots2, send2, recv2, n_col, k, dev2)


def global_sum(v, mesh_shape):
    n_col = mesh_shape["chan"] // GROUP
    n_f = mesh_shape["freq"]
    g1 = GROUP * n_f
    tile = jnp.full((8, 128), v, jnp.float32)
    out = pl.pallas_call(
        functools.partial(sum_kernel, n_col, n_f),
        out_shape=jax.ShapeDtypeStruct((8, 128), jnp.float32),
        in_specs=[pl.BlockSpec(memory_space=pltpu.VMEM)],
        out_specs=pl.BlockSpec(memory_space=pltpu.VMEM),
        scratch_shapes=[
            pltpu.VMEM((g1, 8, 128), jnp.float32),
            pltpu.VMEM((n_col, 8, 128), jnp.float32),
            pltpu.VMEM((8, 128), jnp.float32),
            pltpu.SemaphoreType.DMA((g1,)),
            pltpu.SemaphoreType.DMA((g1,)),
            pltpu.SemaphoreType.DMA((n_col,)),
            pltpu.SemaphoreType.DMA((n_col,)),
        ],
        compiler_params=pltpu.CompilerParams(collective_id=0, has_side_effects=True),
    )(tile)
    return out[0, 0]


def shards(spectra, model, channel_ok, limits, mesh_shape, n_chunks):
    payload = jnp.concatenate([spectra, model], axis=2)
    fl, _, rows, bw = payload.shape
    peers = lax.axis_size("chan")
    me = lax.axis_index("chan")
    j = me % GROUP
    column = me // GROUP
    sub = fl // GROUP // n_chunks
    band_blocks = BAND // bw
    halo_cols = -(-band_blocks // GROUP)
    nblk = GROUP * (1 + halo_cols)

    ok_all = channel_ok.astype(jnp.float32)
    ok_wide = jnp.concatenate([ok_all, ok_all[: nblk * bw]])
    ok_ext = lax.dynamic_slice_in_dim(ok_wide, column * GROUP * bw, nblk * bw).reshape(nblk, bw)
    lim = lax.dynamic_slice_in_dim(limits, column * GROUP, GROUP)

    pieces = payload.reshape(GROUP, n_chunks, sub, 2, rows, bw)
    misfit_sum = jnp.zeros((), jnp.float32)
    outs = []
    for c in range(n_chunks):
        mine = exchange(pieces[:, c], j, peers)
        own = jnp.transpose(mine, (1, 0, 2, 3, 4))
        parts = [own] + [permute(own, shift_pairs(peers, -GROUP * h)) for h in range(1, halo_cols + 1)]
        ext = jnp.concatenate(parts, axis=1)

        first = ext[:, :GROUP]
        ok_first = ok_ext[:GROUP]
        near_acc = jnp.zeros((sub, GROUP, 2, W, bw), jnp.float32)
        far_acc = jnp.zeros((sub, nblk, 2, W, bw), jnp.float32)
        for s in range(band_blocks + 1):
            second = ext[:, s : s + GROUP]
            piece_loss, near_terms, far_terms = pair_terms(
                first, second, ok_first, ok_ext[s : s + GROUP], lim, s
            )
            misfit_sum = misfit_sum + piece_loss
            near_acc = near_acc + near_terms
            far_acc = far_acc.at[:, s : s + GROUP].add(far_terms)
        adj = near_acc + far_acc[:, :GROUP]
        for h in range(1, halo_cols + 1):
            adj = adj + permute(far_acc[:, h * GROUP : (h + 1) * GROUP], shift_pairs(peers, GROUP * h))
        adj = adj * (1.0 / W)
        blocks = jnp.transpose(adj, (1, 0, 2, 3, 4))
        outs.append(exchange(blocks, j, peers))
    misfit_total = global_sum(misfit_sum, mesh_shape)
    adjoint = jnp.stack(outs, axis=1).reshape(fl, 2, W, bw)

    misfit = misfit_total / float(F * bw * peers * BAND)
    return adjoint, misfit


def solution(mesh):
    mesh_shape = dict(mesh.shape)
    return jax.shard_map(
        lambda *a: shards(*a, mesh_shape, CHUNKS),
        mesh=mesh,
        in_specs=(P("freq", None, None, "chan"), P("freq", None, None, "chan"), P(), P()),
        out_specs=(P("freq", None, None, "chan"), P()),
        check_vma=False,
    )
```

```python
import jax
import jax.numpy as jnp
from jax import lax
from jax.experimental import pallas as pl
from jax.experimental.pallas import tpu as pltpu
from jax.sharding import PartitionSpec as P
import functools

F = 256
W = 16
BAND = 1024
GROUP = 4


def permute(x, pairs):
    return lax.ppermute(x, "chan", pairs)


def shift_pairs(peers, by):
    return [(i, (i + by) % peers) for i in range(peers)]


def group_pairs(peers, t):
    return [(i, (i // GROUP) * GROUP + (i % GROUP + t) % GROUP) for i in range(peers)]


def exchange(chunks, j, peers):
    rel = jnp.roll(chunks, -j, axis=0)
    got = [rel[0]] + [permute(rel[t], group_pairs(peers, t)) for t in range(1, GROUP)]
    got = jnp.stack(got, axis=0)
    order = (j - jnp.arange(GROUP)) % GROUP
    return jnp.take(got, order, axis=0)


def pair_terms(first, second, ok_first, ok_second, limit_first, shift_blocks):
    fb, nb, _, row_count, block_width = first.shape
    row_scale = jnp.concatenate(
        [jnp.full((W,), 1.0 / W, jnp.float32), jnp.full((row_count - W,), -1.0, jnp.float32)]
    ).astype(jnp.bfloat16)
    scaled = first * row_scale[None, None, None, :, None]
    stacked_left = jnp.stack(
        [
            scaled.reshape(fb, nb, 2 * row_count, block_width),
            jnp.concatenate([scaled[:, :, 1], -scaled[:, :, 0]], axis=2),
        ],
        axis=2,
    )
    right_rows = second.reshape(fb, nb, 2 * row_count, block_width)
    cross_spec = jnp.einsum(
        "fbxrc,fbrd->fbxcd", stacked_left, right_rows, preferred_element_type=jnp.float32
    )
    row_index = lax.broadcasted_iota(jnp.int32, (block_width, block_width), 0)
    col_index = lax.broadcasted_iota(jnp.int32, (block_width, block_width), 1)
    offset = shift_blocks * block_width + col_index - row_index
    inside = ((offset[None] >= 1) & (offset[None] <= limit_first[:, None, None])).astype(jnp.float32)
    live_mask = ok_first[:, :, None] * ok_second[:, None, :] * inside
    residual = cross_spec * live_mask[None, :, None]
    piece_loss = 0.5 * jnp.sum(residual * residual)
    rounded = residual.astype(jnp.bfloat16)
    far_spec = second[:, :, :, :W].reshape(fb, nb, 2 * W, block_width)
    near_spec = first[:, :, :, :W].reshape(fb, nb, 2 * W, block_width)
    toward = jnp.einsum("fbxcd,fbvd->fbxvc", rounded, far_spec, preferred_element_type=jnp.float32)
    first_real = toward[:, :, 0, :W] - toward[:, :, 1, W:]
    first_imag = toward[:, :, 0, W:] + toward[:, :, 1, :W]
    backward = jnp.einsum("fbxcd,fbvc->fbxvd", rounded, near_spec, preferred_element_type=jnp.float32)
    second_real = backward[:, :, 0, :W] + backward[:, :, 1, W:]
    second_imag = backward[:, :, 0, W:] - backward[:, :, 1, :W]
    return (
        piece_loss,
        jnp.stack([first_real, first_imag], axis=2),
        jnp.stack([second_real, second_imag], axis=2),
    )


MESH = pl.DeviceIdType.MESH

def tail_kernel(n_col, n_f, blocks_ref, val_ref, out_ref, sum_ref,
                got, slots1, slots2, stage, send_o, recv_o, send1, recv1, send2, recv2):
    c = lax.axis_index("chan")
    f = lax.axis_index("freq")
    k = c // GROUP
    j = c % GROUP
    g1 = GROUP * n_f
    me1 = j * n_f + f

    def dev1(slot):
        return (k * GROUP + slot // n_f, slot % n_f)

    def dev2(col):
        return (col * GROUP + j, f)

    def devg(b):
        return (k * GROUP + b, f)

    barrier = pltpu.get_barrier_semaphore()
    for t in range(1, g1):
        pl.semaphore_signal(barrier, 1, device_id=dev1((me1 + t) % g1), device_id_type=MESH)
    for t in range(1, n_col):
        pl.semaphore_signal(barrier, 1, device_id=dev2((k + t) % n_col), device_id_type=MESH)
    pl.semaphore_wait(barrier, g1 - 1 + n_col - 1)

    def start_gather(src, slots, sends, recvs, count, mine, dev):
        out = []
        for t in range(1, count):
            peer = (mine + t) % count
            cp = pltpu.make_async_remote_copy(
                src_ref=src, dst_ref=slots.at[mine], send_sem=sends.at[peer],
                recv_sem=recvs.at[mine], device_id=dev(peer), device_id_type=MESH)
            cp.start()
            out.append(cp)
        return out

    def finish_gather(src, slots, sends, recvs, count, mine, dev, started):
        slots[mine] = src[...]
        for t in range(1, count):
            peer = (mine + t) % count
            pltpu.make_async_remote_copy(
                src_ref=src, dst_ref=slots.at[peer], send_sem=sends.at[peer],
                recv_sem=recvs.at[peer], device_id=dev(peer), device_id_type=MESH).wait_recv()
        for cp in started:
            cp.wait_send()
        acc = slots[0]
        for s in range(1, count):
            acc = acc + slots[s]
        return acc

    first = start_gather(val_ref, slots1, send1, recv1, g1, me1, dev1)
    outgoing = []
    for t in range(1, GROUP):
        b = (j + t) % GROUP
        cp = pltpu.make_async_remote_copy(
            src_ref=blocks_ref.at[b], dst_ref=got.at[j], send_sem=send_o.at[b],
            recv_sem=recv_o.at[j], device_id=devg(b), device_id_type=MESH)
        cp.start()
        outgoing.append(cp)
    stage[...] = finish_gather(val_ref, slots1, send1, recv1, g1, me1, dev1, first)
    second = start_gather(stage, slots2, send2, recv2, n_col, k, dev2)
    sum_ref[...] = finish_gather(stage, slots2, send2, recv2, n_col, k, dev2, second)
    got[j] = blocks_ref[j]
    for t in range(1, GROUP):
        b = (j + t) % GROUP
        pltpu.make_async_remote_copy(
            src_ref=blocks_ref.at[b], dst_ref=got.at[b], send_sem=send_o.at[b],
            recv_sem=recv_o.at[b], device_id=devg(b), device_id_type=MESH).wait_recv()
    for cp in outgoing:
        cp.wait_send()
    out_ref[...] = got[...]


def finish(blocks, v, mesh_shape):
    n_col = mesh_shape["chan"] // GROUP
    n_f = mesh_shape["freq"]
    g1 = GROUP * n_f
    tile = jnp.full((8, 128), v, jnp.float32)
    vmem = pl.BlockSpec(memory_space=pltpu.VMEM)
    out, total = pl.pallas_call(
        functools.partial(tail_kernel, n_col, n_f),
        out_shape=(jax.ShapeDtypeStruct(blocks.shape, blocks.dtype),
                   jax.ShapeDtypeStruct((8, 128), jnp.float32)),
        in_specs=[vmem, vmem],
        out_specs=(vmem, vmem),
        scratch_shapes=[
            pltpu.VMEM(blocks.shape, blocks.dtype),
            pltpu.VMEM((g1, 8, 128), jnp.float32),
            pltpu.VMEM((n_col, 8, 128), jnp.float32),
            pltpu.VMEM((8, 128), jnp.float32),
            pltpu.SemaphoreType.DMA((GROUP,)),
            pltpu.SemaphoreType.DMA((GROUP,)),
            pltpu.SemaphoreType.DMA((g1,)),
            pltpu.SemaphoreType.DMA((g1,)),
            pltpu.SemaphoreType.DMA((n_col,)),
            pltpu.SemaphoreType.DMA((n_col,)),
        ],
        compiler_params=pltpu.CompilerParams(collective_id=0, has_side_effects=True),
    )(blocks, tile)
    return out, total[0, 0]


def shards(spectra, model, channel_ok, limits, mesh_shape):
    payload = jnp.concatenate([spectra, model], axis=2)
    fl, _, rows, bw = payload.shape
    peers = lax.axis_size("chan")
    me = lax.axis_index("chan")
    j = me % GROUP
    column = me // GROUP
    sub = fl // GROUP
    band_blocks = BAND // bw
    halo_cols = -(-band_blocks // GROUP)
    nblk = GROUP * (1 + halo_cols)

    chunks = payload.reshape(GROUP, sub, 2, rows, bw)
    mine = exchange(chunks, j, peers)
    own = jnp.transpose(mine, (1, 0, 2, 3, 4))

    parts = [own] + [permute(own, shift_pairs(peers, -GROUP * h)) for h in range(1, halo_cols + 1)]
    ext = jnp.concatenate(parts, axis=1)

    ok_all = channel_ok.astype(jnp.float32)
    ok_wide = jnp.concatenate([ok_all, ok_all[: nblk * bw]])
    ok_ext = lax.dynamic_slice_in_dim(ok_wide, column * GROUP * bw, nblk * bw).reshape(nblk, bw)
    lim = lax.dynamic_slice_in_dim(limits, column * GROUP, GROUP)

    first = ext[:, :GROUP]
    ok_first = ok_ext[:GROUP]
    misfit_sum = jnp.zeros((), jnp.float32)
    near_acc = jnp.zeros((sub, GROUP, 2, W, bw), jnp.float32)
    far_acc = jnp.zeros((sub, nblk, 2, W, bw), jnp.float32)
    for s in range(band_blocks + 1):
        second = ext[:, s : s + GROUP]
        piece_loss, near_terms, far_terms = pair_terms(
            first, second, ok_first, ok_ext[s : s + GROUP], lim, s
        )
        misfit_sum = misfit_sum + piece_loss
        near_acc = near_acc + near_terms
        far_acc = far_acc.at[:, s : s + GROUP].add(far_terms)
    adj = near_acc + far_acc[:, :GROUP]
    for h in range(1, halo_cols + 1):
        adj = adj + permute(far_acc[:, h * GROUP : (h + 1) * GROUP], shift_pairs(peers, GROUP * h))
    adj = adj * (1.0 / W)

    blocks = jnp.transpose(adj, (1, 0, 2, 3, 4))
    back, misfit_total = finish(blocks, misfit_sum, mesh_shape)
    adjoint = back.reshape(fl, 2, W, bw)

    misfit = misfit_total / float(F * bw * peers * BAND)
    return adjoint, misfit


def solution(mesh):
    mesh_shape = dict(mesh.shape)
    return jax.shard_map(
        lambda *a: shards(*a, mesh_shape),
        mesh=mesh,
        in_specs=(P("freq", None, None, "chan"), P("freq", None, None, "chan"), P(), P()),
        out_specs=(P("freq", None, None, "chan"), P()),
        check_vma=False,
    )
```

```python
import jax
import jax.numpy as jnp
from jax import lax
from jax.experimental import pallas as pl
from jax.experimental.pallas import tpu as pltpu
from jax.sharding import PartitionSpec as P
import functools

F = 256
W = 16
BAND = 1024
HALVES = 2
GROUP = 4


def permute(x, pairs):
    return lax.ppermute(x, "chan", pairs)


def shift_pairs(peers, by):
    return [(i, (i + by) % peers) for i in range(peers)]


def group_pairs(peers, t):
    return [(i, (i // GROUP) * GROUP + (i % GROUP + t) % GROUP) for i in range(peers)]


def exchange(chunks, j, peers):
    rel = jnp.roll(chunks, -j, axis=0)
    got = [rel[0]] + [permute(rel[t], group_pairs(peers, t)) for t in range(1, GROUP)]
    got = jnp.stack(got, axis=0)
    order = (j - jnp.arange(GROUP)) % GROUP
    return jnp.take(got, order, axis=0)


def pair_terms(first, second, ok_first, ok_second, limit_first, shift_blocks):
    fb, nb, _, row_count, block_width = first.shape
    row_scale = jnp.concatenate(
        [jnp.full((W,), 1.0 / W, jnp.float32), jnp.full((row_count - W,), -1.0, jnp.float32)]
    ).astype(jnp.bfloat16)
    scaled = first * row_scale[None, None, None, :, None]
    stacked_left = jnp.stack(
        [
            scaled.reshape(fb, nb, 2 * row_count, block_width),
            jnp.concatenate([scaled[:, :, 1], -scaled[:, :, 0]], axis=2),
        ],
        axis=2,
    )
    right_rows = second.reshape(fb, nb, 2 * row_count, block_width)
    cross_spec = jnp.einsum(
        "fbxrc,fbrd->fbxcd", stacked_left, right_rows, preferred_element_type=jnp.float32
    )
    row_index = lax.broadcasted_iota(jnp.int32, (block_width, block_width), 0)
    col_index = lax.broadcasted_iota(jnp.int32, (block_width, block_width), 1)
    offset = shift_blocks * block_width + col_index - row_index
    inside = ((offset[None] >= 1) & (offset[None] <= limit_first[:, None, None])).astype(jnp.float32)
    live_mask = ok_first[:, :, None] * ok_second[:, None, :] * inside
    residual = cross_spec * live_mask[None, :, None]
    piece_loss = 0.5 * jnp.sum(residual * residual)
    rounded = residual.astype(jnp.bfloat16)
    far_spec = second[:, :, :, :W].reshape(fb, nb, 2 * W, block_width)
    near_spec = first[:, :, :, :W].reshape(fb, nb, 2 * W, block_width)
    toward = jnp.einsum("fbxcd,fbvd->fbxvc", rounded, far_spec, preferred_element_type=jnp.float32)
    first_real = toward[:, :, 0, :W] - toward[:, :, 1, W:]
    first_imag = toward[:, :, 0, W:] + toward[:, :, 1, :W]
    backward = jnp.einsum("fbxcd,fbvc->fbxvd", rounded, near_spec, preferred_element_type=jnp.float32)
    second_real = backward[:, :, 0, :W] + backward[:, :, 1, W:]
    second_imag = backward[:, :, 0, W:] - backward[:, :, 1, :W]
    return (
        piece_loss,
        jnp.stack([first_real, first_imag], axis=2),
        jnp.stack([second_real, second_imag], axis=2),
    )


MESH = pl.DeviceIdType.MESH

def head_kernel(n_halves, halo_cols, chunks_ref, out_ref, held, send_e, recv_e, send_h, recv_h, own_sem):
    c = lax.axis_index("chan")
    f = lax.axis_index("freq")
    peers = lax.axis_size("chan")
    k = c // GROUP
    j = c % GROUP

    def devg(b):
        return (k * GROUP + b, f)

    def devh(h, sign):
        return ((c + sign * GROUP * h) % peers, f)

    barrier = pltpu.get_barrier_semaphore()
    for t in range(1, GROUP):
        pl.semaphore_signal(barrier, 1, device_id=devg((j + t) % GROUP), device_id_type=MESH)
    for h in range(1, halo_cols + 1):
        pl.semaphore_signal(barrier, 1, device_id=devh(h, -1), device_id_type=MESH)
        pl.semaphore_signal(barrier, 1, device_id=devh(h, 1), device_id_type=MESH)
    pl.semaphore_wait(barrier, GROUP - 1 + 2 * halo_cols)

    sends = []
    locals_ = []
    for half in range(n_halves):
        for t in range(1, GROUP):
            b = (j + t) % GROUP
            cp = pltpu.make_async_remote_copy(
                src_ref=chunks_ref.at[b, half], dst_ref=held.at[half, 0, j],
                send_sem=send_e.at[half, b], recv_sem=recv_e.at[half, j],
                device_id=devg(b), device_id_type=MESH)
            cp.start()
            sends.append(cp)
        cp = pltpu.make_async_copy(chunks_ref.at[j, half], held.at[half, 0, j], own_sem.at[half])
        cp.start()
        locals_.append(cp)
    for half in range(n_halves):
        locals_[half].wait()
        for t in range(1, GROUP):
            b = (j + t) % GROUP
            pltpu.make_async_remote_copy(
                src_ref=chunks_ref.at[b, half], dst_ref=held.at[half, 0, b],
                send_sem=send_e.at[half, b], recv_sem=recv_e.at[half, b],
                device_id=devg(b), device_id_type=MESH).wait_recv()
        for h in range(1, halo_cols + 1):
            cp = pltpu.make_async_remote_copy(
                src_ref=held.at[half, 0], dst_ref=held.at[half, h],
                send_sem=send_h.at[half, h], recv_sem=recv_h.at[half, h],
                device_id=devh(h, -1), device_id_type=MESH)
            cp.start()
            sends.append(cp)
    for half in range(n_halves):
        for h in range(1, halo_cols + 1):
            pltpu.make_async_remote_copy(
                src_ref=held.at[half, 0], dst_ref=held.at[half, h],
                send_sem=send_h.at[half, h], recv_sem=recv_h.at[half, h],
                device_id=devh(h, 1), device_id_type=MESH).wait_recv()
    for cp in sends:
        cp.wait_send()
    out_ref[...] = held[...]


def gather_columns(payload, halo_cols, n_halves):
    fl, two, rows, bw = payload.shape
    q = fl // GROUP // n_halves
    chunks = payload.reshape(GROUP, n_halves, q, two, rows, bw)
    shape = (n_halves, 1 + halo_cols, GROUP, q, two, rows, bw)
    vmem = pl.BlockSpec(memory_space=pltpu.VMEM)
    held = pl.pallas_call(
        functools.partial(head_kernel, n_halves, halo_cols),
        out_shape=jax.ShapeDtypeStruct(shape, payload.dtype),
        in_specs=[vmem],
        out_specs=vmem,
        scratch_shapes=[
            pltpu.VMEM(shape, payload.dtype),
            pltpu.SemaphoreType.DMA((n_halves, GROUP)),
            pltpu.SemaphoreType.DMA((n_halves, GROUP)),
            pltpu.SemaphoreType.DMA((n_halves, 1 + halo_cols)),
            pltpu.SemaphoreType.DMA((n_halves, 1 + halo_cols)),
            pltpu.SemaphoreType.DMA((n_halves,)),
        ],
        compiler_params=pltpu.CompilerParams(collective_id=1, has_side_effects=True),
    )(chunks)
    held = jnp.transpose(held, (0, 3, 1, 2, 4, 5, 6))
    return held.reshape(n_halves * q, (1 + halo_cols) * GROUP, two, rows, bw)


def tail_kernel(n_col, n_f, blocks_ref, val_ref, out_ref, sum_ref,
                got, slots1, slots2, stage, send_o, recv_o, send1, recv1, send2, recv2):
    c = lax.axis_index("chan")
    f = lax.axis_index("freq")
    k = c // GROUP
    j = c % GROUP
    g1 = GROUP * n_f
    me1 = j * n_f + f

    def dev1(slot):
        return (k * GROUP + slot // n_f, slot % n_f)

    def dev2(col):
        return (col * GROUP + j, f)

    def devg(b):
        return (k * GROUP + b, f)

    barrier = pltpu.get_barrier_semaphore()
    for t in range(1, g1):
        pl.semaphore_signal(barrier, 1, device_id=dev1((me1 + t) % g1), device_id_type=MESH)
    for t in range(1, n_col):
        pl.semaphore_signal(barrier, 1, device_id=dev2((k + t) % n_col), device_id_type=MESH)
    pl.semaphore_wait(barrier, g1 - 1 + n_col - 1)

    def start_gather(src, slots, sends, recvs, count, mine, dev):
        out = []
        for t in range(1, count):
            peer = (mine + t) % count
            cp = pltpu.make_async_remote_copy(
                src_ref=src, dst_ref=slots.at[mine], send_sem=sends.at[peer],
                recv_sem=recvs.at[mine], device_id=dev(peer), device_id_type=MESH)
            cp.start()
            out.append(cp)
        return out

    def finish_gather(src, slots, sends, recvs, count, mine, dev, started):
        slots[mine] = src[...]
        for t in range(1, count):
            peer = (mine + t) % count
            pltpu.make_async_remote_copy(
                src_ref=src, dst_ref=slots.at[peer], send_sem=sends.at[peer],
                recv_sem=recvs.at[peer], device_id=dev(peer), device_id_type=MESH).wait_recv()
        for cp in started:
            cp.wait_send()
        acc = slots[0]
        for s in range(1, count):
            acc = acc + slots[s]
        return acc

    first = start_gather(val_ref, slots1, send1, recv1, g1, me1, dev1)
    outgoing = []
    for t in range(1, GROUP):
        b = (j + t) % GROUP
        cp = pltpu.make_async_remote_copy(
            src_ref=blocks_ref.at[b], dst_ref=got.at[j], send_sem=send_o.at[b],
            recv_sem=recv_o.at[j], device_id=devg(b), device_id_type=MESH)
        cp.start()
        outgoing.append(cp)
    stage[...] = finish_gather(val_ref, slots1, send1, recv1, g1, me1, dev1, first)
    second = start_gather(stage, slots2, send2, recv2, n_col, k, dev2)
    sum_ref[...] = finish_gather(stage, slots2, send2, recv2, n_col, k, dev2, second)
    got[j] = blocks_ref[j]
    for t in range(1, GROUP):
        b = (j + t) % GROUP
        pltpu.make_async_remote_copy(
            src_ref=blocks_ref.at[b], dst_ref=got.at[b], send_sem=send_o.at[b],
            recv_sem=recv_o.at[b], device_id=devg(b), device_id_type=MESH).wait_recv()
    for cp in outgoing:
        cp.wait_send()
    out_ref[...] = got[...]


def finish(blocks, v, mesh_shape):
    n_col = mesh_shape["chan"] // GROUP
    n_f = mesh_shape["freq"]
    g1 = GROUP * n_f
    tile = jnp.full((8, 128), v, jnp.float32)
    vmem = pl.BlockSpec(memory_space=pltpu.VMEM)
    out, total = pl.pallas_call(
        functools.partial(tail_kernel, n_col, n_f),
        out_shape=(jax.ShapeDtypeStruct(blocks.shape, blocks.dtype),
                   jax.ShapeDtypeStruct((8, 128), jnp.float32)),
        in_specs=[vmem, vmem],
        out_specs=(vmem, vmem),
        scratch_shapes=[
            pltpu.VMEM(blocks.shape, blocks.dtype),
            pltpu.VMEM((g1, 8, 128), jnp.float32),
            pltpu.VMEM((n_col, 8, 128), jnp.float32),
            pltpu.VMEM((8, 128), jnp.float32),
            pltpu.SemaphoreType.DMA((GROUP,)),
            pltpu.SemaphoreType.DMA((GROUP,)),
            pltpu.SemaphoreType.DMA((g1,)),
            pltpu.SemaphoreType.DMA((g1,)),
            pltpu.SemaphoreType.DMA((n_col,)),
            pltpu.SemaphoreType.DMA((n_col,)),
        ],
        compiler_params=pltpu.CompilerParams(collective_id=0, has_side_effects=True),
    )(blocks, tile)
    return out, total[0, 0]


def shards(spectra, model, channel_ok, limits, mesh_shape):
    payload = jnp.concatenate([spectra, model], axis=2)
    fl, _, rows, bw = payload.shape
    peers = lax.axis_size("chan")
    me = lax.axis_index("chan")
    j = me % GROUP
    column = me // GROUP
    sub = fl // GROUP
    band_blocks = BAND // bw
    halo_cols = -(-band_blocks // GROUP)
    nblk = GROUP * (1 + halo_cols)

    ext = gather_columns(payload, halo_cols, HALVES)

    ok_all = channel_ok.astype(jnp.float32)
    ok_wide = jnp.concatenate([ok_all, ok_all[: nblk * bw]])
    ok_ext = lax.dynamic_slice_in_dim(ok_wide, column * GROUP * bw, nblk * bw).reshape(nblk, bw)
    lim = lax.dynamic_slice_in_dim(limits, column * GROUP, GROUP)

    first = ext[:, :GROUP]
    ok_first = ok_ext[:GROUP]
    misfit_sum = jnp.zeros((), jnp.float32)
    near_acc = jnp.zeros((sub, GROUP, 2, W, bw), jnp.float32)
    far_acc = jnp.zeros((sub, nblk, 2, W, bw), jnp.float32)
    for s in range(band_blocks + 1):
        second = ext[:, s : s + GROUP]
        piece_loss, near_terms, far_terms = pair_terms(
            first, second, ok_first, ok_ext[s : s + GROUP], lim, s
        )
        misfit_sum = misfit_sum + piece_loss
        near_acc = near_acc + near_terms
        far_acc = far_acc.at[:, s : s + GROUP].add(far_terms)
    adj = near_acc + far_acc[:, :GROUP]
    for h in range(1, halo_cols + 1):
        adj = adj + permute(far_acc[:, h * GROUP : (h + 1) * GROUP], shift_pairs(peers, GROUP * h))
    adj = adj * (1.0 / W)

    blocks = jnp.transpose(adj, (1, 0, 2, 3, 4))
    back, misfit_total = finish(blocks, misfit_sum, mesh_shape)
    adjoint = back.reshape(fl, 2, W, bw)

    misfit = misfit_total / float(F * bw * peers * BAND)
    return adjoint, misfit


def solution(mesh):
    mesh_shape = dict(mesh.shape)
    return jax.shard_map(
        lambda *a: shards(*a, mesh_shape),
        mesh=mesh,
        in_specs=(P("freq", None, None, "chan"), P("freq", None, None, "chan"), P(), P()),
        out_specs=(P("freq", None, None, "chan"), P()),
        check_vma=False,
    )
```

```python
import jax
import jax.numpy as jnp
from jax import lax
from jax.experimental import pallas as pl
from jax.experimental.pallas import tpu as pltpu
from jax.sharding import PartitionSpec as P
import functools

F = 256
W = 16
BAND = 1024
HALVES = 2
GROUP = 4


def permute(x, pairs):
    return lax.ppermute(x, "chan", pairs)


def shift_pairs(peers, by):
    return [(i, (i + by) % peers) for i in range(peers)]


def group_pairs(peers, t):
    return [(i, (i // GROUP) * GROUP + (i % GROUP + t) % GROUP) for i in range(peers)]


def exchange(chunks, j, peers):
    rel = jnp.roll(chunks, -j, axis=0)
    got = [rel[0]] + [permute(rel[t], group_pairs(peers, t)) for t in range(1, GROUP)]
    got = jnp.stack(got, axis=0)
    order = (j - jnp.arange(GROUP)) % GROUP
    return jnp.take(got, order, axis=0)


def pair_terms(first, second, ok_first, ok_second, limit_first, shift_blocks):
    fb, nb, _, row_count, block_width = first.shape
    row_scale = jnp.concatenate(
        [jnp.full((W,), 1.0 / W, jnp.float32), jnp.full((row_count - W,), -1.0, jnp.float32)]
    ).astype(jnp.bfloat16)
    scaled = first * row_scale[None, None, None, :, None]
    stacked_left = jnp.stack(
        [
            scaled.reshape(fb, nb, 2 * row_count, block_width),
            jnp.concatenate([scaled[:, :, 1], -scaled[:, :, 0]], axis=2),
        ],
        axis=2,
    )
    right_rows = second.reshape(fb, nb, 2 * row_count, block_width)
    cross_spec = jnp.einsum(
        "fbxrc,fbrd->fbxcd", stacked_left, right_rows, preferred_element_type=jnp.float32
    )
    row_index = lax.broadcasted_iota(jnp.int32, (block_width, block_width), 0)
    col_index = lax.broadcasted_iota(jnp.int32, (block_width, block_width), 1)
    offset = shift_blocks[:, None, None] * block_width + col_index[None] - row_index[None]
    inside = ((offset >= 1) & (offset <= limit_first[:, None, None])).astype(jnp.float32)
    live_mask = ok_first[:, :, None] * ok_second[:, None, :] * inside
    residual = cross_spec * live_mask[None, :, None]
    piece_loss = 0.5 * jnp.sum(residual * residual)
    rounded = residual.astype(jnp.bfloat16)
    far_spec = second[:, :, :, :W].reshape(fb, nb, 2 * W, block_width)
    near_spec = first[:, :, :, :W].reshape(fb, nb, 2 * W, block_width)
    toward = jnp.einsum("fbxcd,fbvd->fbxvc", rounded, far_spec, preferred_element_type=jnp.float32)
    first_real = toward[:, :, 0, :W] - toward[:, :, 1, W:]
    first_imag = toward[:, :, 0, W:] + toward[:, :, 1, :W]
    backward = jnp.einsum("fbxcd,fbvc->fbxvd", rounded, near_spec, preferred_element_type=jnp.float32)
    second_real = backward[:, :, 0, :W] + backward[:, :, 1, W:]
    second_imag = backward[:, :, 0, W:] - backward[:, :, 1, :W]
    return (
        piece_loss,
        jnp.stack([first_real, first_imag], axis=2),
        jnp.stack([second_real, second_imag], axis=2),
    )


MESH = pl.DeviceIdType.MESH

def head_kernel(n_halves, halo_cols, chunks_ref, out_ref, held, send_e, recv_e, send_h, recv_h, own_sem):
    c = lax.axis_index("chan")
    f = lax.axis_index("freq")
    peers = lax.axis_size("chan")
    k = c // GROUP
    j = c % GROUP

    def devg(b):
        return (k * GROUP + b, f)

    def devh(h, sign):
        return ((c + sign * GROUP * h) % peers, f)

    barrier = pltpu.get_barrier_semaphore()
    for t in range(1, GROUP):
        pl.semaphore_signal(barrier, 1, device_id=devg((j + t) % GROUP), device_id_type=MESH)
    for h in range(1, halo_cols + 1):
        pl.semaphore_signal(barrier, 1, device_id=devh(h, -1), device_id_type=MESH)
        pl.semaphore_signal(barrier, 1, device_id=devh(h, 1), device_id_type=MESH)
    pl.semaphore_wait(barrier, GROUP - 1 + 2 * halo_cols)

    sends = []
    locals_ = []
    for half in range(n_halves):
        for t in range(1, GROUP):
            b = (j + t) % GROUP
            cp = pltpu.make_async_remote_copy(
                src_ref=chunks_ref.at[b, half], dst_ref=held.at[half, 0, j],
                send_sem=send_e.at[half, b], recv_sem=recv_e.at[half, j],
                device_id=devg(b), device_id_type=MESH)
            cp.start()
            sends.append(cp)
        cp = pltpu.make_async_copy(chunks_ref.at[j, half], held.at[half, 0, j], own_sem.at[half])
        cp.start()
        locals_.append(cp)
    for half in range(n_halves):
        locals_[half].wait()
        for t in range(1, GROUP):
            b = (j + t) % GROUP
            pltpu.make_async_remote_copy(
                src_ref=chunks_ref.at[b, half], dst_ref=held.at[half, 0, b],
                send_sem=send_e.at[half, b], recv_sem=recv_e.at[half, b],
                device_id=devg(b), device_id_type=MESH).wait_recv()
        for h in range(1, halo_cols + 1):
            cp = pltpu.make_async_remote_copy(
                src_ref=held.at[half, 0], dst_ref=held.at[half, h],
                send_sem=send_h.at[half, h], recv_sem=recv_h.at[half, h],
                device_id=devh(h, -1), device_id_type=MESH)
            cp.start()
            sends.append(cp)
    for half in range(n_halves):
        for h in range(1, halo_cols + 1):
            pltpu.make_async_remote_copy(
                src_ref=held.at[half, 0], dst_ref=held.at[half, h],
                send_sem=send_h.at[half, h], recv_sem=recv_h.at[half, h],
                device_id=devh(h, 1), device_id_type=MESH).wait_recv()
    for cp in sends:
        cp.wait_send()
    out_ref[...] = held[...]


def gather_columns(payload, halo_cols, n_halves):
    fl, two, rows, bw = payload.shape
    q = fl // GROUP // n_halves
    chunks = payload.reshape(GROUP, n_halves, q, two, rows, bw)
    shape = (n_halves, 1 + halo_cols, GROUP, q, two, rows, bw)
    vmem = pl.BlockSpec(memory_space=pltpu.VMEM)
    held = pl.pallas_call(
        functools.partial(head_kernel, n_halves, halo_cols),
        out_shape=jax.ShapeDtypeStruct(shape, payload.dtype),
        in_specs=[vmem],
        out_specs=vmem,
        scratch_shapes=[
            pltpu.VMEM(shape, payload.dtype),
            pltpu.SemaphoreType.DMA((n_halves, GROUP)),
            pltpu.SemaphoreType.DMA((n_halves, GROUP)),
            pltpu.SemaphoreType.DMA((n_halves, 1 + halo_cols)),
            pltpu.SemaphoreType.DMA((n_halves, 1 + halo_cols)),
            pltpu.SemaphoreType.DMA((n_halves,)),
        ],
        compiler_params=pltpu.CompilerParams(collective_id=1, has_side_effects=True),
    )(chunks)
    held = jnp.transpose(held, (0, 3, 1, 2, 4, 5, 6))
    return held.reshape(n_halves * q, (1 + halo_cols) * GROUP, two, rows, bw)


def tail_kernel(n_col, n_f, blocks_ref, val_ref, out_ref, sum_ref,
                got, slots1, slots2, stage, send_o, recv_o, send1, recv1, send2, recv2):
    c = lax.axis_index("chan")
    f = lax.axis_index("freq")
    k = c // GROUP
    j = c % GROUP
    g1 = GROUP * n_f
    me1 = j * n_f + f

    def dev1(slot):
        return (k * GROUP + slot // n_f, slot % n_f)

    def dev2(col):
        return (col * GROUP + j, f)

    def devg(b):
        return (k * GROUP + b, f)

    barrier = pltpu.get_barrier_semaphore()
    for t in range(1, g1):
        pl.semaphore_signal(barrier, 1, device_id=dev1((me1 + t) % g1), device_id_type=MESH)
    for t in range(1, n_col):
        pl.semaphore_signal(barrier, 1, device_id=dev2((k + t) % n_col), device_id_type=MESH)
    pl.semaphore_wait(barrier, g1 - 1 + n_col - 1)

    def start_gather(src, slots, sends, recvs, count, mine, dev):
        out = []
        for t in range(1, count):
            peer = (mine + t) % count
            cp = pltpu.make_async_remote_copy(
                src_ref=src, dst_ref=slots.at[mine], send_sem=sends.at[peer],
                recv_sem=recvs.at[mine], device_id=dev(peer), device_id_type=MESH)
            cp.start()
            out.append(cp)
        return out

    def finish_gather(src, slots, sends, recvs, count, mine, dev, started):
        slots[mine] = src[...]
        for t in range(1, count):
            peer = (mine + t) % count
            pltpu.make_async_remote_copy(
                src_ref=src, dst_ref=slots.at[peer], send_sem=sends.at[peer],
                recv_sem=recvs.at[peer], device_id=dev(peer), device_id_type=MESH).wait_recv()
        for cp in started:
            cp.wait_send()
        acc = slots[0]
        for s in range(1, count):
            acc = acc + slots[s]
        return acc

    first = start_gather(val_ref, slots1, send1, recv1, g1, me1, dev1)
    outgoing = []
    for t in range(1, GROUP):
        b = (j + t) % GROUP
        cp = pltpu.make_async_remote_copy(
            src_ref=blocks_ref.at[b], dst_ref=got.at[j], send_sem=send_o.at[b],
            recv_sem=recv_o.at[j], device_id=devg(b), device_id_type=MESH)
        cp.start()
        outgoing.append(cp)
    stage[...] = finish_gather(val_ref, slots1, send1, recv1, g1, me1, dev1, first)
    second = start_gather(stage, slots2, send2, recv2, n_col, k, dev2)
    sum_ref[...] = finish_gather(stage, slots2, send2, recv2, n_col, k, dev2, second)
    got[j] = blocks_ref[j]
    for t in range(1, GROUP):
        b = (j + t) % GROUP
        pltpu.make_async_remote_copy(
            src_ref=blocks_ref.at[b], dst_ref=got.at[b], send_sem=send_o.at[b],
            recv_sem=recv_o.at[b], device_id=devg(b), device_id_type=MESH).wait_recv()
    for cp in outgoing:
        cp.wait_send()
    out_ref[...] = got[...]


def finish(blocks, v, mesh_shape):
    n_col = mesh_shape["chan"] // GROUP
    n_f = mesh_shape["freq"]
    g1 = GROUP * n_f
    tile = jnp.full((8, 128), v, jnp.float32)
    vmem = pl.BlockSpec(memory_space=pltpu.VMEM)
    out, total = pl.pallas_call(
        functools.partial(tail_kernel, n_col, n_f),
        out_shape=(jax.ShapeDtypeStruct(blocks.shape, blocks.dtype),
                   jax.ShapeDtypeStruct((8, 128), jnp.float32)),
        in_specs=[vmem, vmem],
        out_specs=(vmem, vmem),
        scratch_shapes=[
            pltpu.VMEM(blocks.shape, blocks.dtype),
            pltpu.VMEM((g1, 8, 128), jnp.float32),
            pltpu.VMEM((n_col, 8, 128), jnp.float32),
            pltpu.VMEM((8, 128), jnp.float32),
            pltpu.SemaphoreType.DMA((GROUP,)),
            pltpu.SemaphoreType.DMA((GROUP,)),
            pltpu.SemaphoreType.DMA((g1,)),
            pltpu.SemaphoreType.DMA((g1,)),
            pltpu.SemaphoreType.DMA((n_col,)),
            pltpu.SemaphoreType.DMA((n_col,)),
        ],
        compiler_params=pltpu.CompilerParams(collective_id=0, has_side_effects=True),
    )(blocks, tile)
    return out, total[0, 0]


def shards(spectra, model, channel_ok, limits, mesh_shape):
    payload = jnp.concatenate([spectra, model], axis=2)
    fl, _, rows, bw = payload.shape
    peers = lax.axis_size("chan")
    me = lax.axis_index("chan")
    j = me % GROUP
    column = me // GROUP
    sub = fl // GROUP
    band_blocks = BAND // bw
    halo_cols = -(-band_blocks // GROUP)
    nblk = GROUP * (1 + halo_cols)

    ext = gather_columns(payload, halo_cols, HALVES)

    ok_all = channel_ok.astype(jnp.float32)
    ok_wide = jnp.concatenate([ok_all, ok_all[: nblk * bw]])
    ok_ext = lax.dynamic_slice_in_dim(ok_wide, column * GROUP * bw, nblk * bw).reshape(nblk, bw)
    lim = lax.dynamic_slice_in_dim(limits, column * GROUP, GROUP)

    near_acc = [None] * GROUP
    far_acc = [None] * nblk
    misfit_sum = jnp.zeros((), jnp.float32)
    span = band_blocks + 1
    groups = [
        [(bb, t) for bb in range(GROUP) for t in range(lo, hi) if bb <= t < bb + span]
        for lo, hi in [(GROUP * h, GROUP * (h + 1)) for h in range(halo_cols, -1, -1)]
    ]
    for pairs in groups:
        firsts = [bb for bb, _ in pairs]
        seconds = [t for _, t in pairs]
        first = jnp.stack([ext[:, bb] for bb in firsts], axis=1)
        second = jnp.stack([ext[:, t] for t in seconds], axis=1)
        shifts = jnp.array([t - bb for bb, t in pairs], jnp.int32)
        piece_loss, near_terms, far_terms = pair_terms(
            first, second, jnp.stack([ok_ext[bb] for bb in firsts]),
            jnp.stack([ok_ext[t] for t in seconds]), jnp.stack([lim[bb] for bb in firsts]), shifts
        )
        misfit_sum = misfit_sum + piece_loss
        for q, (bb, t) in enumerate(pairs):
            near_acc[bb] = near_terms[:, q] if near_acc[bb] is None else near_acc[bb] + near_terms[:, q]
            far_acc[t] = far_terms[:, q] if far_acc[t] is None else far_acc[t] + far_terms[:, q]
    near_acc = jnp.stack(near_acc, axis=1)
    far_acc = jnp.stack(far_acc, axis=1)
    adj = near_acc + far_acc[:, :GROUP]
    for h in range(1, halo_cols + 1):
        adj = adj + permute(far_acc[:, h * GROUP : (h + 1) * GROUP], shift_pairs(peers, GROUP * h))
    adj = adj * (1.0 / W)

    blocks = jnp.transpose(adj, (1, 0, 2, 3, 4))
    back, misfit_total = finish(blocks, misfit_sum, mesh_shape)
    adjoint = back.reshape(fl, 2, W, bw)

    misfit = misfit_total / float(F * bw * peers * BAND)
    return adjoint, misfit


def solution(mesh):
    mesh_shape = dict(mesh.shape)
    return jax.shard_map(
        lambda *a: shards(*a, mesh_shape),
        mesh=mesh,
        in_specs=(P("freq", None, None, "chan"), P("freq", None, None, "chan"), P(), P()),
        out_specs=(P("freq", None, None, "chan"), P()),
        check_vma=False,
    )
```

```python
import jax
import jax.numpy as jnp
from jax import lax
from jax.experimental import pallas as pl
from jax.experimental.pallas import tpu as pltpu
from jax.sharding import PartitionSpec as P
import functools

F = 256
W = 16
BAND = 1024
HALVES = 2
GROUP = 4


def permute(x, pairs):
    return lax.ppermute(x, "chan", pairs)


def shift_pairs(peers, by):
    return [(i, (i + by) % peers) for i in range(peers)]


def group_pairs(peers, t):
    return [(i, (i // GROUP) * GROUP + (i % GROUP + t) % GROUP) for i in range(peers)]


def exchange(chunks, j, peers):
    rel = jnp.roll(chunks, -j, axis=0)
    got = [rel[0]] + [permute(rel[t], group_pairs(peers, t)) for t in range(1, GROUP)]
    got = jnp.stack(got, axis=0)
    order = (j - jnp.arange(GROUP)) % GROUP
    return jnp.take(got, order, axis=0)


def pair_terms(first, second, ok_first, ok_second, limit_first, shift_blocks):
    fb, nb, _, row_count, block_width = first.shape
    row_scale = jnp.concatenate(
        [jnp.full((W,), 1.0 / W, jnp.float32), jnp.full((row_count - W,), -1.0, jnp.float32)]
    ).astype(jnp.bfloat16)
    scaled = first * row_scale[None, None, None, :, None]
    stacked_left = jnp.stack(
        [
            scaled.reshape(fb, nb, 2 * row_count, block_width),
            jnp.concatenate([scaled[:, :, 1], -scaled[:, :, 0]], axis=2),
        ],
        axis=2,
    )
    right_rows = second.reshape(fb, nb, 2 * row_count, block_width)
    cross_spec = jnp.einsum(
        "fbxrc,fbrd->fbxcd", stacked_left, right_rows, preferred_element_type=jnp.float32
    )
    row_index = lax.broadcasted_iota(jnp.int32, (block_width, block_width), 0)
    col_index = lax.broadcasted_iota(jnp.int32, (block_width, block_width), 1)
    offset = shift_blocks * block_width + col_index - row_index
    inside = ((offset[None] >= 1) & (offset[None] <= limit_first[:, None, None])).astype(jnp.float32)
    live_mask = ok_first[:, :, None] * ok_second[:, None, :] * inside
    residual = cross_spec * live_mask[None, :, None]
    piece_loss = 0.5 * jnp.sum(residual * residual)
    rounded = residual.astype(jnp.bfloat16)
    far_spec = second[:, :, :, :W].reshape(fb, nb, 2 * W, block_width)
    near_spec = first[:, :, :, :W].reshape(fb, nb, 2 * W, block_width)
    toward = jnp.einsum("fbxcd,fbvd->fbxvc", rounded, far_spec, preferred_element_type=jnp.float32)
    first_real = toward[:, :, 0, :W] - toward[:, :, 1, W:]
    first_imag = toward[:, :, 0, W:] + toward[:, :, 1, :W]
    backward = jnp.einsum("fbxcd,fbvc->fbxvd", rounded, near_spec, preferred_element_type=jnp.float32)
    second_real = backward[:, :, 0, :W] + backward[:, :, 1, W:]
    second_imag = backward[:, :, 0, W:] - backward[:, :, 1, :W]
    return (
        piece_loss,
        jnp.stack([first_real, first_imag], axis=2),
        jnp.stack([second_real, second_imag], axis=2),
    )


MESH = pl.DeviceIdType.MESH

def head_kernel(n_halves, halo_cols, chunks_ref, out_ref, held, send_e, recv_e, send_h, recv_h, own_sem):
    c = lax.axis_index("chan")
    f = lax.axis_index("freq")
    peers = lax.axis_size("chan")
    k = c // GROUP
    j = c % GROUP

    def devg(b):
        return (k * GROUP + b, f)

    def devh(h, sign):
        return ((c + sign * GROUP * h) % peers, f)

    barrier = pltpu.get_barrier_semaphore()
    for t in range(1, GROUP):
        pl.semaphore_signal(barrier, 1, device_id=devg((j + t) % GROUP), device_id_type=MESH)
    for h in range(1, halo_cols + 1):
        pl.semaphore_signal(barrier, 1, device_id=devh(h, -1), device_id_type=MESH)
        pl.semaphore_signal(barrier, 1, device_id=devh(h, 1), device_id_type=MESH)
    pl.semaphore_wait(barrier, GROUP - 1 + 2 * halo_cols)

    sends = []
    locals_ = []
    for half in range(n_halves):
        for t in range(1, GROUP):
            b = (j + t) % GROUP
            cp = pltpu.make_async_remote_copy(
                src_ref=chunks_ref.at[b, half], dst_ref=held.at[half, 0, j],
                send_sem=send_e.at[half, b], recv_sem=recv_e.at[half, j],
                device_id=devg(b), device_id_type=MESH)
            cp.start()
            sends.append(cp)
        cp = pltpu.make_async_copy(chunks_ref.at[j, half], held.at[half, 0, j], own_sem.at[half])
        cp.start()
        locals_.append(cp)
    for half in range(n_halves):
        locals_[half].wait()
        for t in range(1, GROUP):
            b = (j + t) % GROUP
            pltpu.make_async_remote_copy(
                src_ref=chunks_ref.at[b, half], dst_ref=held.at[half, 0, b],
                send_sem=send_e.at[half, b], recv_sem=recv_e.at[half, b],
                device_id=devg(b), device_id_type=MESH).wait_recv()
        for h in range(1, halo_cols + 1):
            cp = pltpu.make_async_remote_copy(
                src_ref=held.at[half, 0], dst_ref=held.at[half, h],
                send_sem=send_h.at[half, h], recv_sem=recv_h.at[half, h],
                device_id=devh(h, -1), device_id_type=MESH)
            cp.start()
            sends.append(cp)
    for half in range(n_halves):
        for h in range(1, halo_cols + 1):
            pltpu.make_async_remote_copy(
                src_ref=held.at[half, 0], dst_ref=held.at[half, h],
                send_sem=send_h.at[half, h], recv_sem=recv_h.at[half, h],
                device_id=devh(h, 1), device_id_type=MESH).wait_recv()
    for cp in sends:
        cp.wait_send()
    out_ref[...] = held[...]


def gather_columns(payload, halo_cols, n_halves):
    fl, two, rows, bw = payload.shape
    q = fl // GROUP // n_halves
    chunks = payload.reshape(GROUP, n_halves, q, two, rows, bw)
    shape = (n_halves, 1 + halo_cols, GROUP, q, two, rows, bw)
    vmem = pl.BlockSpec(memory_space=pltpu.VMEM)
    held = pl.pallas_call(
        functools.partial(head_kernel, n_halves, halo_cols),
        out_shape=jax.ShapeDtypeStruct(shape, payload.dtype),
        in_specs=[vmem],
        out_specs=vmem,
        scratch_shapes=[
            pltpu.VMEM(shape, payload.dtype),
            pltpu.SemaphoreType.DMA((n_halves, GROUP)),
            pltpu.SemaphoreType.DMA((n_halves, GROUP)),
            pltpu.SemaphoreType.DMA((n_halves, 1 + halo_cols)),
            pltpu.SemaphoreType.DMA((n_halves, 1 + halo_cols)),
            pltpu.SemaphoreType.DMA((n_halves,)),
        ],
        compiler_params=pltpu.CompilerParams(collective_id=1, has_side_effects=True),
    )(chunks)
    held = jnp.transpose(held, (0, 3, 1, 2, 4, 5, 6))
    return held.reshape(n_halves * q, (1 + halo_cols) * GROUP, two, rows, bw)


def tail_kernel(n_col, n_f, blocks_ref, val_ref, out_ref, sum_ref,
                got, slots1, slots2, stage, send_o, recv_o, send1, recv1, send2, recv2):
    c = lax.axis_index("chan")
    f = lax.axis_index("freq")
    k = c // GROUP
    j = c % GROUP
    g1 = GROUP * n_f
    me1 = j * n_f + f

    def dev1(slot):
        return (k * GROUP + slot // n_f, slot % n_f)

    def dev2(col):
        return (col * GROUP + j, f)

    def devg(b):
        return (k * GROUP + b, f)

    barrier = pltpu.get_barrier_semaphore()
    for t in range(1, g1):
        pl.semaphore_signal(barrier, 1, device_id=dev1((me1 + t) % g1), device_id_type=MESH)
    for t in range(1, n_col):
        pl.semaphore_signal(barrier, 1, device_id=dev2((k + t) % n_col), device_id_type=MESH)
    pl.semaphore_wait(barrier, g1 - 1 + n_col - 1)

    def start_gather(src, slots, sends, recvs, count, mine, dev):
        out = []
        for t in range(1, count):
            peer = (mine + t) % count
            cp = pltpu.make_async_remote_copy(
                src_ref=src, dst_ref=slots.at[mine], send_sem=sends.at[peer],
                recv_sem=recvs.at[mine], device_id=dev(peer), device_id_type=MESH)
            cp.start()
            out.append(cp)
        return out

    def finish_gather(src, slots, sends, recvs, count, mine, dev, started):
        slots[mine] = src[...]
        for t in range(1, count):
            peer = (mine + t) % count
            pltpu.make_async_remote_copy(
                src_ref=src, dst_ref=slots.at[peer], send_sem=sends.at[peer],
                recv_sem=recvs.at[peer], device_id=dev(peer), device_id_type=MESH).wait_recv()
        for cp in started:
            cp.wait_send()
        acc = slots[0]
        for s in range(1, count):
            acc = acc + slots[s]
        return acc

    first = start_gather(val_ref, slots1, send1, recv1, g1, me1, dev1)
    outgoing = []
    for t in range(1, GROUP):
        b = (j + t) % GROUP
        cp = pltpu.make_async_remote_copy(
            src_ref=blocks_ref.at[b], dst_ref=got.at[j], send_sem=send_o.at[b],
            recv_sem=recv_o.at[j], device_id=devg(b), device_id_type=MESH)
        cp.start()
        outgoing.append(cp)
    stage[...] = finish_gather(val_ref, slots1, send1, recv1, g1, me1, dev1, first)
    second = start_gather(stage, slots2, send2, recv2, n_col, k, dev2)
    sum_ref[...] = finish_gather(stage, slots2, send2, recv2, n_col, k, dev2, second)
    got[j] = blocks_ref[j]
    for t in range(1, GROUP):
        b = (j + t) % GROUP
        pltpu.make_async_remote_copy(
            src_ref=blocks_ref.at[b], dst_ref=got.at[b], send_sem=send_o.at[b],
            recv_sem=recv_o.at[b], device_id=devg(b), device_id_type=MESH).wait_recv()
    for cp in outgoing:
        cp.wait_send()
    out_ref[...] = got[...]


def finish(blocks, v, mesh_shape):
    n_col = mesh_shape["chan"] // GROUP
    n_f = mesh_shape["freq"]
    g1 = GROUP * n_f
    tile = jnp.full((8, 128), v, jnp.float32)
    vmem = pl.BlockSpec(memory_space=pltpu.VMEM)
    out, total = pl.pallas_call(
        functools.partial(tail_kernel, n_col, n_f),
        out_shape=(jax.ShapeDtypeStruct(blocks.shape, blocks.dtype),
                   jax.ShapeDtypeStruct((8, 128), jnp.float32)),
        in_specs=[vmem, vmem],
        out_specs=(vmem, vmem),
        scratch_shapes=[
            pltpu.VMEM(blocks.shape, blocks.dtype),
            pltpu.VMEM((g1, 8, 128), jnp.float32),
            pltpu.VMEM((n_col, 8, 128), jnp.float32),
            pltpu.VMEM((8, 128), jnp.float32),
            pltpu.SemaphoreType.DMA((GROUP,)),
            pltpu.SemaphoreType.DMA((GROUP,)),
            pltpu.SemaphoreType.DMA((g1,)),
            pltpu.SemaphoreType.DMA((g1,)),
            pltpu.SemaphoreType.DMA((n_col,)),
            pltpu.SemaphoreType.DMA((n_col,)),
        ],
        compiler_params=pltpu.CompilerParams(collective_id=0, has_side_effects=True),
    )(blocks, tile)
    return out, total[0, 0]


def shards(spectra, model, channel_ok, limits, mesh_shape):
    payload = jnp.concatenate([spectra, model], axis=2)
    fl, _, rows, bw = payload.shape
    peers = lax.axis_size("chan")
    me = lax.axis_index("chan")
    j = me % GROUP
    column = me // GROUP
    sub = fl // GROUP
    band_blocks = BAND // bw
    halo_cols = -(-band_blocks // GROUP)
    nblk = GROUP * (1 + halo_cols)

    ext = gather_columns(payload, halo_cols, HALVES)

    ok_all = channel_ok.astype(jnp.float32)
    ok_wide = jnp.concatenate([ok_all, ok_all[: nblk * bw]])
    ok_ext = lax.dynamic_slice_in_dim(ok_wide, column * GROUP * bw, nblk * bw).reshape(nblk, bw)
    lim = lax.dynamic_slice_in_dim(limits, column * GROUP, GROUP)

    first = ext[:, :GROUP]
    ok_first = ok_ext[:GROUP]
    misfit_sum = jnp.zeros((), jnp.float32)
    near_acc = jnp.zeros((sub, GROUP, 2, W, bw), jnp.float32)
    far_acc = [jnp.zeros((sub, 2, W, bw), jnp.float32) for _ in range(nblk)]
    sent = []
    for s in range(band_blocks, -1, -1):
        second = ext[:, s : s + GROUP]
        piece_loss, near_terms, far_terms = pair_terms(
            first, second, ok_first, ok_ext[s : s + GROUP], lim, s
        )
        misfit_sum = misfit_sum + piece_loss
        near_acc = near_acc + near_terms
        for bb in range(GROUP):
            far_acc[s + bb] = far_acc[s + bb] + far_terms[:, bb]
        for h in range(1, halo_cols + 1):
            if s == max(GROUP * h - GROUP + 1, 0) and h * GROUP < nblk:
                done = jnp.stack(far_acc[h * GROUP : (h + 1) * GROUP], axis=1)
                done, ext = lax.optimization_barrier((done, ext))
                first = ext[:, :GROUP]
                sent.append(permute(done, shift_pairs(peers, GROUP * h)))
    adj = near_acc + jnp.stack(far_acc[:GROUP], axis=1)
    for part in sent:
        adj = adj + part
    adj = adj * (1.0 / W)

    blocks = jnp.transpose(adj, (1, 0, 2, 3, 4))
    back, misfit_total = finish(blocks, misfit_sum, mesh_shape)
    adjoint = back.reshape(fl, 2, W, bw)

    misfit = misfit_total / float(F * bw * peers * BAND)
    return adjoint, misfit


def solution(mesh):
    mesh_shape = dict(mesh.shape)
    return jax.shard_map(
        lambda *a: shards(*a, mesh_shape),
        mesh=mesh,
        in_specs=(P("freq", None, None, "chan"), P("freq", None, None, "chan"), P(), P()),
        out_specs=(P("freq", None, None, "chan"), P()),
        check_vma=False,
    )
```

```python
import jax
import jax.numpy as jnp
from jax import lax
from jax.experimental import pallas as pl
from jax.experimental.pallas import tpu as pltpu
from jax.sharding import PartitionSpec as P
import functools

F = 256
W = 16
BAND = 1024
HALVES = 4
GROUP = 4


def permute(x, pairs):
    return lax.ppermute(x, "chan", pairs)


def shift_pairs(peers, by):
    return [(i, (i + by) % peers) for i in range(peers)]


def group_pairs(peers, t):
    return [(i, (i // GROUP) * GROUP + (i % GROUP + t) % GROUP) for i in range(peers)]


def exchange(chunks, j, peers):
    rel = jnp.roll(chunks, -j, axis=0)
    got = [rel[0]] + [permute(rel[t], group_pairs(peers, t)) for t in range(1, GROUP)]
    got = jnp.stack(got, axis=0)
    order = (j - jnp.arange(GROUP)) % GROUP
    return jnp.take(got, order, axis=0)


def pair_terms(first, second, ok_first, ok_second, limit_first, shift_blocks):
    fb, nb, _, row_count, block_width = first.shape
    row_scale = jnp.concatenate(
        [jnp.full((W,), 1.0 / W, jnp.float32), jnp.full((row_count - W,), -1.0, jnp.float32)]
    ).astype(jnp.bfloat16)
    scaled = first * row_scale[None, None, None, :, None]
    stacked_left = jnp.stack(
        [
            scaled.reshape(fb, nb, 2 * row_count, block_width),
            jnp.concatenate([scaled[:, :, 1], -scaled[:, :, 0]], axis=2),
        ],
        axis=2,
    )
    right_rows = second.reshape(fb, nb, 2 * row_count, block_width)
    cross_spec = jnp.einsum(
        "fbxrc,fbrd->fbxcd", stacked_left, right_rows, preferred_element_type=jnp.float32
    )
    row_index = lax.broadcasted_iota(jnp.int32, (block_width, block_width), 0)
    col_index = lax.broadcasted_iota(jnp.int32, (block_width, block_width), 1)
    offset = shift_blocks * block_width + col_index - row_index
    inside = ((offset[None] >= 1) & (offset[None] <= limit_first[:, None, None])).astype(jnp.float32)
    live_mask = ok_first[:, :, None] * ok_second[:, None, :] * inside
    residual = cross_spec * live_mask[None, :, None]
    piece_loss = 0.5 * jnp.sum(residual * residual)
    rounded = residual.astype(jnp.bfloat16)
    far_spec = second[:, :, :, :W].reshape(fb, nb, 2 * W, block_width)
    near_spec = first[:, :, :, :W].reshape(fb, nb, 2 * W, block_width)
    toward = jnp.einsum("fbxcd,fbvd->fbxvc", rounded, far_spec, preferred_element_type=jnp.float32)
    first_real = toward[:, :, 0, :W] - toward[:, :, 1, W:]
    first_imag = toward[:, :, 0, W:] + toward[:, :, 1, :W]
    backward = jnp.einsum("fbxcd,fbvc->fbxvd", rounded, near_spec, preferred_element_type=jnp.float32)
    second_real = backward[:, :, 0, :W] + backward[:, :, 1, W:]
    second_imag = backward[:, :, 0, W:] - backward[:, :, 1, :W]
    return (
        piece_loss,
        jnp.stack([first_real, first_imag], axis=2),
        jnp.stack([second_real, second_imag], axis=2),
    )


MESH = pl.DeviceIdType.MESH

def head_kernel(n_halves, halo_cols, chunks_ref, out_ref, held, send_e, recv_e, send_h, recv_h, own_sem):
    c = lax.axis_index("chan")
    f = lax.axis_index("freq")
    peers = lax.axis_size("chan")
    k = c // GROUP
    j = c % GROUP

    def devg(b):
        return (k * GROUP + b, f)

    def devh(h, sign):
        return ((c + sign * GROUP * h) % peers, f)

    barrier = pltpu.get_barrier_semaphore()
    for t in range(1, GROUP):
        pl.semaphore_signal(barrier, 1, device_id=devg((j + t) % GROUP), device_id_type=MESH)
    for h in range(1, halo_cols + 1):
        pl.semaphore_signal(barrier, 1, device_id=devh(h, -1), device_id_type=MESH)
        pl.semaphore_signal(barrier, 1, device_id=devh(h, 1), device_id_type=MESH)
    pl.semaphore_wait(barrier, GROUP - 1 + 2 * halo_cols)

    sends = []
    locals_ = []
    for half in range(n_halves):
        for t in range(1, GROUP):
            b = (j + t) % GROUP
            cp = pltpu.make_async_remote_copy(
                src_ref=chunks_ref.at[b, half], dst_ref=held.at[half, 0, j],
                send_sem=send_e.at[half, b], recv_sem=recv_e.at[half, j],
                device_id=devg(b), device_id_type=MESH)
            cp.start()
            sends.append(cp)
        cp = pltpu.make_async_copy(chunks_ref.at[j, half], held.at[half, 0, j], own_sem.at[half])
        cp.start()
        locals_.append(cp)
    for half in range(n_halves):
        locals_[half].wait()
        for t in range(1, GROUP):
            b = (j + t) % GROUP
            pltpu.make_async_remote_copy(
                src_ref=chunks_ref.at[b, half], dst_ref=held.at[half, 0, b],
                send_sem=send_e.at[half, b], recv_sem=recv_e.at[half, b],
                device_id=devg(b), device_id_type=MESH).wait_recv()
        for h in range(1, halo_cols + 1):
            cp = pltpu.make_async_remote_copy(
                src_ref=held.at[half, 0], dst_ref=held.at[half, h],
                send_sem=send_h.at[half, h], recv_sem=recv_h.at[half, h],
                device_id=devh(h, -1), device_id_type=MESH)
            cp.start()
            sends.append(cp)
    for half in range(n_halves):
        for h in range(1, halo_cols + 1):
            pltpu.make_async_remote_copy(
                src_ref=held.at[half, 0], dst_ref=held.at[half, h],
                send_sem=send_h.at[half, h], recv_sem=recv_h.at[half, h],
                device_id=devh(h, 1), device_id_type=MESH).wait_recv()
    for cp in sends:
        cp.wait_send()
    out_ref[...] = held[...]


def gather_columns(payload, halo_cols, n_halves):
    fl, two, rows, bw = payload.shape
    q = fl // GROUP // n_halves
    chunks = payload.reshape(GROUP, n_halves, q, two, rows, bw)
    shape = (n_halves, 1 + halo_cols, GROUP, q, two, rows, bw)
    vmem = pl.BlockSpec(memory_space=pltpu.VMEM)
    held = pl.pallas_call(
        functools.partial(head_kernel, n_halves, halo_cols),
        out_shape=jax.ShapeDtypeStruct(shape, payload.dtype),
        in_specs=[vmem],
        out_specs=vmem,
        scratch_shapes=[
            pltpu.VMEM(shape, payload.dtype),
            pltpu.SemaphoreType.DMA((n_halves, GROUP)),
            pltpu.SemaphoreType.DMA((n_halves, GROUP)),
            pltpu.SemaphoreType.DMA((n_halves, 1 + halo_cols)),
            pltpu.SemaphoreType.DMA((n_halves, 1 + halo_cols)),
            pltpu.SemaphoreType.DMA((n_halves,)),
        ],
        compiler_params=pltpu.CompilerParams(collective_id=1, has_side_effects=True),
    )(chunks)
    held = jnp.transpose(held, (0, 3, 1, 2, 4, 5, 6))
    return held.reshape(n_halves * q, (1 + halo_cols) * GROUP, two, rows, bw)


def tail_kernel(n_col, n_f, blocks_ref, val_ref, out_ref, sum_ref,
                got, slots1, slots2, stage, send_o, recv_o, send1, recv1, send2, recv2):
    c = lax.axis_index("chan")
    f = lax.axis_index("freq")
    k = c // GROUP
    j = c % GROUP
    g1 = GROUP * n_f
    me1 = j * n_f + f

    def dev1(slot):
        return (k * GROUP + slot // n_f, slot % n_f)

    def dev2(col):
        return (col * GROUP + j, f)

    def devg(b):
        return (k * GROUP + b, f)

    barrier = pltpu.get_barrier_semaphore()
    for t in range(1, g1):
        pl.semaphore_signal(barrier, 1, device_id=dev1((me1 + t) % g1), device_id_type=MESH)
    for t in range(1, n_col):
        pl.semaphore_signal(barrier, 1, device_id=dev2((k + t) % n_col), device_id_type=MESH)
    pl.semaphore_wait(barrier, g1 - 1 + n_col - 1)

    def start_gather(src, slots, sends, recvs, count, mine, dev):
        out = []
        for t in range(1, count):
            peer = (mine + t) % count
            cp = pltpu.make_async_remote_copy(
                src_ref=src, dst_ref=slots.at[mine], send_sem=sends.at[peer],
                recv_sem=recvs.at[mine], device_id=dev(peer), device_id_type=MESH)
            cp.start()
            out.append(cp)
        return out

    def finish_gather(src, slots, sends, recvs, count, mine, dev, started):
        slots[mine] = src[...]
        for t in range(1, count):
            peer = (mine + t) % count
            pltpu.make_async_remote_copy(
                src_ref=src, dst_ref=slots.at[peer], send_sem=sends.at[peer],
                recv_sem=recvs.at[peer], device_id=dev(peer), device_id_type=MESH).wait_recv()
        for cp in started:
            cp.wait_send()
        acc = slots[0]
        for s in range(1, count):
            acc = acc + slots[s]
        return acc

    first = start_gather(val_ref, slots1, send1, recv1, g1, me1, dev1)
    outgoing = []
    for t in range(1, GROUP):
        b = (j + t) % GROUP
        cp = pltpu.make_async_remote_copy(
            src_ref=blocks_ref.at[b], dst_ref=got.at[j], send_sem=send_o.at[b],
            recv_sem=recv_o.at[j], device_id=devg(b), device_id_type=MESH)
        cp.start()
        outgoing.append(cp)
    stage[...] = finish_gather(val_ref, slots1, send1, recv1, g1, me1, dev1, first)
    second = start_gather(stage, slots2, send2, recv2, n_col, k, dev2)
    sum_ref[...] = finish_gather(stage, slots2, send2, recv2, n_col, k, dev2, second)
    got[j] = blocks_ref[j]
    for t in range(1, GROUP):
        b = (j + t) % GROUP
        pltpu.make_async_remote_copy(
            src_ref=blocks_ref.at[b], dst_ref=got.at[b], send_sem=send_o.at[b],
            recv_sem=recv_o.at[b], device_id=devg(b), device_id_type=MESH).wait_recv()
    for cp in outgoing:
        cp.wait_send()
    out_ref[...] = got[...]


def finish(blocks, v, mesh_shape):
    n_col = mesh_shape["chan"] // GROUP
    n_f = mesh_shape["freq"]
    g1 = GROUP * n_f
    tile = jnp.full((8, 128), v, jnp.float32)
    vmem = pl.BlockSpec(memory_space=pltpu.VMEM)
    out, total = pl.pallas_call(
        functools.partial(tail_kernel, n_col, n_f),
        out_shape=(jax.ShapeDtypeStruct(blocks.shape, blocks.dtype),
                   jax.ShapeDtypeStruct((8, 128), jnp.float32)),
        in_specs=[vmem, vmem],
        out_specs=(vmem, vmem),
        scratch_shapes=[
            pltpu.VMEM(blocks.shape, blocks.dtype),
            pltpu.VMEM((g1, 8, 128), jnp.float32),
            pltpu.VMEM((n_col, 8, 128), jnp.float32),
            pltpu.VMEM((8, 128), jnp.float32),
            pltpu.SemaphoreType.DMA((GROUP,)),
            pltpu.SemaphoreType.DMA((GROUP,)),
            pltpu.SemaphoreType.DMA((g1,)),
            pltpu.SemaphoreType.DMA((g1,)),
            pltpu.SemaphoreType.DMA((n_col,)),
            pltpu.SemaphoreType.DMA((n_col,)),
        ],
        compiler_params=pltpu.CompilerParams(collective_id=0, has_side_effects=True),
    )(blocks, tile)
    return out, total[0, 0]


def shards(spectra, model, channel_ok, limits, mesh_shape):
    payload = jnp.concatenate([spectra, model], axis=2)
    fl, _, rows, bw = payload.shape
    peers = lax.axis_size("chan")
    me = lax.axis_index("chan")
    j = me % GROUP
    column = me // GROUP
    sub = fl // GROUP
    band_blocks = BAND // bw
    halo_cols = -(-band_blocks // GROUP)
    nblk = GROUP * (1 + halo_cols)

    ext = gather_columns(payload, halo_cols, HALVES)

    ok_all = channel_ok.astype(jnp.float32)
    ok_wide = jnp.concatenate([ok_all, ok_all[: nblk * bw]])
    ok_ext = lax.dynamic_slice_in_dim(ok_wide, column * GROUP * bw, nblk * bw).reshape(nblk, bw)
    lim = lax.dynamic_slice_in_dim(limits, column * GROUP, GROUP)

    first = ext[:, :GROUP]
    ok_first = ok_ext[:GROUP]
    misfit_sum = jnp.zeros((), jnp.float32)
    near_acc = jnp.zeros((sub, GROUP, 2, W, bw), jnp.float32)
    far_acc = [jnp.zeros((sub, 2, W, bw), jnp.float32) for _ in range(nblk)]
    sent = []
    for s in range(band_blocks, -1, -1):
        second = ext[:, s : s + GROUP]
        piece_loss, near_terms, far_terms = pair_terms(
            first, second, ok_first, ok_ext[s : s + GROUP], lim, s
        )
        misfit_sum = misfit_sum + piece_loss
        near_acc = near_acc + near_terms
        for bb in range(GROUP):
            far_acc[s + bb] = far_acc[s + bb] + far_terms[:, bb]
        for h in range(1, halo_cols + 1):
            if s == max(GROUP * h - GROUP + 1, 0) and h * GROUP < nblk:
                done = jnp.stack(far_acc[h * GROUP : (h + 1) * GROUP], axis=1)
                done, ext = lax.optimization_barrier((done, ext))
                first = ext[:, :GROUP]
                sent.append(permute(done, shift_pairs(peers, GROUP * h)))
    adj = near_acc + jnp.stack(far_acc[:GROUP], axis=1)
    for part in sent:
        adj = adj + part
    adj = adj * (1.0 / W)

    blocks = jnp.transpose(adj, (1, 0, 2, 3, 4))
    back, misfit_total = finish(blocks, misfit_sum, mesh_shape)
    adjoint = back.reshape(fl, 2, W, bw)

    misfit = misfit_total / float(F * bw * peers * BAND)
    return adjoint, misfit


def solution(mesh):
    mesh_shape = dict(mesh.shape)
    return jax.shard_map(
        lambda *a: shards(*a, mesh_shape),
        mesh=mesh,
        in_specs=(P("freq", None, None, "chan"), P("freq", None, None, "chan"), P(), P()),
        out_specs=(P("freq", None, None, "chan"), P()),
        check_vma=False,
    )
```

```python
import jax
import jax.numpy as jnp
from jax import lax
from jax.experimental import pallas as pl
from jax.experimental.pallas import tpu as pltpu
from jax.sharding import PartitionSpec as P
import functools

F = 256
W = 16
BAND = 1024
HALVES = 4
PIECE = 2
GROUP = 4


def permute(x, pairs):
    return lax.ppermute(x, "chan", pairs)


def shift_pairs(peers, by):
    return [(i, (i + by) % peers) for i in range(peers)]


def group_pairs(peers, t):
    return [(i, (i // GROUP) * GROUP + (i % GROUP + t) % GROUP) for i in range(peers)]


def exchange(chunks, j, peers):
    rel = jnp.roll(chunks, -j, axis=0)
    got = [rel[0]] + [permute(rel[t], group_pairs(peers, t)) for t in range(1, GROUP)]
    got = jnp.stack(got, axis=0)
    order = (j - jnp.arange(GROUP)) % GROUP
    return jnp.take(got, order, axis=0)


def pair_terms(first, second, ok_first, ok_second, limit_first, shift_blocks):
    fb, nb, _, row_count, block_width = first.shape
    row_scale = jnp.concatenate(
        [jnp.full((W,), 1.0 / W, jnp.float32), jnp.full((row_count - W,), -1.0, jnp.float32)]
    ).astype(jnp.bfloat16)
    scaled = first * row_scale[None, None, None, :, None]
    stacked_left = jnp.stack(
        [
            scaled.reshape(fb, nb, 2 * row_count, block_width),
            jnp.concatenate([scaled[:, :, 1], -scaled[:, :, 0]], axis=2),
        ],
        axis=2,
    )
    right_rows = second.reshape(fb, nb, 2 * row_count, block_width)
    cross_spec = jnp.einsum(
        "fbxrc,fbrd->fbxcd", stacked_left, right_rows, preferred_element_type=jnp.float32
    )
    row_index = lax.broadcasted_iota(jnp.int32, (block_width, block_width), 0)
    col_index = lax.broadcasted_iota(jnp.int32, (block_width, block_width), 1)
    offset = shift_blocks * block_width + col_index - row_index
    inside = ((offset[None] >= 1) & (offset[None] <= limit_first[:, None, None])).astype(jnp.float32)
    live_mask = ok_first[:, :, None] * ok_second[:, None, :] * inside
    residual = cross_spec * live_mask[None, :, None]
    piece_loss = 0.5 * jnp.sum(residual * residual)
    rounded = residual.astype(jnp.bfloat16)
    far_spec = second[:, :, :, :W].reshape(fb, nb, 2 * W, block_width)
    near_spec = first[:, :, :, :W].reshape(fb, nb, 2 * W, block_width)
    toward = jnp.einsum("fbxcd,fbvd->fbxvc", rounded, far_spec, preferred_element_type=jnp.float32)
    first_real = toward[:, :, 0, :W] - toward[:, :, 1, W:]
    first_imag = toward[:, :, 0, W:] + toward[:, :, 1, :W]
    backward = jnp.einsum("fbxcd,fbvc->fbxvd", rounded, near_spec, preferred_element_type=jnp.float32)
    second_real = backward[:, :, 0, :W] + backward[:, :, 1, W:]
    second_imag = backward[:, :, 0, W:] - backward[:, :, 1, :W]
    return (
        piece_loss,
        jnp.stack([first_real, first_imag], axis=2),
        jnp.stack([second_real, second_imag], axis=2),
    )


MESH = pl.DeviceIdType.MESH

def head_kernel(n_halves, halo_cols, chunks_ref, out_ref, held, send_e, recv_e, send_h, recv_h, own_sem):
    c = lax.axis_index("chan")
    f = lax.axis_index("freq")
    peers = lax.axis_size("chan")
    k = c // GROUP
    j = c % GROUP

    def devg(b):
        return (k * GROUP + b, f)

    def devh(h, sign):
        return ((c + sign * GROUP * h) % peers, f)

    barrier = pltpu.get_barrier_semaphore()
    for t in range(1, GROUP):
        pl.semaphore_signal(barrier, 1, device_id=devg((j + t) % GROUP), device_id_type=MESH)
    for h in range(1, halo_cols + 1):
        pl.semaphore_signal(barrier, 1, device_id=devh(h, -1), device_id_type=MESH)
        pl.semaphore_signal(barrier, 1, device_id=devh(h, 1), device_id_type=MESH)
    pl.semaphore_wait(barrier, GROUP - 1 + 2 * halo_cols)

    sends = []
    locals_ = []
    for half in range(n_halves):
        for t in range(1, GROUP):
            b = (j + t) % GROUP
            cp = pltpu.make_async_remote_copy(
                src_ref=chunks_ref.at[b, half], dst_ref=held.at[half, 0, j],
                send_sem=send_e.at[half, b], recv_sem=recv_e.at[half, j],
                device_id=devg(b), device_id_type=MESH)
            cp.start()
            sends.append(cp)
        cp = pltpu.make_async_copy(chunks_ref.at[j, half], held.at[half, 0, j], own_sem.at[half])
        cp.start()
        locals_.append(cp)
    for half in range(n_halves):
        locals_[half].wait()
        for t in range(1, GROUP):
            b = (j + t) % GROUP
            pltpu.make_async_remote_copy(
                src_ref=chunks_ref.at[b, half], dst_ref=held.at[half, 0, b],
                send_sem=send_e.at[half, b], recv_sem=recv_e.at[half, b],
                device_id=devg(b), device_id_type=MESH).wait_recv()
        for h in range(1, halo_cols + 1):
            cp = pltpu.make_async_remote_copy(
                src_ref=held.at[half, 0], dst_ref=held.at[half, h],
                send_sem=send_h.at[half, h], recv_sem=recv_h.at[half, h],
                device_id=devh(h, -1), device_id_type=MESH)
            cp.start()
            sends.append(cp)
    for half in range(n_halves):
        for h in range(1, halo_cols + 1):
            pltpu.make_async_remote_copy(
                src_ref=held.at[half, 0], dst_ref=held.at[half, h],
                send_sem=send_h.at[half, h], recv_sem=recv_h.at[half, h],
                device_id=devh(h, 1), device_id_type=MESH).wait_recv()
    for cp in sends:
        cp.wait_send()
    out_ref[...] = held[...]


def gather_columns(payload, halo_cols, n_halves):
    fl, two, rows, bw = payload.shape
    q = fl // GROUP // n_halves
    chunks = payload.reshape(GROUP, n_halves, q, two, rows, bw)
    shape = (n_halves, 1 + halo_cols, GROUP, q, two, rows, bw)
    vmem = pl.BlockSpec(memory_space=pltpu.VMEM)
    held = pl.pallas_call(
        functools.partial(head_kernel, n_halves, halo_cols),
        out_shape=jax.ShapeDtypeStruct(shape, payload.dtype),
        in_specs=[vmem],
        out_specs=vmem,
        scratch_shapes=[
            pltpu.VMEM(shape, payload.dtype),
            pltpu.SemaphoreType.DMA((n_halves, GROUP)),
            pltpu.SemaphoreType.DMA((n_halves, GROUP)),
            pltpu.SemaphoreType.DMA((n_halves, 1 + halo_cols)),
            pltpu.SemaphoreType.DMA((n_halves, 1 + halo_cols)),
            pltpu.SemaphoreType.DMA((n_halves,)),
        ],
        compiler_params=pltpu.CompilerParams(collective_id=1, has_side_effects=True),
    )(chunks)
    held = jnp.transpose(held, (0, 3, 1, 2, 4, 5, 6))
    return held.reshape(n_halves * q, (1 + halo_cols) * GROUP, two, rows, bw)


def tail_kernel(n_col, n_f, blocks_ref, val_ref, out_ref, sum_ref,
                got, slots1, slots2, stage, send_o, recv_o, send1, recv1, send2, recv2):
    c = lax.axis_index("chan")
    f = lax.axis_index("freq")
    k = c // GROUP
    j = c % GROUP
    g1 = GROUP * n_f
    me1 = j * n_f + f

    def dev1(slot):
        return (k * GROUP + slot // n_f, slot % n_f)

    def dev2(col):
        return (col * GROUP + j, f)

    def devg(b):
        return (k * GROUP + b, f)

    barrier = pltpu.get_barrier_semaphore()
    for t in range(1, g1):
        pl.semaphore_signal(barrier, 1, device_id=dev1((me1 + t) % g1), device_id_type=MESH)
    for t in range(1, n_col):
        pl.semaphore_signal(barrier, 1, device_id=dev2((k + t) % n_col), device_id_type=MESH)
    pl.semaphore_wait(barrier, g1 - 1 + n_col - 1)

    def start_gather(src, slots, sends, recvs, count, mine, dev):
        out = []
        for t in range(1, count):
            peer = (mine + t) % count
            cp = pltpu.make_async_remote_copy(
                src_ref=src, dst_ref=slots.at[mine], send_sem=sends.at[peer],
                recv_sem=recvs.at[mine], device_id=dev(peer), device_id_type=MESH)
            cp.start()
            out.append(cp)
        return out

    def finish_gather(src, slots, sends, recvs, count, mine, dev, started):
        slots[mine] = src[...]
        for t in range(1, count):
            peer = (mine + t) % count
            pltpu.make_async_remote_copy(
                src_ref=src, dst_ref=slots.at[peer], send_sem=sends.at[peer],
                recv_sem=recvs.at[peer], device_id=dev(peer), device_id_type=MESH).wait_recv()
        for cp in started:
            cp.wait_send()
        acc = slots[0]
        for s in range(1, count):
            acc = acc + slots[s]
        return acc

    first = start_gather(val_ref, slots1, send1, recv1, g1, me1, dev1)
    outgoing = []
    for t in range(1, GROUP):
        b = (j + t) % GROUP
        cp = pltpu.make_async_remote_copy(
            src_ref=blocks_ref.at[b], dst_ref=got.at[j], send_sem=send_o.at[b],
            recv_sem=recv_o.at[j], device_id=devg(b), device_id_type=MESH)
        cp.start()
        outgoing.append(cp)
    stage[...] = finish_gather(val_ref, slots1, send1, recv1, g1, me1, dev1, first)
    second = start_gather(stage, slots2, send2, recv2, n_col, k, dev2)
    sum_ref[...] = finish_gather(stage, slots2, send2, recv2, n_col, k, dev2, second)
    got[j] = blocks_ref[j]
    for t in range(1, GROUP):
        b = (j + t) % GROUP
        pltpu.make_async_remote_copy(
            src_ref=blocks_ref.at[b], dst_ref=got.at[b], send_sem=send_o.at[b],
            recv_sem=recv_o.at[b], device_id=devg(b), device_id_type=MESH).wait_recv()
    for cp in outgoing:
        cp.wait_send()
    out_ref[...] = got[...]


def finish(blocks, v, mesh_shape):
    n_col = mesh_shape["chan"] // GROUP
    n_f = mesh_shape["freq"]
    g1 = GROUP * n_f
    tile = jnp.full((8, 128), v, jnp.float32)
    vmem = pl.BlockSpec(memory_space=pltpu.VMEM)
    out, total = pl.pallas_call(
        functools.partial(tail_kernel, n_col, n_f),
        out_shape=(jax.ShapeDtypeStruct(blocks.shape, blocks.dtype),
                   jax.ShapeDtypeStruct((8, 128), jnp.float32)),
        in_specs=[vmem, vmem],
        out_specs=(vmem, vmem),
        scratch_shapes=[
            pltpu.VMEM(blocks.shape, blocks.dtype),
            pltpu.VMEM((g1, 8, 128), jnp.float32),
            pltpu.VMEM((n_col, 8, 128), jnp.float32),
            pltpu.VMEM((8, 128), jnp.float32),
            pltpu.SemaphoreType.DMA((GROUP,)),
            pltpu.SemaphoreType.DMA((GROUP,)),
            pltpu.SemaphoreType.DMA((g1,)),
            pltpu.SemaphoreType.DMA((g1,)),
            pltpu.SemaphoreType.DMA((n_col,)),
            pltpu.SemaphoreType.DMA((n_col,)),
        ],
        compiler_params=pltpu.CompilerParams(collective_id=0, has_side_effects=True),
    )(blocks, tile)
    return out, total[0, 0]


def shards(spectra, model, channel_ok, limits, mesh_shape):
    payload = jnp.concatenate([spectra, model], axis=2)
    fl, _, rows, bw = payload.shape
    peers = lax.axis_size("chan")
    me = lax.axis_index("chan")
    j = me % GROUP
    column = me // GROUP
    sub = fl // GROUP
    band_blocks = BAND // bw
    halo_cols = -(-band_blocks // GROUP)
    nblk = GROUP * (1 + halo_cols)

    ext = gather_columns(payload, halo_cols, HALVES)

    ok_all = channel_ok.astype(jnp.float32)
    ok_wide = jnp.concatenate([ok_all, ok_all[: nblk * bw]])
    ok_ext = lax.dynamic_slice_in_dim(ok_wide, column * GROUP * bw, nblk * bw).reshape(nblk, bw)
    lim = lax.dynamic_slice_in_dim(limits, column * GROUP, GROUP)

    first = ext[:, :GROUP]
    ok_first = ok_ext[:GROUP]
    misfit_sum = jnp.zeros((), jnp.float32)
    near_acc = jnp.zeros((sub, GROUP, 2, W, bw), jnp.float32)
    far_acc = [jnp.zeros((sub, 2, W, bw), jnp.float32) for _ in range(nblk)]
    sent = []
    for s in range(band_blocks, -1, -1):
        second = ext[:, s : s + GROUP]
        piece_loss, near_terms, far_terms = pair_terms(
            first, second, ok_first, ok_ext[s : s + GROUP], lim, s
        )
        misfit_sum = misfit_sum + piece_loss
        near_acc = near_acc + near_terms
        for bb in range(GROUP):
            far_acc[s + bb] = far_acc[s + bb] + far_terms[:, bb]
        for lo in range(GROUP, nblk, PIECE):
            if s == max(lo - (GROUP - 1), 0):
                done = jnp.stack(far_acc[lo : lo + PIECE], axis=1)
                done, ext = lax.optimization_barrier((done, ext))
                first = ext[:, :GROUP]
                sent.append((lo % GROUP, permute(done, shift_pairs(peers, GROUP * (lo // GROUP)))))
    pieces = [jnp.stack(far_acc[:GROUP], axis=1)]
    for at in range(0, GROUP, PIECE):
        got = [part for pos, part in sent if pos == at]
        total = got[0]
        for part in got[1:]:
            total = total + part
        pieces.append(jnp.pad(total, ((0, 0), (at, GROUP - at - PIECE), (0, 0), (0, 0), (0, 0))))
    adj = near_acc
    for part in pieces:
        adj = adj + part
    adj = adj * (1.0 / W)

    blocks = jnp.transpose(adj, (1, 0, 2, 3, 4))
    back, misfit_total = finish(blocks, misfit_sum, mesh_shape)
    adjoint = back.reshape(fl, 2, W, bw)

    misfit = misfit_total / float(F * bw * peers * BAND)
    return adjoint, misfit


def solution(mesh):
    mesh_shape = dict(mesh.shape)
    return jax.shard_map(
        lambda *a: shards(*a, mesh_shape),
        mesh=mesh,
        in_specs=(P("freq", None, None, "chan"), P("freq", None, None, "chan"), P(), P()),
        out_specs=(P("freq", None, None, "chan"), P()),
        check_vma=False,
    )
```

```python
import jax
import jax.numpy as jnp
from jax import lax
from jax.experimental import pallas as pl
from jax.experimental.pallas import tpu as pltpu
from jax.sharding import PartitionSpec as P
import functools

F = 256
W = 16
BAND = 1024
HALVES = 4
GROUP = 4


def permute(x, pairs):
    return lax.ppermute(x, "chan", pairs)


def shift_pairs(peers, by):
    return [(i, (i + by) % peers) for i in range(peers)]


def group_pairs(peers, t):
    return [(i, (i // GROUP) * GROUP + (i % GROUP + t) % GROUP) for i in range(peers)]


def exchange(chunks, j, peers):
    rel = jnp.roll(chunks, -j, axis=0)
    got = [rel[0]] + [permute(rel[t], group_pairs(peers, t)) for t in range(1, GROUP)]
    got = jnp.stack(got, axis=0)
    order = (j - jnp.arange(GROUP)) % GROUP
    return jnp.take(got, order, axis=0)


def pair_terms(first, second, ok_first, ok_second, limit_first, shift_blocks):
    fb, nb, _, row_count, block_width = first.shape
    row_scale = jnp.concatenate(
        [jnp.full((W,), 1.0 / W, jnp.float32), jnp.full((row_count - W,), -1.0, jnp.float32)]
    ).astype(jnp.bfloat16)
    scaled = first * row_scale[None, None, None, :, None]
    stacked_left = jnp.stack(
        [
            scaled.reshape(fb, nb, 2 * row_count, block_width),
            jnp.concatenate([scaled[:, :, 1], -scaled[:, :, 0]], axis=2),
        ],
        axis=2,
    )
    right_rows = second.reshape(fb, nb, 2 * row_count, block_width)
    cross_spec = jnp.einsum(
        "fbxrc,fbrd->fbxcd", stacked_left, right_rows, preferred_element_type=jnp.float32
    )
    row_index = lax.broadcasted_iota(jnp.int32, (block_width, block_width), 0)
    col_index = lax.broadcasted_iota(jnp.int32, (block_width, block_width), 1)
    offset = shift_blocks * block_width + col_index - row_index
    inside = ((offset[None] >= 1) & (offset[None] <= limit_first[:, None, None])).astype(jnp.float32)
    live_mask = ok_first[:, :, None] * ok_second[:, None, :] * inside
    residual = cross_spec * live_mask[None, :, None]
    squares = (residual * residual).reshape(-1, block_width // 8, 8, block_width)
    piece_loss = jnp.sum(squares, axis=(0, 1))
    rounded = residual.astype(jnp.bfloat16)
    far_spec = second[:, :, :, :W].reshape(fb, nb, 2 * W, block_width)
    near_spec = first[:, :, :, :W].reshape(fb, nb, 2 * W, block_width)
    toward = jnp.einsum("fbxcd,fbvd->fbxvc", rounded, far_spec, preferred_element_type=jnp.float32)
    first_real = toward[:, :, 0, :W] - toward[:, :, 1, W:]
    first_imag = toward[:, :, 0, W:] + toward[:, :, 1, :W]
    backward = jnp.einsum("fbxcd,fbvc->fbxvd", rounded, near_spec, preferred_element_type=jnp.float32)
    second_real = backward[:, :, 0, :W] + backward[:, :, 1, W:]
    second_imag = backward[:, :, 0, W:] - backward[:, :, 1, :W]
    return (
        piece_loss,
        jnp.stack([first_real, first_imag], axis=2),
        jnp.stack([second_real, second_imag], axis=2),
    )


MESH = pl.DeviceIdType.MESH

def head_kernel(n_halves, halo_cols, chunks_ref, out_ref, held, send_e, recv_e, send_h, recv_h, own_sem):
    c = lax.axis_index("chan")
    f = lax.axis_index("freq")
    peers = lax.axis_size("chan")
    k = c // GROUP
    j = c % GROUP

    def devg(b):
        return (k * GROUP + b, f)

    def devh(h, sign):
        return ((c + sign * GROUP * h) % peers, f)

    barrier = pltpu.get_barrier_semaphore()
    for t in range(1, GROUP):
        pl.semaphore_signal(barrier, 1, device_id=devg((j + t) % GROUP), device_id_type=MESH)
    for h in range(1, halo_cols + 1):
        pl.semaphore_signal(barrier, 1, device_id=devh(h, -1), device_id_type=MESH)
        pl.semaphore_signal(barrier, 1, device_id=devh(h, 1), device_id_type=MESH)
    pl.semaphore_wait(barrier, GROUP - 1 + 2 * halo_cols)

    sends = []
    locals_ = []
    for half in range(n_halves):
        for t in range(1, GROUP):
            b = (j + t) % GROUP
            cp = pltpu.make_async_remote_copy(
                src_ref=chunks_ref.at[b, half], dst_ref=held.at[half, 0, j],
                send_sem=send_e.at[half, b], recv_sem=recv_e.at[half, j],
                device_id=devg(b), device_id_type=MESH)
            cp.start()
            sends.append(cp)
        cp = pltpu.make_async_copy(chunks_ref.at[j, half], held.at[half, 0, j], own_sem.at[half])
        cp.start()
        locals_.append(cp)
    for half in range(n_halves):
        locals_[half].wait()
        for t in range(1, GROUP):
            b = (j + t) % GROUP
            pltpu.make_async_remote_copy(
                src_ref=chunks_ref.at[b, half], dst_ref=held.at[half, 0, b],
                send_sem=send_e.at[half, b], recv_sem=recv_e.at[half, b],
                device_id=devg(b), device_id_type=MESH).wait_recv()
        for h in range(1, halo_cols + 1):
            cp = pltpu.make_async_remote_copy(
                src_ref=held.at[half, 0], dst_ref=held.at[half, h],
                send_sem=send_h.at[half, h], recv_sem=recv_h.at[half, h],
                device_id=devh(h, -1), device_id_type=MESH)
            cp.start()
            sends.append(cp)
    for half in range(n_halves):
        for h in range(1, halo_cols + 1):
            pltpu.make_async_remote_copy(
                src_ref=held.at[half, 0], dst_ref=held.at[half, h],
                send_sem=send_h.at[half, h], recv_sem=recv_h.at[half, h],
                device_id=devh(h, 1), device_id_type=MESH).wait_recv()
    for cp in sends:
        cp.wait_send()
    out_ref[...] = held[...]


def gather_columns(payload, halo_cols, n_halves):
    fl, two, rows, bw = payload.shape
    q = fl // GROUP // n_halves
    chunks = payload.reshape(GROUP, n_halves, q, two, rows, bw)
    shape = (n_halves, 1 + halo_cols, GROUP, q, two, rows, bw)
    vmem = pl.BlockSpec(memory_space=pltpu.VMEM)
    held = pl.pallas_call(
        functools.partial(head_kernel, n_halves, halo_cols),
        out_shape=jax.ShapeDtypeStruct(shape, payload.dtype),
        in_specs=[vmem],
        out_specs=vmem,
        scratch_shapes=[
            pltpu.VMEM(shape, payload.dtype),
            pltpu.SemaphoreType.DMA((n_halves, GROUP)),
            pltpu.SemaphoreType.DMA((n_halves, GROUP)),
            pltpu.SemaphoreType.DMA((n_halves, 1 + halo_cols)),
            pltpu.SemaphoreType.DMA((n_halves, 1 + halo_cols)),
            pltpu.SemaphoreType.DMA((n_halves,)),
        ],
        compiler_params=pltpu.CompilerParams(collective_id=1, has_side_effects=True),
    )(chunks)
    held = jnp.transpose(held, (0, 3, 1, 2, 4, 5, 6))
    return held.reshape(n_halves * q, (1 + halo_cols) * GROUP, two, rows, bw)


def tail_kernel(n_col, n_f, blocks_ref, val_ref, out_ref, sum_ref,
                got, slots1, slots2, stage, send_o, recv_o, send1, recv1, send2, recv2):
    c = lax.axis_index("chan")
    f = lax.axis_index("freq")
    k = c // GROUP
    j = c % GROUP
    g1 = GROUP * n_f
    me1 = j * n_f + f

    def dev1(slot):
        return (k * GROUP + slot // n_f, slot % n_f)

    def dev2(col):
        return (col * GROUP + j, f)

    def devg(b):
        return (k * GROUP + b, f)

    barrier = pltpu.get_barrier_semaphore()
    for t in range(1, g1):
        pl.semaphore_signal(barrier, 1, device_id=dev1((me1 + t) % g1), device_id_type=MESH)
    for t in range(1, n_col):
        pl.semaphore_signal(barrier, 1, device_id=dev2((k + t) % n_col), device_id_type=MESH)
    pl.semaphore_wait(barrier, g1 - 1 + n_col - 1)

    def start_gather(src, slots, sends, recvs, count, mine, dev):
        out = []
        for t in range(1, count):
            peer = (mine + t) % count
            cp = pltpu.make_async_remote_copy(
                src_ref=src, dst_ref=slots.at[mine], send_sem=sends.at[peer],
                recv_sem=recvs.at[mine], device_id=dev(peer), device_id_type=MESH)
            cp.start()
            out.append(cp)
        return out

    def finish_gather(src, slots, sends, recvs, count, mine, dev, started):
        slots[mine] = src[...]
        for t in range(1, count):
            peer = (mine + t) % count
            pltpu.make_async_remote_copy(
                src_ref=src, dst_ref=slots.at[peer], send_sem=sends.at[peer],
                recv_sem=recvs.at[peer], device_id=dev(peer), device_id_type=MESH).wait_recv()
        for cp in started:
            cp.wait_send()
        acc = slots[0]
        for s in range(1, count):
            acc = acc + slots[s]
        return acc

    first = start_gather(val_ref, slots1, send1, recv1, g1, me1, dev1)
    outgoing = []
    for t in range(1, GROUP):
        b = (j + t) % GROUP
        cp = pltpu.make_async_remote_copy(
            src_ref=blocks_ref.at[b], dst_ref=got.at[j], send_sem=send_o.at[b],
            recv_sem=recv_o.at[j], device_id=devg(b), device_id_type=MESH)
        cp.start()
        outgoing.append(cp)
    stage[...] = finish_gather(val_ref, slots1, send1, recv1, g1, me1, dev1, first)
    second = start_gather(stage, slots2, send2, recv2, n_col, k, dev2)
    sum_ref[...] = finish_gather(stage, slots2, send2, recv2, n_col, k, dev2, second)
    got[j] = blocks_ref[j]
    for t in range(1, GROUP):
        b = (j + t) % GROUP
        pltpu.make_async_remote_copy(
            src_ref=blocks_ref.at[b], dst_ref=got.at[b], send_sem=send_o.at[b],
            recv_sem=recv_o.at[b], device_id=devg(b), device_id_type=MESH).wait_recv()
    for cp in outgoing:
        cp.wait_send()
    out_ref[...] = got[...]


def finish(blocks, v, mesh_shape):
    n_col = mesh_shape["chan"] // GROUP
    n_f = mesh_shape["freq"]
    g1 = GROUP * n_f
    tile = jnp.full((8, 128), v, jnp.float32)
    vmem = pl.BlockSpec(memory_space=pltpu.VMEM)
    out, total = pl.pallas_call(
        functools.partial(tail_kernel, n_col, n_f),
        out_shape=(jax.ShapeDtypeStruct(blocks.shape, blocks.dtype),
                   jax.ShapeDtypeStruct((8, 128), jnp.float32)),
        in_specs=[vmem, vmem],
        out_specs=(vmem, vmem),
        scratch_shapes=[
            pltpu.VMEM(blocks.shape, blocks.dtype),
            pltpu.VMEM((g1, 8, 128), jnp.float32),
            pltpu.VMEM((n_col, 8, 128), jnp.float32),
            pltpu.VMEM((8, 128), jnp.float32),
            pltpu.SemaphoreType.DMA((GROUP,)),
            pltpu.SemaphoreType.DMA((GROUP,)),
            pltpu.SemaphoreType.DMA((g1,)),
            pltpu.SemaphoreType.DMA((g1,)),
            pltpu.SemaphoreType.DMA((n_col,)),
            pltpu.SemaphoreType.DMA((n_col,)),
        ],
        compiler_params=pltpu.CompilerParams(collective_id=0, has_side_effects=True),
    )(blocks, tile)
    return out, total[0, 0]


def shards(spectra, model, channel_ok, limits, mesh_shape):
    payload = jnp.concatenate([spectra, model], axis=2)
    fl, _, rows, bw = payload.shape
    peers = lax.axis_size("chan")
    me = lax.axis_index("chan")
    j = me % GROUP
    column = me // GROUP
    sub = fl // GROUP
    band_blocks = BAND // bw
    halo_cols = -(-band_blocks // GROUP)
    nblk = GROUP * (1 + halo_cols)

    ext = gather_columns(payload, halo_cols, HALVES)

    ok_all = channel_ok.astype(jnp.float32)
    ok_wide = jnp.concatenate([ok_all, ok_all[: nblk * bw]])
    ok_ext = lax.dynamic_slice_in_dim(ok_wide, column * GROUP * bw, nblk * bw).reshape(nblk, bw)
    lim = lax.dynamic_slice_in_dim(limits, column * GROUP, GROUP)

    first = ext[:, :GROUP]
    ok_first = ok_ext[:GROUP]
    misfit_part = jnp.zeros((8, bw), jnp.float32)
    near_acc = jnp.zeros((sub, GROUP, 2, W, bw), jnp.float32)
    far_acc = [jnp.zeros((sub, 2, W, bw), jnp.float32) for _ in range(nblk)]
    sent = []
    for s in range(band_blocks, -1, -1):
        second = ext[:, s : s + GROUP]
        piece_loss, near_terms, far_terms = pair_terms(
            first, second, ok_first, ok_ext[s : s + GROUP], lim, s
        )
        misfit_part = misfit_part + piece_loss
        near_acc = near_acc + near_terms
        for bb in range(GROUP):
            far_acc[s + bb] = far_acc[s + bb] + far_terms[:, bb]
        for h in range(1, halo_cols + 1):
            if s == max(GROUP * h - GROUP + 1, 0) and h * GROUP < nblk:
                done = jnp.stack(far_acc[h * GROUP : (h + 1) * GROUP], axis=1)
                done, ext = lax.optimization_barrier((done, ext))
                first = ext[:, :GROUP]
                sent.append(permute(done, shift_pairs(peers, GROUP * h)))
    misfit_sum = 0.5 * jnp.sum(misfit_part)
    adj = near_acc + jnp.stack(far_acc[:GROUP], axis=1)
    for part in sent:
        adj = adj + part
    adj = adj * (1.0 / W)

    blocks = jnp.transpose(adj, (1, 0, 2, 3, 4))
    back, misfit_total = finish(blocks, misfit_sum, mesh_shape)
    adjoint = back.reshape(fl, 2, W, bw)

    misfit = misfit_total / float(F * bw * peers * BAND)
    return adjoint, misfit


def solution(mesh):
    mesh_shape = dict(mesh.shape)
    return jax.shard_map(
        lambda *a: shards(*a, mesh_shape),
        mesh=mesh,
        in_specs=(P("freq", None, None, "chan"), P("freq", None, None, "chan"), P(), P()),
        out_specs=(P("freq", None, None, "chan"), P()),
        check_vma=False,
    )
```

```python
import jax
import jax.numpy as jnp
from jax import lax
from jax.experimental import pallas as pl
from jax.experimental.pallas import tpu as pltpu
from jax.sharding import PartitionSpec as P
import functools

F = 256
W = 16
BAND = 1024
HALVES = 4
GROUP = 4


def permute(x, pairs):
    return lax.ppermute(x, "chan", pairs)


def shift_pairs(peers, by):
    return [(i, (i + by) % peers) for i in range(peers)]


def group_pairs(peers, t):
    return [(i, (i // GROUP) * GROUP + (i % GROUP + t) % GROUP) for i in range(peers)]


def exchange(chunks, j, peers):
    rel = jnp.roll(chunks, -j, axis=0)
    got = [rel[0]] + [permute(rel[t], group_pairs(peers, t)) for t in range(1, GROUP)]
    got = jnp.stack(got, axis=0)
    order = (j - jnp.arange(GROUP)) % GROUP
    return jnp.take(got, order, axis=0)


def pair_terms(first, second, ok_first, ok_second, limit_first, shift_blocks):
    fb, nb, _, row_count, block_width = first.shape
    row_scale = jnp.concatenate(
        [jnp.full((W,), 1.0 / W, jnp.float32), jnp.full((row_count - W,), -1.0, jnp.float32)]
    ).astype(jnp.bfloat16)
    scaled = first * row_scale[None, None, None, :, None]
    stacked_left = jnp.stack(
        [
            scaled.reshape(fb, nb, 2 * row_count, block_width),
            jnp.concatenate([scaled[:, :, 1], -scaled[:, :, 0]], axis=2),
        ],
        axis=2,
    )
    right_rows = second.reshape(fb, nb, 2 * row_count, block_width)
    cross_spec = jnp.einsum(
        "fbxrc,fbrd->fbxcd", stacked_left, right_rows, preferred_element_type=jnp.float32
    )
    row_index = lax.broadcasted_iota(jnp.int32, (block_width, block_width), 0)
    col_index = lax.broadcasted_iota(jnp.int32, (block_width, block_width), 1)
    offset = shift_blocks * block_width + col_index - row_index
    inside = ((offset[None] >= 1) & (offset[None] <= limit_first[:, None, None])).astype(jnp.float32)
    live_mask = ok_first[:, :, None] * ok_second[:, None, :] * inside
    residual = cross_spec * live_mask[None, :, None]
    squares = (residual * residual).reshape(-1, block_width // 8, 8, block_width)
    piece_loss = jnp.sum(squares, axis=(0, 1))
    rounded = residual.astype(jnp.bfloat16)
    far_spec = second[:, :, :, :W].reshape(fb, nb, 2 * W, block_width)
    near_spec = first[:, :, :, :W].reshape(fb, nb, 2 * W, block_width)
    toward = jnp.einsum("fbxcd,fbvd->fbxvc", rounded, far_spec, preferred_element_type=jnp.float32)
    first_real = toward[:, :, 0, :W] - toward[:, :, 1, W:]
    first_imag = toward[:, :, 0, W:] + toward[:, :, 1, :W]
    backward = jnp.einsum("fbxcd,fbvc->fbxvd", rounded, near_spec, preferred_element_type=jnp.float32)
    second_real = backward[:, :, 0, :W] + backward[:, :, 1, W:]
    second_imag = backward[:, :, 0, W:] - backward[:, :, 1, :W]
    return (
        piece_loss,
        jnp.stack([first_real, first_imag], axis=2),
        jnp.stack([second_real, second_imag], axis=2),
    )


MESH = pl.DeviceIdType.MESH

def head_kernel(n_halves, halo_cols, chunks_ref, out_ref, held, send_e, recv_e, send_h, recv_h, own_sem):
    c = lax.axis_index("chan")
    f = lax.axis_index("freq")
    peers = lax.axis_size("chan")
    k = c // GROUP
    j = c % GROUP
    back = 1 + halo_cols

    def devg(b):
        return (k * GROUP + b, f)

    def devh(h, sign):
        return ((c + sign * GROUP * h) % peers, f)

    barrier = pltpu.get_barrier_semaphore()
    for t in range(1, GROUP):
        pl.semaphore_signal(barrier, 1, device_id=devg((j + t) % GROUP), device_id_type=MESH)
    for h in range(1, halo_cols + 1):
        pl.semaphore_signal(barrier, 1, device_id=devh(h, -1), device_id_type=MESH)
        pl.semaphore_signal(barrier, 1, device_id=devh(h, 1), device_id_type=MESH)
    pl.semaphore_wait(barrier, GROUP - 1 + 2 * halo_cols)

    sends = []
    locals_ = []
    for half in range(n_halves):
        for t in range(1, GROUP):
            b = (j + t) % GROUP
            cp = pltpu.make_async_remote_copy(
                src_ref=chunks_ref.at[b, half], dst_ref=held.at[half, 0, j],
                send_sem=send_e.at[half, b], recv_sem=recv_e.at[half, j],
                device_id=devg(b), device_id_type=MESH)
            cp.start()
            sends.append(cp)
        cp = pltpu.make_async_copy(chunks_ref.at[j, half], held.at[half, 0, j], own_sem.at[half])
        cp.start()
        locals_.append(cp)
    for half in range(n_halves):
        locals_[half].wait()
        for t in range(1, GROUP):
            b = (j + t) % GROUP
            pltpu.make_async_remote_copy(
                src_ref=chunks_ref.at[b, half], dst_ref=held.at[half, 0, b],
                send_sem=send_e.at[half, b], recv_sem=recv_e.at[half, b],
                device_id=devg(b), device_id_type=MESH).wait_recv()
        for h in range(1, halo_cols + 1):
            cp = pltpu.make_async_remote_copy(
                src_ref=held.at[half, 0], dst_ref=held.at[half, h],
                send_sem=send_h.at[half, h], recv_sem=recv_h.at[half, h],
                device_id=devh(h, -1), device_id_type=MESH)
            cp.start()
            sends.append(cp)
        cp = pltpu.make_async_remote_copy(
            src_ref=held.at[half, 0], dst_ref=held.at[half, back],
            send_sem=send_h.at[half, back], recv_sem=recv_h.at[half, back],
            device_id=devh(halo_cols, 1), device_id_type=MESH)
        cp.start()
        sends.append(cp)
    for half in range(n_halves):
        for h in range(1, halo_cols + 1):
            pltpu.make_async_remote_copy(
                src_ref=held.at[half, 0], dst_ref=held.at[half, h],
                send_sem=send_h.at[half, h], recv_sem=recv_h.at[half, h],
                device_id=devh(h, 1), device_id_type=MESH).wait_recv()
        pltpu.make_async_remote_copy(
            src_ref=held.at[half, 0], dst_ref=held.at[half, back],
            send_sem=send_h.at[half, back], recv_sem=recv_h.at[half, back],
            device_id=devh(halo_cols, -1), device_id_type=MESH).wait_recv()
    for cp in sends:
        cp.wait_send()
    out_ref[...] = held[...]


def gather_columns(payload, halo_cols, n_halves):
    fl, two, rows, bw = payload.shape
    q = fl // GROUP // n_halves
    chunks = payload.reshape(GROUP, n_halves, q, two, rows, bw)
    shape = (n_halves, 2 + halo_cols, GROUP, q, two, rows, bw)
    vmem = pl.BlockSpec(memory_space=pltpu.VMEM)
    held = pl.pallas_call(
        functools.partial(head_kernel, n_halves, halo_cols),
        out_shape=jax.ShapeDtypeStruct(shape, payload.dtype),
        in_specs=[vmem],
        out_specs=vmem,
        scratch_shapes=[
            pltpu.VMEM(shape, payload.dtype),
            pltpu.SemaphoreType.DMA((n_halves, GROUP)),
            pltpu.SemaphoreType.DMA((n_halves, GROUP)),
            pltpu.SemaphoreType.DMA((n_halves, 2 + halo_cols)),
            pltpu.SemaphoreType.DMA((n_halves, 2 + halo_cols)),
            pltpu.SemaphoreType.DMA((n_halves,)),
        ],
        compiler_params=pltpu.CompilerParams(collective_id=1, has_side_effects=True),
    )(chunks)
    held = jnp.transpose(held, (0, 3, 1, 2, 4, 5, 6))
    return held.reshape(n_halves * q, (2 + halo_cols) * GROUP, two, rows, bw)


def tail_kernel(n_col, n_f, blocks_ref, val_ref, out_ref, sum_ref,
                got, slots1, slots2, stage, send_o, recv_o, send1, recv1, send2, recv2):
    c = lax.axis_index("chan")
    f = lax.axis_index("freq")
    k = c // GROUP
    j = c % GROUP
    g1 = GROUP * n_f
    me1 = j * n_f + f

    def dev1(slot):
        return (k * GROUP + slot // n_f, slot % n_f)

    def dev2(col):
        return (col * GROUP + j, f)

    def devg(b):
        return (k * GROUP + b, f)

    barrier = pltpu.get_barrier_semaphore()
    for t in range(1, g1):
        pl.semaphore_signal(barrier, 1, device_id=dev1((me1 + t) % g1), device_id_type=MESH)
    for t in range(1, n_col):
        pl.semaphore_signal(barrier, 1, device_id=dev2((k + t) % n_col), device_id_type=MESH)
    pl.semaphore_wait(barrier, g1 - 1 + n_col - 1)

    def start_gather(src, slots, sends, recvs, count, mine, dev):
        out = []
        for t in range(1, count):
            peer = (mine + t) % count
            cp = pltpu.make_async_remote_copy(
                src_ref=src, dst_ref=slots.at[mine], send_sem=sends.at[peer],
                recv_sem=recvs.at[mine], device_id=dev(peer), device_id_type=MESH)
            cp.start()
            out.append(cp)
        return out

    def finish_gather(src, slots, sends, recvs, count, mine, dev, started):
        slots[mine] = src[...]
        for t in range(1, count):
            peer = (mine + t) % count
            pltpu.make_async_remote_copy(
                src_ref=src, dst_ref=slots.at[peer], send_sem=sends.at[peer],
                recv_sem=recvs.at[peer], device_id=dev(peer), device_id_type=MESH).wait_recv()
        for cp in started:
            cp.wait_send()
        acc = slots[0]
        for s in range(1, count):
            acc = acc + slots[s]
        return acc

    first = start_gather(val_ref, slots1, send1, recv1, g1, me1, dev1)
    outgoing = []
    for t in range(1, GROUP):
        b = (j + t) % GROUP
        cp = pltpu.make_async_remote_copy(
            src_ref=blocks_ref.at[b], dst_ref=got.at[j], send_sem=send_o.at[b],
            recv_sem=recv_o.at[j], device_id=devg(b), device_id_type=MESH)
        cp.start()
        outgoing.append(cp)
    stage[...] = finish_gather(val_ref, slots1, send1, recv1, g1, me1, dev1, first)
    second = start_gather(stage, slots2, send2, recv2, n_col, k, dev2)
    sum_ref[...] = finish_gather(stage, slots2, send2, recv2, n_col, k, dev2, second)
    got[j] = blocks_ref[j]
    for t in range(1, GROUP):
        b = (j + t) % GROUP
        pltpu.make_async_remote_copy(
            src_ref=blocks_ref.at[b], dst_ref=got.at[b], send_sem=send_o.at[b],
            recv_sem=recv_o.at[b], device_id=devg(b), device_id_type=MESH).wait_recv()
    for cp in outgoing:
        cp.wait_send()
    out_ref[...] = got[...]


def finish(blocks, v, mesh_shape):
    n_col = mesh_shape["chan"] // GROUP
    n_f = mesh_shape["freq"]
    g1 = GROUP * n_f
    tile = jnp.full((8, 128), v, jnp.float32)
    vmem = pl.BlockSpec(memory_space=pltpu.VMEM)
    out, total = pl.pallas_call(
        functools.partial(tail_kernel, n_col, n_f),
        out_shape=(jax.ShapeDtypeStruct(blocks.shape, blocks.dtype),
                   jax.ShapeDtypeStruct((8, 128), jnp.float32)),
        in_specs=[vmem, vmem],
        out_specs=(vmem, vmem),
        scratch_shapes=[
            pltpu.VMEM(blocks.shape, blocks.dtype),
            pltpu.VMEM((g1, 8, 128), jnp.float32),
            pltpu.VMEM((n_col, 8, 128), jnp.float32),
            pltpu.VMEM((8, 128), jnp.float32),
            pltpu.SemaphoreType.DMA((GROUP,)),
            pltpu.SemaphoreType.DMA((GROUP,)),
            pltpu.SemaphoreType.DMA((g1,)),
            pltpu.SemaphoreType.DMA((g1,)),
            pltpu.SemaphoreType.DMA((n_col,)),
            pltpu.SemaphoreType.DMA((n_col,)),
        ],
        compiler_params=pltpu.CompilerParams(collective_id=0, has_side_effects=True),
    )(blocks, tile)
    return out, total[0, 0]


def shards(spectra, model, channel_ok, limits, mesh_shape):
    payload = jnp.concatenate([spectra, model], axis=2)
    fl, _, rows, bw = payload.shape
    peers = lax.axis_size("chan")
    me = lax.axis_index("chan")
    j = me % GROUP
    column = me // GROUP
    sub = fl // GROUP
    band_blocks = BAND // bw
    halo_cols = -(-band_blocks // GROUP)
    nblk = GROUP * (1 + halo_cols)

    full = gather_columns(payload, halo_cols, HALVES)
    ext = full[:, :nblk]
    behind = full[:, nblk:]

    ok_all = channel_ok.astype(jnp.float32)
    ok_wide = jnp.concatenate([ok_all, ok_all[: nblk * bw]])
    ok_ext = lax.dynamic_slice_in_dim(ok_wide, column * GROUP * bw, nblk * bw).reshape(nblk, bw)
    lim = lax.dynamic_slice_in_dim(limits, column * GROUP, GROUP)
    back_col = (column - halo_cols) % (peers // GROUP)
    ok_back = lax.dynamic_slice_in_dim(ok_all, back_col * GROUP * bw, GROUP * bw).reshape(GROUP, bw)
    lim_back = lax.dynamic_slice_in_dim(limits, back_col * GROUP, GROUP)

    first = ext[:, :GROUP]
    ok_first = ok_ext[:GROUP]
    misfit_part = jnp.zeros((8, bw), jnp.float32)
    near_acc = jnp.zeros((sub, GROUP, 2, W, bw), jnp.float32)
    far_acc = [jnp.zeros((sub, 2, W, bw), jnp.float32) for _ in range(nblk)]
    sent = []
    for s in range(band_blocks, -1, -1):
        second = ext[:, s : s + GROUP]
        piece_loss, near_terms, far_terms = pair_terms(
            first, second, ok_first, ok_ext[s : s + GROUP], lim, s
        )
        misfit_part = misfit_part + piece_loss
        near_acc = near_acc + near_terms
        for bb in range(GROUP):
            far_acc[s + bb] = far_acc[s + bb] + far_terms[:, bb]
        for h in range(1, halo_cols):
            if s == max(GROUP * h - GROUP + 1, 0):
                done = jnp.stack(far_acc[h * GROUP : (h + 1) * GROUP], axis=1)
                done, ext = lax.optimization_barrier((done, ext))
                first = ext[:, :GROUP]
                sent.append(permute(done, shift_pairs(peers, GROUP * h)))
    misfit_sum = 0.5 * jnp.sum(misfit_part)
    for d in range(GROUP):
        _, _, back_terms = pair_terms(
            behind[:, d:], ext[:, : GROUP - d], ok_back[d:], ok_ext[: GROUP - d],
            lim_back[d:], GROUP * halo_cols - d,
        )
        sent.append(jnp.pad(back_terms, ((0, 0), (0, d), (0, 0), (0, 0), (0, 0))))
    adj = near_acc + jnp.stack(far_acc[:GROUP], axis=1)
    for part in sent:
        adj = adj + part
    adj = adj * (1.0 / W)

    blocks = jnp.transpose(adj, (1, 0, 2, 3, 4))
    back, misfit_total = finish(blocks, misfit_sum, mesh_shape)
    adjoint = back.reshape(fl, 2, W, bw)

    misfit = misfit_total / float(F * bw * peers * BAND)
    return adjoint, misfit


def solution(mesh):
    mesh_shape = dict(mesh.shape)
    return jax.shard_map(
        lambda *a: shards(*a, mesh_shape),
        mesh=mesh,
        in_specs=(P("freq", None, None, "chan"), P("freq", None, None, "chan"), P(), P()),
        out_specs=(P("freq", None, None, "chan"), P()),
        check_vma=False,
    )
```

```python
import jax
import jax.numpy as jnp
from jax import lax
from jax.experimental import pallas as pl
from jax.experimental.pallas import tpu as pltpu
from jax.sharding import PartitionSpec as P
import functools

F = 256
W = 16
BAND = 1024
HALVES = 4
GROUP = 4


def permute(x, pairs):
    return lax.ppermute(x, "chan", pairs)


def shift_pairs(peers, by):
    return [(i, (i + by) % peers) for i in range(peers)]


def group_pairs(peers, t):
    return [(i, (i // GROUP) * GROUP + (i % GROUP + t) % GROUP) for i in range(peers)]


def exchange(chunks, j, peers):
    rel = jnp.roll(chunks, -j, axis=0)
    got = [rel[0]] + [permute(rel[t], group_pairs(peers, t)) for t in range(1, GROUP)]
    got = jnp.stack(got, axis=0)
    order = (j - jnp.arange(GROUP)) % GROUP
    return jnp.take(got, order, axis=0)


def pair_terms(first, second, ok_first, ok_second, limit_first, shift_blocks):
    fb, nb, _, row_count, block_width = first.shape
    row_scale = jnp.concatenate(
        [jnp.full((W,), 1.0 / W, jnp.float32), jnp.full((row_count - W,), -1.0, jnp.float32)]
    ).astype(jnp.bfloat16)
    scaled = first * row_scale[None, None, None, :, None]
    stacked_left = jnp.stack(
        [
            scaled.reshape(fb, nb, 2 * row_count, block_width),
            jnp.concatenate([scaled[:, :, 1], -scaled[:, :, 0]], axis=2),
        ],
        axis=2,
    )
    right_rows = second.reshape(fb, nb, 2 * row_count, block_width)
    cross_spec = jnp.einsum(
        "fbxrc,fbrd->fbxcd", stacked_left, right_rows, preferred_element_type=jnp.float32
    )
    row_index = lax.broadcasted_iota(jnp.int32, (block_width, block_width), 0)
    col_index = lax.broadcasted_iota(jnp.int32, (block_width, block_width), 1)
    offset = shift_blocks * block_width + col_index - row_index
    inside = ((offset[None] >= 1) & (offset[None] <= limit_first[:, None, None])).astype(jnp.float32)
    live_mask = ok_first[:, :, None] * ok_second[:, None, :] * inside
    residual = cross_spec * live_mask[None, :, None]
    squares = (residual * residual).reshape(-1, block_width // 8, 8, block_width)
    piece_loss = jnp.sum(squares, axis=(0, 1))
    rounded = residual.astype(jnp.bfloat16)
    far_spec = second[:, :, :, :W].reshape(fb, nb, 2 * W, block_width)
    near_spec = first[:, :, :, :W].reshape(fb, nb, 2 * W, block_width)
    toward = jnp.einsum("fbxcd,fbvd->fbxvc", rounded, far_spec, preferred_element_type=jnp.float32)
    first_real = toward[:, :, 0, :W] - toward[:, :, 1, W:]
    first_imag = toward[:, :, 0, W:] + toward[:, :, 1, :W]
    backward = jnp.einsum("fbxcd,fbvc->fbxvd", rounded, near_spec, preferred_element_type=jnp.float32)
    second_real = backward[:, :, 0, :W] + backward[:, :, 1, W:]
    second_imag = backward[:, :, 0, W:] - backward[:, :, 1, :W]
    return (
        piece_loss,
        jnp.stack([first_real, first_imag], axis=2),
        jnp.stack([second_real, second_imag], axis=2),
    )


MESH = pl.DeviceIdType.MESH

def head_kernel(n_halves, halo_cols, chunks_ref, out_ref, held, send_e, recv_e, send_h, recv_h, own_sem):
    c = lax.axis_index("chan")
    f = lax.axis_index("freq")
    peers = lax.axis_size("chan")
    k = c // GROUP
    j = c % GROUP

    def devg(b):
        return (k * GROUP + b, f)

    def devh(h, sign):
        return ((c + sign * GROUP * h) % peers, f)

    barrier = pltpu.get_barrier_semaphore()
    for t in range(1, GROUP):
        pl.semaphore_signal(barrier, 1, device_id=devg((j + t) % GROUP), device_id_type=MESH)
    for h in range(1, halo_cols + 1):
        pl.semaphore_signal(barrier, 1, device_id=devh(h, -1), device_id_type=MESH)
        pl.semaphore_signal(barrier, 1, device_id=devh(h, 1), device_id_type=MESH)
    pl.semaphore_wait(barrier, GROUP - 1 + 2 * halo_cols)

    sends = []
    locals_ = []
    for half in range(n_halves):
        for t in range(1, GROUP):
            b = (j + t) % GROUP
            cp = pltpu.make_async_remote_copy(
                src_ref=chunks_ref.at[b, half], dst_ref=held.at[half, 0, j],
                send_sem=send_e.at[half, b], recv_sem=recv_e.at[half, j],
                device_id=devg(b), device_id_type=MESH)
            cp.start()
            sends.append(cp)
        cp = pltpu.make_async_copy(chunks_ref.at[j, half], held.at[half, 0, j], own_sem.at[half])
        cp.start()
        locals_.append(cp)
    for half in range(n_halves):
        locals_[half].wait()
        for t in range(1, GROUP):
            b = (j + t) % GROUP
            pltpu.make_async_remote_copy(
                src_ref=chunks_ref.at[b, half], dst_ref=held.at[half, 0, b],
                send_sem=send_e.at[half, b], recv_sem=recv_e.at[half, b],
                device_id=devg(b), device_id_type=MESH).wait_recv()
        for h in range(1, halo_cols + 1):
            cp = pltpu.make_async_remote_copy(
                src_ref=held.at[half, 0], dst_ref=held.at[half, h],
                send_sem=send_h.at[half, h], recv_sem=recv_h.at[half, h],
                device_id=devh(h, -1), device_id_type=MESH)
            cp.start()
            sends.append(cp)
    for half in range(n_halves):
        for h in range(1, halo_cols + 1):
            pltpu.make_async_remote_copy(
                src_ref=held.at[half, 0], dst_ref=held.at[half, h],
                send_sem=send_h.at[half, h], recv_sem=recv_h.at[half, h],
                device_id=devh(h, 1), device_id_type=MESH).wait_recv()
    for cp in sends:
        cp.wait_send()
    out_ref[...] = held[...]


def gather_columns(payload, halo_cols, n_halves):
    fl, two, rows, bw = payload.shape
    q = fl // GROUP // n_halves
    chunks = payload.reshape(GROUP, n_halves, q, two, rows, bw)
    shape = (n_halves, 1 + halo_cols, GROUP, q, two, rows, bw)
    vmem = pl.BlockSpec(memory_space=pltpu.VMEM)
    held = pl.pallas_call(
        functools.partial(head_kernel, n_halves, halo_cols),
        out_shape=jax.ShapeDtypeStruct(shape, payload.dtype),
        in_specs=[vmem],
        out_specs=vmem,
        scratch_shapes=[
            pltpu.VMEM(shape, payload.dtype),
            pltpu.SemaphoreType.DMA((n_halves, GROUP)),
            pltpu.SemaphoreType.DMA((n_halves, GROUP)),
            pltpu.SemaphoreType.DMA((n_halves, 1 + halo_cols)),
            pltpu.SemaphoreType.DMA((n_halves, 1 + halo_cols)),
            pltpu.SemaphoreType.DMA((n_halves,)),
        ],
        compiler_params=pltpu.CompilerParams(collective_id=1, has_side_effects=True),
    )(chunks)
    held = jnp.transpose(held, (0, 3, 1, 2, 4, 5, 6))
    return held.reshape(n_halves * q, (1 + halo_cols) * GROUP, two, rows, bw)


def tail_kernel(n_col, n_f, blocks_ref, val_ref, out_ref, sum_ref,
                got, slots1, slots2, stage, send_o, recv_o, send1, recv1, send2, recv2):
    c = lax.axis_index("chan")
    f = lax.axis_index("freq")
    k = c // GROUP
    j = c % GROUP
    g1 = GROUP * n_f
    me1 = j * n_f + f

    def dev1(slot):
        return (k * GROUP + slot // n_f, slot % n_f)

    def dev2(col):
        return (col * GROUP + j, f)

    def devg(b):
        return (k * GROUP + b, f)

    barrier = pltpu.get_barrier_semaphore()
    for t in range(1, g1):
        pl.semaphore_signal(barrier, 1, device_id=dev1((me1 + t) % g1), device_id_type=MESH)
    for t in range(1, n_col):
        pl.semaphore_signal(barrier, 1, device_id=dev2((k + t) % n_col), device_id_type=MESH)
    pl.semaphore_wait(barrier, g1 - 1 + n_col - 1)

    def start_gather(src, slots, sends, recvs, count, mine, dev):
        out = []
        for t in range(1, count):
            peer = (mine + t) % count
            cp = pltpu.make_async_remote_copy(
                src_ref=src, dst_ref=slots.at[mine], send_sem=sends.at[peer],
                recv_sem=recvs.at[mine], device_id=dev(peer), device_id_type=MESH)
            cp.start()
            out.append(cp)
        return out

    def finish_gather(src, slots, sends, recvs, count, mine, dev, started):
        slots[mine] = src[...]
        for t in range(1, count):
            peer = (mine + t) % count
            pltpu.make_async_remote_copy(
                src_ref=src, dst_ref=slots.at[peer], send_sem=sends.at[peer],
                recv_sem=recvs.at[peer], device_id=dev(peer), device_id_type=MESH).wait_recv()
        for cp in started:
            cp.wait_send()
        acc = slots[0]
        for s in range(1, count):
            acc = acc + slots[s]
        return acc

    first = start_gather(val_ref, slots1, send1, recv1, g1, me1, dev1)
    outgoing = []
    for t in range(1, GROUP):
        b = (j + t) % GROUP
        cp = pltpu.make_async_remote_copy(
            src_ref=blocks_ref.at[b], dst_ref=got.at[j], send_sem=send_o.at[b],
            recv_sem=recv_o.at[j], device_id=devg(b), device_id_type=MESH)
        cp.start()
        outgoing.append(cp)
    stage[...] = finish_gather(val_ref, slots1, send1, recv1, g1, me1, dev1, first)
    second = start_gather(stage, slots2, send2, recv2, n_col, k, dev2)
    sum_ref[...] = finish_gather(stage, slots2, send2, recv2, n_col, k, dev2, second)
    got[j] = blocks_ref[j]
    for t in range(1, GROUP):
        b = (j + t) % GROUP
        pltpu.make_async_remote_copy(
            src_ref=blocks_ref.at[b], dst_ref=got.at[b], send_sem=send_o.at[b],
            recv_sem=recv_o.at[b], device_id=devg(b), device_id_type=MESH).wait_recv()
    for cp in outgoing:
        cp.wait_send()
    out_ref[...] = got[...]


def finish(blocks, v, mesh_shape):
    n_col = mesh_shape["chan"] // GROUP
    n_f = mesh_shape["freq"]
    g1 = GROUP * n_f
    tile = jnp.full((8, 128), v, jnp.float32)
    vmem = pl.BlockSpec(memory_space=pltpu.VMEM)
    out, total = pl.pallas_call(
        functools.partial(tail_kernel, n_col, n_f),
        out_shape=(jax.ShapeDtypeStruct(blocks.shape, blocks.dtype),
                   jax.ShapeDtypeStruct((8, 128), jnp.float32)),
        in_specs=[vmem, vmem],
        out_specs=(vmem, vmem),
        scratch_shapes=[
            pltpu.VMEM(blocks.shape, blocks.dtype),
            pltpu.VMEM((g1, 8, 128), jnp.float32),
            pltpu.VMEM((n_col, 8, 128), jnp.float32),
            pltpu.VMEM((8, 128), jnp.float32),
            pltpu.SemaphoreType.DMA((GROUP,)),
            pltpu.SemaphoreType.DMA((GROUP,)),
            pltpu.SemaphoreType.DMA((g1,)),
            pltpu.SemaphoreType.DMA((g1,)),
            pltpu.SemaphoreType.DMA((n_col,)),
            pltpu.SemaphoreType.DMA((n_col,)),
        ],
        compiler_params=pltpu.CompilerParams(collective_id=0, has_side_effects=True),
    )(blocks, tile)
    return out, total[0, 0]


def shards(spectra, model, channel_ok, limits, mesh_shape):
    payload = jnp.concatenate([spectra, model], axis=2)
    fl, _, rows, bw = payload.shape
    peers = lax.axis_size("chan")
    me = lax.axis_index("chan")
    j = me % GROUP
    column = me // GROUP
    sub = fl // GROUP
    band_blocks = BAND // bw
    halo_cols = -(-band_blocks // GROUP)
    nblk = GROUP * (1 + halo_cols)

    ext = gather_columns(payload, halo_cols, HALVES)

    ok_all = channel_ok.astype(jnp.float32)
    ok_wide = jnp.concatenate([ok_all, ok_all[: nblk * bw]])
    ok_ext = lax.dynamic_slice_in_dim(ok_wide, column * GROUP * bw, nblk * bw).reshape(nblk, bw)
    lim = lax.dynamic_slice_in_dim(limits, column * GROUP, GROUP)

    first = ext[:, :GROUP]
    ok_first = ok_ext[:GROUP]
    misfit_part = jnp.zeros((8, bw), jnp.float32)
    near_acc = jnp.zeros((sub, GROUP, 2, W, bw), jnp.float32)
    far_acc = [jnp.zeros((sub, 2, W, bw), jnp.float32) for _ in range(nblk)]
    sent = []
    for s in range(band_blocks, -1, -1):
        second = ext[:, s : s + GROUP]
        piece_loss, near_terms, far_terms = pair_terms(
            first, second, ok_first, ok_ext[s : s + GROUP], lim, s
        )
        misfit_part = misfit_part + piece_loss
        near_acc = near_acc + near_terms
        for bb in range(GROUP):
            far_acc[s + bb] = far_acc[s + bb] + far_terms[:, bb]
        for h in range(1, halo_cols + 1):
            if s == max(GROUP * h - GROUP + 1, 0) and h * GROUP < nblk:
                done = jnp.stack(far_acc[h * GROUP : (h + 1) * GROUP], axis=1)
                done, ext = lax.optimization_barrier((done, ext))
                first = ext[:, :GROUP]
                sent.append(permute(done, shift_pairs(peers, GROUP * h)))
    misfit_sum = 0.5 * jnp.sum(misfit_part)
    adj = near_acc + jnp.stack(far_acc[:GROUP], axis=1)
    for part in sent:
        adj = adj + part

    blocks = jnp.transpose(adj, (1, 0, 2, 3, 4))
    back, misfit_total = finish(blocks, misfit_sum, mesh_shape)
    adjoint = back.reshape(fl, 2, W, bw) * (1.0 / W)

    misfit = misfit_total / float(F * bw * peers * BAND)
    return adjoint, misfit


def solution(mesh):
    mesh_shape = dict(mesh.shape)
    return jax.shard_map(
        lambda *a: shards(*a, mesh_shape),
        mesh=mesh,
        in_specs=(P("freq", None, None, "chan"), P("freq", None, None, "chan"), P(), P()),
        out_specs=(P("freq", None, None, "chan"), P()),
        check_vma=False,
    )
```

```python
import jax
import jax.numpy as jnp
from jax import lax
from jax.experimental import pallas as pl
from jax.experimental.pallas import tpu as pltpu
from jax.sharding import PartitionSpec as P
import functools

F = 256
W = 16
BAND = 1024
HALVES = 8
GROUP = 4


def permute(x, pairs):
    return lax.ppermute(x, "chan", pairs)


def shift_pairs(peers, by):
    return [(i, (i + by) % peers) for i in range(peers)]


def group_pairs(peers, t):
    return [(i, (i // GROUP) * GROUP + (i % GROUP + t) % GROUP) for i in range(peers)]


def exchange(chunks, j, peers):
    rel = jnp.roll(chunks, -j, axis=0)
    got = [rel[0]] + [permute(rel[t], group_pairs(peers, t)) for t in range(1, GROUP)]
    got = jnp.stack(got, axis=0)
    order = (j - jnp.arange(GROUP)) % GROUP
    return jnp.take(got, order, axis=0)


def pair_terms(first, second, ok_first, ok_second, limit_first, shift_blocks):
    fb, nb, _, row_count, block_width = first.shape
    row_scale = jnp.concatenate(
        [jnp.full((W,), 1.0 / W, jnp.float32), jnp.full((row_count - W,), -1.0, jnp.float32)]
    ).astype(jnp.bfloat16)
    scaled = first * row_scale[None, None, None, :, None]
    stacked_left = jnp.stack(
        [
            scaled.reshape(fb, nb, 2 * row_count, block_width),
            jnp.concatenate([scaled[:, :, 1], -scaled[:, :, 0]], axis=2),
        ],
        axis=2,
    )
    right_rows = second.reshape(fb, nb, 2 * row_count, block_width)
    cross_spec = jnp.einsum(
        "fbxrc,fbrd->fbxcd", stacked_left, right_rows, preferred_element_type=jnp.float32
    )
    row_index = lax.broadcasted_iota(jnp.int32, (block_width, block_width), 0)
    col_index = lax.broadcasted_iota(jnp.int32, (block_width, block_width), 1)
    offset = shift_blocks * block_width + col_index - row_index
    inside = ((offset[None] >= 1) & (offset[None] <= limit_first[:, None, None])).astype(jnp.float32)
    live_mask = ok_first[:, :, None] * ok_second[:, None, :] * inside
    residual = cross_spec * live_mask[None, :, None]
    squares = (residual * residual).reshape(-1, block_width // 8, 8, block_width)
    piece_loss = jnp.sum(squares, axis=(0, 1))
    rounded = residual.astype(jnp.bfloat16)
    far_spec = second[:, :, :, :W].reshape(fb, nb, 2 * W, block_width)
    near_spec = first[:, :, :, :W].reshape(fb, nb, 2 * W, block_width)
    toward = jnp.einsum("fbxcd,fbvd->fbxvc", rounded, far_spec, preferred_element_type=jnp.float32)
    first_real = toward[:, :, 0, :W] - toward[:, :, 1, W:]
    first_imag = toward[:, :, 0, W:] + toward[:, :, 1, :W]
    backward = jnp.einsum("fbxcd,fbvc->fbxvd", rounded, near_spec, preferred_element_type=jnp.float32)
    second_real = backward[:, :, 0, :W] + backward[:, :, 1, W:]
    second_imag = backward[:, :, 0, W:] - backward[:, :, 1, :W]
    return (
        piece_loss,
        jnp.stack([first_real, first_imag], axis=2),
        jnp.stack([second_real, second_imag], axis=2),
    )


MESH = pl.DeviceIdType.MESH

def head_kernel(n_halves, halo_cols, chunks_ref, out_ref, held, send_e, recv_e, send_h, recv_h, own_sem):
    c = lax.axis_index("chan")
    f = lax.axis_index("freq")
    peers = lax.axis_size("chan")
    k = c // GROUP
    j = c % GROUP

    def devg(b):
        return (k * GROUP + b, f)

    def devh(h, sign):
        return ((c + sign * GROUP * h) % peers, f)

    barrier = pltpu.get_barrier_semaphore()
    for t in range(1, GROUP):
        pl.semaphore_signal(barrier, 1, device_id=devg((j + t) % GROUP), device_id_type=MESH)
    for h in range(1, halo_cols + 1):
        pl.semaphore_signal(barrier, 1, device_id=devh(h, -1), device_id_type=MESH)
        pl.semaphore_signal(barrier, 1, device_id=devh(h, 1), device_id_type=MESH)
    pl.semaphore_wait(barrier, GROUP - 1 + 2 * halo_cols)

    sends = []
    locals_ = []
    for half in range(n_halves):
        for t in range(1, GROUP):
            b = (j + t) % GROUP
            cp = pltpu.make_async_remote_copy(
                src_ref=chunks_ref.at[b, half], dst_ref=held.at[half, 0, j],
                send_sem=send_e.at[half, b], recv_sem=recv_e.at[half, j],
                device_id=devg(b), device_id_type=MESH)
            cp.start()
            sends.append(cp)
        cp = pltpu.make_async_copy(chunks_ref.at[j, half], held.at[half, 0, j], own_sem.at[half])
        cp.start()
        locals_.append(cp)
    for half in range(n_halves):
        locals_[half].wait()
        for t in range(1, GROUP):
            b = (j + t) % GROUP
            pltpu.make_async_remote_copy(
                src_ref=chunks_ref.at[b, half], dst_ref=held.at[half, 0, b],
                send_sem=send_e.at[half, b], recv_sem=recv_e.at[half, b],
                device_id=devg(b), device_id_type=MESH).wait_recv()
        for h in range(1, halo_cols + 1):
            cp = pltpu.make_async_remote_copy(
                src_ref=held.at[half, 0], dst_ref=held.at[half, h],
                send_sem=send_h.at[half, h], recv_sem=recv_h.at[half, h],
                device_id=devh(h, -1), device_id_type=MESH)
            cp.start()
            sends.append(cp)
    for half in range(n_halves):
        for h in range(1, halo_cols + 1):
            pltpu.make_async_remote_copy(
                src_ref=held.at[half, 0], dst_ref=held.at[half, h],
                send_sem=send_h.at[half, h], recv_sem=recv_h.at[half, h],
                device_id=devh(h, 1), device_id_type=MESH).wait_recv()
    for cp in sends:
        cp.wait_send()
    out_ref[...] = held[...]


def gather_columns(payload, halo_cols, n_halves):
    fl, two, rows, bw = payload.shape
    q = fl // GROUP // n_halves
    chunks = payload.reshape(GROUP, n_halves, q, two, rows, bw)
    shape = (n_halves, 1 + halo_cols, GROUP, q, two, rows, bw)
    vmem = pl.BlockSpec(memory_space=pltpu.VMEM)
    held = pl.pallas_call(
        functools.partial(head_kernel, n_halves, halo_cols),
        out_shape=jax.ShapeDtypeStruct(shape, payload.dtype),
        in_specs=[vmem],
        out_specs=vmem,
        scratch_shapes=[
            pltpu.VMEM(shape, payload.dtype),
            pltpu.SemaphoreType.DMA((n_halves, GROUP)),
            pltpu.SemaphoreType.DMA((n_halves, GROUP)),
            pltpu.SemaphoreType.DMA((n_halves, 1 + halo_cols)),
            pltpu.SemaphoreType.DMA((n_halves, 1 + halo_cols)),
            pltpu.SemaphoreType.DMA((n_halves,)),
        ],
        compiler_params=pltpu.CompilerParams(collective_id=1, has_side_effects=True),
    )(chunks)
    held = jnp.transpose(held, (0, 3, 1, 2, 4, 5, 6))
    return held.reshape(n_halves * q, (1 + halo_cols) * GROUP, two, rows, bw)


def tail_kernel(n_col, n_f, blocks_ref, val_ref, out_ref, sum_ref,
                got, slots1, slots2, stage, send_o, recv_o, send1, recv1, send2, recv2):
    c = lax.axis_index("chan")
    f = lax.axis_index("freq")
    k = c // GROUP
    j = c % GROUP
    g1 = GROUP * n_f
    me1 = j * n_f + f

    def dev1(slot):
        return (k * GROUP + slot // n_f, slot % n_f)

    def dev2(col):
        return (col * GROUP + j, f)

    def devg(b):
        return (k * GROUP + b, f)

    barrier = pltpu.get_barrier_semaphore()
    for t in range(1, g1):
        pl.semaphore_signal(barrier, 1, device_id=dev1((me1 + t) % g1), device_id_type=MESH)
    for t in range(1, n_col):
        pl.semaphore_signal(barrier, 1, device_id=dev2((k + t) % n_col), device_id_type=MESH)
    pl.semaphore_wait(barrier, g1 - 1 + n_col - 1)

    def start_gather(src, slots, sends, recvs, count, mine, dev):
        out = []
        for t in range(1, count):
            peer = (mine + t) % count
            cp = pltpu.make_async_remote_copy(
                src_ref=src, dst_ref=slots.at[mine], send_sem=sends.at[peer],
                recv_sem=recvs.at[mine], device_id=dev(peer), device_id_type=MESH)
            cp.start()
            out.append(cp)
        return out

    def finish_gather(src, slots, sends, recvs, count, mine, dev, started):
        slots[mine] = src[...]
        for t in range(1, count):
            peer = (mine + t) % count
            pltpu.make_async_remote_copy(
                src_ref=src, dst_ref=slots.at[peer], send_sem=sends.at[peer],
                recv_sem=recvs.at[peer], device_id=dev(peer), device_id_type=MESH).wait_recv()
        for cp in started:
            cp.wait_send()
        acc = slots[0]
        for s in range(1, count):
            acc = acc + slots[s]
        return acc

    first = start_gather(val_ref, slots1, send1, recv1, g1, me1, dev1)
    outgoing = []
    for t in range(1, GROUP):
        b = (j + t) % GROUP
        cp = pltpu.make_async_remote_copy(
            src_ref=blocks_ref.at[b], dst_ref=got.at[j], send_sem=send_o.at[b],
            recv_sem=recv_o.at[j], device_id=devg(b), device_id_type=MESH)
        cp.start()
        outgoing.append(cp)
    stage[...] = finish_gather(val_ref, slots1, send1, recv1, g1, me1, dev1, first)
    second = start_gather(stage, slots2, send2, recv2, n_col, k, dev2)
    sum_ref[...] = finish_gather(stage, slots2, send2, recv2, n_col, k, dev2, second)
    got[j] = blocks_ref[j]
    for t in range(1, GROUP):
        b = (j + t) % GROUP
        pltpu.make_async_remote_copy(
            src_ref=blocks_ref.at[b], dst_ref=got.at[b], send_sem=send_o.at[b],
            recv_sem=recv_o.at[b], device_id=devg(b), device_id_type=MESH).wait_recv()
    for cp in outgoing:
        cp.wait_send()
    out_ref[...] = got[...]


def finish(blocks, v, mesh_shape):
    n_col = mesh_shape["chan"] // GROUP
    n_f = mesh_shape["freq"]
    g1 = GROUP * n_f
    tile = jnp.full((8, 128), v, jnp.float32)
    vmem = pl.BlockSpec(memory_space=pltpu.VMEM)
    out, total = pl.pallas_call(
        functools.partial(tail_kernel, n_col, n_f),
        out_shape=(jax.ShapeDtypeStruct(blocks.shape, blocks.dtype),
                   jax.ShapeDtypeStruct((8, 128), jnp.float32)),
        in_specs=[vmem, vmem],
        out_specs=(vmem, vmem),
        scratch_shapes=[
            pltpu.VMEM(blocks.shape, blocks.dtype),
            pltpu.VMEM((g1, 8, 128), jnp.float32),
            pltpu.VMEM((n_col, 8, 128), jnp.float32),
            pltpu.VMEM((8, 128), jnp.float32),
            pltpu.SemaphoreType.DMA((GROUP,)),
            pltpu.SemaphoreType.DMA((GROUP,)),
            pltpu.SemaphoreType.DMA((g1,)),
            pltpu.SemaphoreType.DMA((g1,)),
            pltpu.SemaphoreType.DMA((n_col,)),
            pltpu.SemaphoreType.DMA((n_col,)),
        ],
        compiler_params=pltpu.CompilerParams(collective_id=0, has_side_effects=True),
    )(blocks, tile)
    return out, total[0, 0]


def shards(spectra, model, channel_ok, limits, mesh_shape):
    payload = jnp.concatenate([spectra, model], axis=2)
    fl, _, rows, bw = payload.shape
    peers = lax.axis_size("chan")
    me = lax.axis_index("chan")
    j = me % GROUP
    column = me // GROUP
    sub = fl // GROUP
    band_blocks = BAND // bw
    halo_cols = -(-band_blocks // GROUP)
    nblk = GROUP * (1 + halo_cols)

    ext = gather_columns(payload, halo_cols, HALVES)

    ok_all = channel_ok.astype(jnp.float32)
    ok_wide = jnp.concatenate([ok_all, ok_all[: nblk * bw]])
    ok_ext = lax.dynamic_slice_in_dim(ok_wide, column * GROUP * bw, nblk * bw).reshape(nblk, bw)
    lim = lax.dynamic_slice_in_dim(limits, column * GROUP, GROUP)

    first = ext[:, :GROUP]
    ok_first = ok_ext[:GROUP]
    misfit_part = jnp.zeros((8, bw), jnp.float32)
    near_acc = jnp.zeros((sub, GROUP, 2, W, bw), jnp.float32)
    far_acc = [jnp.zeros((sub, 2, W, bw), jnp.float32) for _ in range(nblk)]
    sent = []
    for s in range(band_blocks, -1, -1):
        second = ext[:, s : s + GROUP]
        piece_loss, near_terms, far_terms = pair_terms(
            first, second, ok_first, ok_ext[s : s + GROUP], lim, s
        )
        misfit_part = misfit_part + piece_loss
        near_acc = near_acc + near_terms
        for bb in range(GROUP):
            far_acc[s + bb] = far_acc[s + bb] + far_terms[:, bb]
        for h in range(1, halo_cols + 1):
            if s == max(GROUP * h - GROUP + 1, 0) and h * GROUP < nblk:
                done = jnp.stack(far_acc[h * GROUP : (h + 1) * GROUP], axis=1)
                done, ext = lax.optimization_barrier((done, ext))
                first = ext[:, :GROUP]
                sent.append(permute(done, shift_pairs(peers, GROUP * h)))
    misfit_sum = 0.5 * jnp.sum(misfit_part)
    adj = near_acc + jnp.stack(far_acc[:GROUP], axis=1)
    for part in sent:
        adj = adj + part

    blocks = jnp.transpose(adj, (1, 0, 2, 3, 4))
    back, misfit_total = finish(blocks, misfit_sum, mesh_shape)
    adjoint = back.reshape(fl, 2, W, bw) * (1.0 / W)

    misfit = misfit_total / float(F * bw * peers * BAND)
    return adjoint, misfit


def solution(mesh):
    mesh_shape = dict(mesh.shape)
    return jax.shard_map(
        lambda *a: shards(*a, mesh_shape),
        mesh=mesh,
        in_specs=(P("freq", None, None, "chan"), P("freq", None, None, "chan"), P(), P()),
        out_specs=(P("freq", None, None, "chan"), P()),
        check_vma=False,
    )
```

```python
import jax
import jax.numpy as jnp
from jax import lax
from jax.experimental import pallas as pl
from jax.experimental.pallas import tpu as pltpu
from jax.sharding import PartitionSpec as P
import functools

F = 256
W = 16
BAND = 1024
HALVES = 4
GROUP = 4


def permute(x, pairs):
    return lax.ppermute(x, "chan", pairs)


def shift_pairs(peers, by):
    return [(i, (i + by) % peers) for i in range(peers)]


def group_pairs(peers, t):
    return [(i, (i // GROUP) * GROUP + (i % GROUP + t) % GROUP) for i in range(peers)]


def exchange(chunks, j, peers):
    rel = jnp.roll(chunks, -j, axis=0)
    got = [rel[0]] + [permute(rel[t], group_pairs(peers, t)) for t in range(1, GROUP)]
    got = jnp.stack(got, axis=0)
    order = (j - jnp.arange(GROUP)) % GROUP
    return jnp.take(got, order, axis=0)


def pair_terms(first, second, ok_first, ok_second, limit_first, shift_blocks):
    fb, nb, _, row_count, block_width = first.shape
    row_scale = jnp.concatenate(
        [jnp.full((W,), 1.0 / W, jnp.float32), jnp.full((row_count - W,), -1.0, jnp.float32)]
    ).astype(jnp.bfloat16)
    scaled = first * row_scale[None, None, None, :, None]
    stacked_left = jnp.stack(
        [
            scaled.reshape(fb, nb, 2 * row_count, block_width),
            jnp.concatenate([scaled[:, :, 1], -scaled[:, :, 0]], axis=2),
        ],
        axis=2,
    )
    right_rows = second.reshape(fb, nb, 2 * row_count, block_width)
    cross_spec = jnp.einsum(
        "fbxrc,fbrd->fbxcd", stacked_left, right_rows, preferred_element_type=jnp.float32
    )
    row_index = lax.broadcasted_iota(jnp.int32, (block_width, block_width), 0)
    col_index = lax.broadcasted_iota(jnp.int32, (block_width, block_width), 1)
    offset = shift_blocks * block_width + col_index - row_index
    inside = ((offset[None] >= 1) & (offset[None] <= limit_first[:, None, None])).astype(jnp.float32)
    live_mask = ok_first[:, :, None] * ok_second[:, None, :] * inside
    residual = cross_spec * live_mask[None, :, None]
    squares = (residual * residual).reshape(-1, block_width // 8, 8, block_width)
    piece_loss = jnp.sum(squares, axis=(0, 1))
    rounded = residual.astype(jnp.bfloat16)
    far_spec = second[:, :, :, :W].reshape(fb, nb, 2 * W, block_width)
    near_spec = first[:, :, :, :W].reshape(fb, nb, 2 * W, block_width)
    toward = jnp.einsum("fbxcd,fbvd->fbxvc", rounded, far_spec, preferred_element_type=jnp.float32)
    first_real = toward[:, :, 0, :W] - toward[:, :, 1, W:]
    first_imag = toward[:, :, 0, W:] + toward[:, :, 1, :W]
    backward = jnp.einsum("fbxcd,fbvc->fbxvd", rounded, near_spec, preferred_element_type=jnp.float32)
    second_real = backward[:, :, 0, :W] + backward[:, :, 1, W:]
    second_imag = backward[:, :, 0, W:] - backward[:, :, 1, :W]
    return (
        piece_loss,
        jnp.stack([first_real, first_imag], axis=2),
        jnp.stack([second_real, second_imag], axis=2),
    )


MESH = pl.DeviceIdType.MESH

def head_kernel(n_halves, halo_cols, chunks_ref, out_ref, held, send_e, recv_e, send_h, recv_h, own_sem):
    c = lax.axis_index("chan")
    f = lax.axis_index("freq")
    peers = lax.axis_size("chan")
    k = c // GROUP
    j = c % GROUP

    def devg(b):
        return (k * GROUP + b, f)

    def devh(h, sign):
        return ((c + sign * GROUP * h) % peers, f)

    barrier = pltpu.get_barrier_semaphore()
    for t in range(1, GROUP):
        pl.semaphore_signal(barrier, 1, device_id=devg((j + t) % GROUP), device_id_type=MESH)
    for h in range(1, halo_cols + 1):
        pl.semaphore_signal(barrier, 1, device_id=devh(h, -1), device_id_type=MESH)
        pl.semaphore_signal(barrier, 1, device_id=devh(h, 1), device_id_type=MESH)
    pl.semaphore_wait(barrier, GROUP - 1 + 2 * halo_cols)

    sends = []
    locals_ = []
    for half in range(n_halves):
        for t in range(1, GROUP):
            b = (j + t) % GROUP
            cp = pltpu.make_async_remote_copy(
                src_ref=chunks_ref.at[b, half], dst_ref=held.at[half, 0, j],
                send_sem=send_e.at[half, b], recv_sem=recv_e.at[half, j],
                device_id=devg(b), device_id_type=MESH)
            cp.start()
            sends.append(cp)
        cp = pltpu.make_async_copy(chunks_ref.at[j, half], held.at[half, 0, j], own_sem.at[half])
        cp.start()
        locals_.append(cp)
    for half in range(n_halves):
        locals_[half].wait()
        for t in range(1, GROUP):
            b = (j + t) % GROUP
            pltpu.make_async_remote_copy(
                src_ref=chunks_ref.at[b, half], dst_ref=held.at[half, 0, b],
                send_sem=send_e.at[half, b], recv_sem=recv_e.at[half, b],
                device_id=devg(b), device_id_type=MESH).wait_recv()
        for h in range(1, halo_cols + 1):
            cp = pltpu.make_async_remote_copy(
                src_ref=held.at[half, 0], dst_ref=held.at[half, h],
                send_sem=send_h.at[half, h], recv_sem=recv_h.at[half, h],
                device_id=devh(h, -1), device_id_type=MESH)
            cp.start()
            sends.append(cp)
    for half in range(n_halves):
        for h in range(1, halo_cols + 1):
            pltpu.make_async_remote_copy(
                src_ref=held.at[half, 0], dst_ref=held.at[half, h],
                send_sem=send_h.at[half, h], recv_sem=recv_h.at[half, h],
                device_id=devh(h, 1), device_id_type=MESH).wait_recv()
    for cp in sends:
        cp.wait_send()
    for half in range(n_halves):
        for col in range(1 + halo_cols):
            for blk in range(GROUP):
                out_ref[half, :, col, blk] = held[half, col, blk]


def gather_columns(payload, halo_cols, n_halves):
    fl, two, rows, bw = payload.shape
    q = fl // GROUP // n_halves
    chunks = payload.reshape(GROUP, n_halves, q, two, rows, bw)
    shape = (n_halves, 1 + halo_cols, GROUP, q, two, rows, bw)
    vmem = pl.BlockSpec(memory_space=pltpu.VMEM)
    out_layout = (n_halves, q, 1 + halo_cols, GROUP, two, rows, bw)
    held = pl.pallas_call(
        functools.partial(head_kernel, n_halves, halo_cols),
        out_shape=jax.ShapeDtypeStruct(out_layout, payload.dtype),
        in_specs=[vmem],
        out_specs=vmem,
        scratch_shapes=[
            pltpu.VMEM(shape, payload.dtype),
            pltpu.SemaphoreType.DMA((n_halves, GROUP)),
            pltpu.SemaphoreType.DMA((n_halves, GROUP)),
            pltpu.SemaphoreType.DMA((n_halves, 1 + halo_cols)),
            pltpu.SemaphoreType.DMA((n_halves, 1 + halo_cols)),
            pltpu.SemaphoreType.DMA((n_halves,)),
        ],
        compiler_params=pltpu.CompilerParams(collective_id=1, has_side_effects=True),
    )(chunks)
    return held.reshape(n_halves * q, (1 + halo_cols) * GROUP, two, rows, bw)


def tail_kernel(n_col, n_f, blocks_ref, val_ref, out_ref, sum_ref,
                got, slots1, slots2, stage, send_o, recv_o, send1, recv1, send2, recv2):
    c = lax.axis_index("chan")
    f = lax.axis_index("freq")
    k = c // GROUP
    j = c % GROUP
    g1 = GROUP * n_f
    me1 = j * n_f + f

    def dev1(slot):
        return (k * GROUP + slot // n_f, slot % n_f)

    def dev2(col):
        return (col * GROUP + j, f)

    def devg(b):
        return (k * GROUP + b, f)

    barrier = pltpu.get_barrier_semaphore()
    for t in range(1, g1):
        pl.semaphore_signal(barrier, 1, device_id=dev1((me1 + t) % g1), device_id_type=MESH)
    for t in range(1, n_col):
        pl.semaphore_signal(barrier, 1, device_id=dev2((k + t) % n_col), device_id_type=MESH)
    pl.semaphore_wait(barrier, g1 - 1 + n_col - 1)

    def start_gather(src, slots, sends, recvs, count, mine, dev):
        out = []
        for t in range(1, count):
            peer = (mine + t) % count
            cp = pltpu.make_async_remote_copy(
                src_ref=src, dst_ref=slots.at[mine], send_sem=sends.at[peer],
                recv_sem=recvs.at[mine], device_id=dev(peer), device_id_type=MESH)
            cp.start()
            out.append(cp)
        return out

    def finish_gather(src, slots, sends, recvs, count, mine, dev, started):
        slots[mine] = src[...]
        for t in range(1, count):
            peer = (mine + t) % count
            pltpu.make_async_remote_copy(
                src_ref=src, dst_ref=slots.at[peer], send_sem=sends.at[peer],
                recv_sem=recvs.at[peer], device_id=dev(peer), device_id_type=MESH).wait_recv()
        for cp in started:
            cp.wait_send()
        acc = slots[0]
        for s in range(1, count):
            acc = acc + slots[s]
        return acc

    outgoing = []
    for t in range(1, GROUP):
        b = (j + t) % GROUP
        cp = pltpu.make_async_remote_copy(
            src_ref=blocks_ref.at[b], dst_ref=got.at[j], send_sem=send_o.at[b],
            recv_sem=recv_o.at[j], device_id=devg(b), device_id_type=MESH)
        cp.start()
        outgoing.append(cp)
    first = start_gather(val_ref, slots1, send1, recv1, g1, me1, dev1)
    stage[...] = finish_gather(val_ref, slots1, send1, recv1, g1, me1, dev1, first)
    second = start_gather(stage, slots2, send2, recv2, n_col, k, dev2)
    sum_ref[...] = finish_gather(stage, slots2, send2, recv2, n_col, k, dev2, second)
    got[j] = blocks_ref[j]
    for t in range(1, GROUP):
        b = (j + t) % GROUP
        pltpu.make_async_remote_copy(
            src_ref=blocks_ref.at[b], dst_ref=got.at[b], send_sem=send_o.at[b],
            recv_sem=recv_o.at[b], device_id=devg(b), device_id_type=MESH).wait_recv()
    for cp in outgoing:
        cp.wait_send()
    out_ref[...] = got[...]


def finish(blocks, v, mesh_shape):
    n_col = mesh_shape["chan"] // GROUP
    n_f = mesh_shape["freq"]
    g1 = GROUP * n_f
    tile = jnp.full((8, 128), v, jnp.float32)
    vmem = pl.BlockSpec(memory_space=pltpu.VMEM)
    out, total = pl.pallas_call(
        functools.partial(tail_kernel, n_col, n_f),
        out_shape=(jax.ShapeDtypeStruct(blocks.shape, blocks.dtype),
                   jax.ShapeDtypeStruct((8, 128), jnp.float32)),
        in_specs=[vmem, vmem],
        out_specs=(vmem, vmem),
        scratch_shapes=[
            pltpu.VMEM(blocks.shape, blocks.dtype),
            pltpu.VMEM((g1, 8, 128), jnp.float32),
            pltpu.VMEM((n_col, 8, 128), jnp.float32),
            pltpu.VMEM((8, 128), jnp.float32),
            pltpu.SemaphoreType.DMA((GROUP,)),
            pltpu.SemaphoreType.DMA((GROUP,)),
            pltpu.SemaphoreType.DMA((g1,)),
            pltpu.SemaphoreType.DMA((g1,)),
            pltpu.SemaphoreType.DMA((n_col,)),
            pltpu.SemaphoreType.DMA((n_col,)),
        ],
        compiler_params=pltpu.CompilerParams(collective_id=0, has_side_effects=True),
    )(blocks, tile)
    return out, total[0, 0]


def shards(spectra, model, channel_ok, limits, mesh_shape):
    payload = jnp.concatenate([spectra, model], axis=2)
    fl, _, rows, bw = payload.shape
    peers = lax.axis_size("chan")
    me = lax.axis_index("chan")
    j = me % GROUP
    column = me // GROUP
    sub = fl // GROUP
    band_blocks = BAND // bw
    halo_cols = -(-band_blocks // GROUP)
    nblk = GROUP * (1 + halo_cols)

    ext = gather_columns(payload, halo_cols, HALVES)

    ok_all = channel_ok.astype(jnp.float32)
    ok_wide = jnp.concatenate([ok_all, ok_all[: nblk * bw]])
    ok_ext = lax.dynamic_slice_in_dim(ok_wide, column * GROUP * bw, nblk * bw).reshape(nblk, bw)
    lim = lax.dynamic_slice_in_dim(limits, column * GROUP, GROUP)

    first = ext[:, :GROUP]
    ok_first = ok_ext[:GROUP]
    misfit_part = jnp.zeros((8, bw), jnp.float32)
    near_acc = jnp.zeros((sub, GROUP, 2, W, bw), jnp.float32)
    far_acc = [jnp.zeros((sub, 2, W, bw), jnp.float32) for _ in range(nblk)]
    sent = []
    for s in range(band_blocks, -1, -1):
        second = ext[:, s : s + GROUP]
        piece_loss, near_terms, far_terms = pair_terms(
            first, second, ok_first, ok_ext[s : s + GROUP], lim, s
        )
        misfit_part = misfit_part + piece_loss
        near_acc = near_acc + near_terms
        for bb in range(GROUP):
            far_acc[s + bb] = far_acc[s + bb] + far_terms[:, bb]
        for h in range(1, halo_cols + 1):
            if s == max(GROUP * h - GROUP + 1, 0) and h * GROUP < nblk:
                done = jnp.stack(far_acc[h * GROUP : (h + 1) * GROUP], axis=1)
                done, ext = lax.optimization_barrier((done, ext))
                first = ext[:, :GROUP]
                sent.append(permute(done, shift_pairs(peers, GROUP * h)))
    misfit_sum = 0.5 * jnp.sum(misfit_part)
    adj = near_acc + jnp.stack(far_acc[:GROUP], axis=1)
    for part in sent:
        adj = adj + part

    blocks = jnp.transpose(adj, (1, 0, 2, 3, 4))
    back, misfit_total = finish(blocks, misfit_sum, mesh_shape)
    adjoint = back.reshape(fl, 2, W, bw) * (1.0 / W)

    misfit = misfit_total / float(F * bw * peers * BAND)
    return adjoint, misfit


def solution(mesh):
    mesh_shape = dict(mesh.shape)
    return jax.shard_map(
        lambda *a: shards(*a, mesh_shape),
        mesh=mesh,
        in_specs=(P("freq", None, None, "chan"), P("freq", None, None, "chan"), P(), P()),
        out_specs=(P("freq", None, None, "chan"), P()),
        check_vma=False,
    )
```

```python
import jax
import jax.numpy as jnp
from jax import lax
from jax.experimental import pallas as pl
from jax.experimental.pallas import tpu as pltpu
from jax.sharding import PartitionSpec as P
import functools

F = 256
W = 16
BAND = 1024
HALVES = 4
GROUP = 4


def permute(x, pairs):
    return lax.ppermute(x, "chan", pairs)


def shift_pairs(peers, by):
    return [(i, (i + by) % peers) for i in range(peers)]


def group_pairs(peers, t):
    return [(i, (i // GROUP) * GROUP + (i % GROUP + t) % GROUP) for i in range(peers)]


def exchange(chunks, j, peers):
    rel = jnp.roll(chunks, -j, axis=0)
    got = [rel[0]] + [permute(rel[t], group_pairs(peers, t)) for t in range(1, GROUP)]
    got = jnp.stack(got, axis=0)
    order = (j - jnp.arange(GROUP)) % GROUP
    return jnp.take(got, order, axis=0)


def pair_terms(first, second, ok_first, ok_second, limit_first, shift_blocks):
    fb, nb, _, row_count, block_width = first.shape
    row_scale = jnp.concatenate(
        [jnp.full((W,), 1.0 / W, jnp.float32), jnp.full((row_count - W,), -1.0, jnp.float32)]
    ).astype(jnp.bfloat16)
    scaled = first * row_scale[None, None, None, :, None]
    stacked_left = jnp.stack(
        [
            scaled.reshape(fb, nb, 2 * row_count, block_width),
            jnp.concatenate([scaled[:, :, 1], -scaled[:, :, 0]], axis=2),
        ],
        axis=2,
    )
    right_rows = second.reshape(fb, nb, 2 * row_count, block_width)
    cross_spec = jnp.einsum(
        "fbxrc,fbrd->fbxcd", stacked_left, right_rows, preferred_element_type=jnp.float32
    )
    row_index = lax.broadcasted_iota(jnp.int32, (block_width, block_width), 0)
    col_index = lax.broadcasted_iota(jnp.int32, (block_width, block_width), 1)
    offset = shift_blocks * block_width + col_index - row_index
    inside = ((offset[None] >= 1) & (offset[None] <= limit_first[:, None, None])).astype(jnp.float32)
    live_mask = ok_first[:, :, None] * ok_second[:, None, :] * inside
    residual = cross_spec * live_mask[None, :, None]
    squares = (residual * residual).reshape(-1, block_width // 8, 8, block_width)
    piece_loss = jnp.sum(squares, axis=(0, 1))
    rounded = residual.astype(jnp.bfloat16)
    far_spec = second[:, :, :, :W].reshape(fb, nb, 2 * W, block_width)
    near_spec = first[:, :, :, :W].reshape(fb, nb, 2 * W, block_width)
    toward = jnp.einsum("fbxcd,fbvd->fbxvc", rounded, far_spec, preferred_element_type=jnp.float32)
    first_real = toward[:, :, 0, :W] - toward[:, :, 1, W:]
    first_imag = toward[:, :, 0, W:] + toward[:, :, 1, :W]
    backward = jnp.einsum("fbxcd,fbvc->fbxvd", rounded, near_spec, preferred_element_type=jnp.float32)
    second_real = backward[:, :, 0, :W] + backward[:, :, 1, W:]
    second_imag = backward[:, :, 0, W:] - backward[:, :, 1, :W]
    return (
        piece_loss,
        jnp.stack([first_real, first_imag], axis=2),
        jnp.stack([second_real, second_imag], axis=2),
    )


MESH = pl.DeviceIdType.MESH

def head_kernel(n_halves, halo_cols, chunks_ref, out_ref, held, send_e, recv_e, send_h, recv_h, own_sem):
    c = lax.axis_index("chan")
    f = lax.axis_index("freq")
    peers = lax.axis_size("chan")
    k = c // GROUP
    j = c % GROUP

    def devg(b):
        return (k * GROUP + b, f)

    def devh(h, sign):
        return ((c + sign * GROUP * h) % peers, f)

    barrier = pltpu.get_barrier_semaphore()
    for t in range(1, GROUP):
        pl.semaphore_signal(barrier, 1, device_id=devg((j + t) % GROUP), device_id_type=MESH)
    for h in range(1, halo_cols + 1):
        pl.semaphore_signal(barrier, 1, device_id=devh(h, -1), device_id_type=MESH)
        pl.semaphore_signal(barrier, 1, device_id=devh(h, 1), device_id_type=MESH)
    pl.semaphore_wait(barrier, GROUP - 1 + 2 * halo_cols)

    sends = []
    locals_ = []
    for half in range(n_halves):
        for t in range(1, GROUP):
            b = (j + t) % GROUP
            cp = pltpu.make_async_remote_copy(
                src_ref=chunks_ref.at[b, half], dst_ref=held.at[half, 0, j],
                send_sem=send_e.at[half, b], recv_sem=recv_e.at[half, j],
                device_id=devg(b), device_id_type=MESH)
            cp.start()
            sends.append(cp)
        cp = pltpu.make_async_copy(chunks_ref.at[j, half], held.at[half, 0, j], own_sem.at[half])
        cp.start()
        locals_.append(cp)
    for half in range(n_halves):
        locals_[half].wait()
        for t in range(1, GROUP):
            b = (j + t) % GROUP
            pltpu.make_async_remote_copy(
                src_ref=chunks_ref.at[b, half], dst_ref=held.at[half, 0, b],
                send_sem=send_e.at[half, b], recv_sem=recv_e.at[half, b],
                device_id=devg(b), device_id_type=MESH).wait_recv()
        for h in range(1, halo_cols + 1):
            cp = pltpu.make_async_remote_copy(
                src_ref=held.at[half, 0], dst_ref=held.at[half, h],
                send_sem=send_h.at[half, h], recv_sem=recv_h.at[half, h],
                device_id=devh(h, -1), device_id_type=MESH)
            cp.start()
            sends.append(cp)
    for half in range(n_halves):
        for h in range(1, halo_cols + 1):
            pltpu.make_async_remote_copy(
                src_ref=held.at[half, 0], dst_ref=held.at[half, h],
                send_sem=send_h.at[half, h], recv_sem=recv_h.at[half, h],
                device_id=devh(h, 1), device_id_type=MESH).wait_recv()
    for cp in sends:
        cp.wait_send()
    for half in range(n_halves):
        for col in range(1 + halo_cols):
            for blk in range(GROUP):
                out_ref[half, :, col, blk] = held[half, col, blk]


def gather_columns(payload, halo_cols, n_halves):
    fl, two, rows, bw = payload.shape
    q = fl // GROUP // n_halves
    chunks = payload.reshape(GROUP, n_halves, q, two, rows, bw)
    shape = (n_halves, 1 + halo_cols, GROUP, q, two, rows, bw)
    vmem = pl.BlockSpec(memory_space=pltpu.VMEM)
    out_layout = (n_halves, q, 1 + halo_cols, GROUP, two, rows, bw)
    held = pl.pallas_call(
        functools.partial(head_kernel, n_halves, halo_cols),
        out_shape=jax.ShapeDtypeStruct(out_layout, payload.dtype),
        in_specs=[vmem],
        out_specs=vmem,
        scratch_shapes=[
            pltpu.VMEM(shape, payload.dtype),
            pltpu.SemaphoreType.DMA((n_halves, GROUP)),
            pltpu.SemaphoreType.DMA((n_halves, GROUP)),
            pltpu.SemaphoreType.DMA((n_halves, 1 + halo_cols)),
            pltpu.SemaphoreType.DMA((n_halves, 1 + halo_cols)),
            pltpu.SemaphoreType.DMA((n_halves,)),
        ],
        compiler_params=pltpu.CompilerParams(collective_id=1, has_side_effects=True),
    )(chunks)
    return held.reshape(n_halves * q, (1 + halo_cols) * GROUP, two, rows, bw)


def tail_kernel(n_col, n_f, blocks_ref, val_ref, out_ref, sum_ref,
                got, slots1, slots2, stage, send_o, recv_o, send1, recv1, send2, recv2):
    c = lax.axis_index("chan")
    f = lax.axis_index("freq")
    k = c // GROUP
    j = c % GROUP
    g1 = GROUP * n_f
    me1 = j * n_f + f

    def dev1(slot):
        return (k * GROUP + slot // n_f, slot % n_f)

    def dev2(col):
        return (col * GROUP + j, f)

    def devg(b):
        return (k * GROUP + b, f)

    barrier = pltpu.get_barrier_semaphore()
    for t in range(1, g1):
        pl.semaphore_signal(barrier, 1, device_id=dev1((me1 + t) % g1), device_id_type=MESH)
    for t in range(1, n_col):
        pl.semaphore_signal(barrier, 1, device_id=dev2((k + t) % n_col), device_id_type=MESH)
    pl.semaphore_wait(barrier, g1 - 1 + n_col - 1)

    def start_gather(src, slots, sends, recvs, count, mine, dev):
        out = []
        for t in range(1, count):
            peer = (mine + t) % count
            cp = pltpu.make_async_remote_copy(
                src_ref=src, dst_ref=slots.at[mine], send_sem=sends.at[peer],
                recv_sem=recvs.at[mine], device_id=dev(peer), device_id_type=MESH)
            cp.start()
            out.append(cp)
        return out

    def finish_gather(src, slots, sends, recvs, count, mine, dev, started):
        slots[mine] = src[...]
        for t in range(1, count):
            peer = (mine + t) % count
            pltpu.make_async_remote_copy(
                src_ref=src, dst_ref=slots.at[peer], send_sem=sends.at[peer],
                recv_sem=recvs.at[peer], device_id=dev(peer), device_id_type=MESH).wait_recv()
        for cp in started:
            cp.wait_send()
        acc = slots[0]
        for s in range(1, count):
            acc = acc + slots[s]
        return acc

    first = start_gather(val_ref, slots1, send1, recv1, g1, me1, dev1)
    outgoing = []
    for t in range(1, GROUP):
        b = (j + t) % GROUP
        cp = pltpu.make_async_remote_copy(
            src_ref=blocks_ref.at[b], dst_ref=got.at[j], send_sem=send_o.at[b],
            recv_sem=recv_o.at[j], device_id=devg(b), device_id_type=MESH)
        cp.start()
        outgoing.append(cp)
    stage[...] = finish_gather(val_ref, slots1, send1, recv1, g1, me1, dev1, first)
    second = start_gather(stage, slots2, send2, recv2, n_col, k, dev2)
    sum_ref[...] = finish_gather(stage, slots2, send2, recv2, n_col, k, dev2, second)
    got[j] = blocks_ref[j]
    for t in range(1, GROUP):
        b = (j + t) % GROUP
        pltpu.make_async_remote_copy(
            src_ref=blocks_ref.at[b], dst_ref=got.at[b], send_sem=send_o.at[b],
            recv_sem=recv_o.at[b], device_id=devg(b), device_id_type=MESH).wait_recv()
    for cp in outgoing:
        cp.wait_send()
    out_ref[...] = got[...]


def finish(blocks, v, mesh_shape):
    n_col = mesh_shape["chan"] // GROUP
    n_f = mesh_shape["freq"]
    g1 = GROUP * n_f
    tile = jnp.full((8, 128), v, jnp.float32)
    vmem = pl.BlockSpec(memory_space=pltpu.VMEM)
    out, total = pl.pallas_call(
        functools.partial(tail_kernel, n_col, n_f),
        out_shape=(jax.ShapeDtypeStruct(blocks.shape, blocks.dtype),
                   jax.ShapeDtypeStruct((8, 128), jnp.float32)),
        in_specs=[vmem, vmem],
        out_specs=(vmem, vmem),
        scratch_shapes=[
            pltpu.VMEM(blocks.shape, blocks.dtype),
            pltpu.VMEM((g1, 8, 128), jnp.float32),
            pltpu.VMEM((n_col, 8, 128), jnp.float32),
            pltpu.VMEM((8, 128), jnp.float32),
            pltpu.SemaphoreType.DMA((GROUP,)),
            pltpu.SemaphoreType.DMA((GROUP,)),
            pltpu.SemaphoreType.DMA((g1,)),
            pltpu.SemaphoreType.DMA((g1,)),
            pltpu.SemaphoreType.DMA((n_col,)),
            pltpu.SemaphoreType.DMA((n_col,)),
        ],
        compiler_params=pltpu.CompilerParams(collective_id=0, has_side_effects=True),
    )(blocks, tile)
    return out, total[0, 0]


def shards(spectra, model, channel_ok, limits, mesh_shape):
    payload = jnp.concatenate([spectra, model], axis=2)
    fl, _, rows, bw = payload.shape
    peers = lax.axis_size("chan")
    me = lax.axis_index("chan")
    j = me % GROUP
    column = me // GROUP
    sub = fl // GROUP
    band_blocks = BAND // bw
    halo_cols = -(-band_blocks // GROUP)
    nblk = GROUP * (1 + halo_cols)

    ext = gather_columns(payload, halo_cols, HALVES)

    ok_all = channel_ok.astype(jnp.float32)
    ok_wide = jnp.concatenate([ok_all, ok_all[: nblk * bw]])
    ok_ext = lax.dynamic_slice_in_dim(ok_wide, column * GROUP * bw, nblk * bw).reshape(nblk, bw)
    lim = lax.dynamic_slice_in_dim(limits, column * GROUP, GROUP)

    first = ext[:, :GROUP]
    ok_first = ok_ext[:GROUP]
    misfit_part = jnp.zeros((8, bw), jnp.float32)
    near_acc = jnp.zeros((sub, GROUP, 2, W, bw), jnp.float32)
    far_acc = [jnp.zeros((sub, 2, W, bw), jnp.float32) for _ in range(nblk)]
    sent = []
    for s in range(band_blocks, -1, -1):
        second = ext[:, s : s + GROUP]
        piece_loss, near_terms, far_terms = pair_terms(
            first, second, ok_first, ok_ext[s : s + GROUP], lim, s
        )
        misfit_part = misfit_part + piece_loss
        near_acc = near_acc + near_terms
        for bb in range(GROUP):
            far_acc[s + bb] = far_acc[s + bb] + far_terms[:, bb]
        for h in range(1, halo_cols + 1):
            if s == max(GROUP * h - GROUP + 1, 0) and h * GROUP < nblk:
                done = jnp.stack(far_acc[h * GROUP : (h + 1) * GROUP], axis=1)
                done, ext = lax.optimization_barrier((done, ext))
                first = ext[:, :GROUP]
                sent.append(permute(done, shift_pairs(peers, GROUP * h)))
    misfit_sum = 0.5 * jnp.sum(misfit_part)
    adj = near_acc + jnp.stack(far_acc[:GROUP], axis=1)
    for part in sent:
        adj = adj + part

    blocks = jnp.transpose(adj, (1, 0, 2, 3, 4))
    back, misfit_total = finish(blocks, misfit_sum, mesh_shape)
    adjoint = back.reshape(fl, 2, W, bw) * (1.0 / W)

    misfit = misfit_total / float(F * bw * peers * BAND)
    return adjoint, misfit


def solution(mesh):
    mesh_shape = dict(mesh.shape)
    return jax.shard_map(
        lambda *a: shards(*a, mesh_shape),
        mesh=mesh,
        in_specs=(P("freq", None, None, "chan"), P("freq", None, None, "chan"), P(), P()),
        out_specs=(P("freq", None, None, "chan"), P()),
        check_vma=False,
    )
```

```python
import jax
import jax.numpy as jnp
from jax import lax
from jax.experimental import pallas as pl
from jax.experimental.pallas import tpu as pltpu
from jax.sharding import PartitionSpec as P
import functools

F = 256
W = 16
BAND = 1024
HALVES = 4
GROUP = 4


def permute(x, pairs):
    return lax.ppermute(x, "chan", pairs)


def shift_pairs(peers, by):
    return [(i, (i + by) % peers) for i in range(peers)]


def group_pairs(peers, t):
    return [(i, (i // GROUP) * GROUP + (i % GROUP + t) % GROUP) for i in range(peers)]


def exchange(chunks, j, peers):
    rel = jnp.roll(chunks, -j, axis=0)
    got = [rel[0]] + [permute(rel[t], group_pairs(peers, t)) for t in range(1, GROUP)]
    got = jnp.stack(got, axis=0)
    order = (j - jnp.arange(GROUP)) % GROUP
    return jnp.take(got, order, axis=0)


def pair_terms(first, second, ok_first, ok_second, limit_first, shift_blocks):
    fb, nb, _, row_count, block_width = first.shape
    row_scale = jnp.concatenate(
        [jnp.full((W,), 1.0 / W, jnp.float32), jnp.full((row_count - W,), -1.0, jnp.float32)]
    ).astype(jnp.bfloat16)
    scaled = first * row_scale[None, None, None, :, None]
    stacked_left = jnp.stack(
        [
            scaled.reshape(fb, nb, 2 * row_count, block_width),
            jnp.concatenate([scaled[:, :, 1], -scaled[:, :, 0]], axis=2),
        ],
        axis=2,
    )
    right_rows = second.reshape(fb, nb, 2 * row_count, block_width)
    cross_spec = jnp.einsum(
        "fbxrc,fbrd->fbxcd", stacked_left, right_rows, preferred_element_type=jnp.float32
    )
    row_index = lax.broadcasted_iota(jnp.int32, (block_width, block_width), 0)
    col_index = lax.broadcasted_iota(jnp.int32, (block_width, block_width), 1)
    offset = shift_blocks * block_width + col_index - row_index
    inside = ((offset[None] >= 1) & (offset[None] <= limit_first[:, None, None])).astype(jnp.float32)
    live_mask = ok_first[:, :, None] * ok_second[:, None, :] * inside
    residual = cross_spec * live_mask[None, :, None]
    squares = (residual * residual).reshape(-1, block_width // 8, 8, block_width)
    piece_loss = jnp.sum(squares, axis=(0, 1))
    rounded = residual.astype(jnp.bfloat16)
    far_spec = second[:, :, :, :W].reshape(fb, nb, 2 * W, block_width)
    near_spec = first[:, :, :, :W].reshape(fb, nb, 2 * W, block_width)
    toward = jnp.einsum("fbxcd,fbvd->fbxvc", rounded, far_spec, preferred_element_type=jnp.float32)
    first_real = toward[:, :, 0, :W] - toward[:, :, 1, W:]
    first_imag = toward[:, :, 0, W:] + toward[:, :, 1, :W]
    backward = jnp.einsum("fbxcd,fbvc->fbxvd", rounded, near_spec, preferred_element_type=jnp.float32)
    second_real = backward[:, :, 0, :W] + backward[:, :, 1, W:]
    second_imag = backward[:, :, 0, W:] - backward[:, :, 1, :W]
    return (
        piece_loss,
        jnp.stack([first_real, first_imag], axis=2),
        jnp.stack([second_real, second_imag], axis=2),
    )


MESH = pl.DeviceIdType.MESH

def head_kernel(n_halves, halo_cols, chunks_ref, out_ref, held, send_e, recv_e, send_h, recv_h, own_sem):
    c = lax.axis_index("chan")
    f = lax.axis_index("freq")
    peers = lax.axis_size("chan")
    k = c // GROUP
    j = c % GROUP

    def devg(b):
        return (k * GROUP + b, f)

    def devh(h, sign):
        return ((c + sign * GROUP * h) % peers, f)

    barrier = pltpu.get_barrier_semaphore()
    for t in range(1, GROUP):
        pl.semaphore_signal(barrier, 1, device_id=devg((j + t) % GROUP), device_id_type=MESH)
    for h in range(1, halo_cols + 1):
        pl.semaphore_signal(barrier, 1, device_id=devh(h, -1), device_id_type=MESH)
        pl.semaphore_signal(barrier, 1, device_id=devh(h, 1), device_id_type=MESH)
    pl.semaphore_wait(barrier, GROUP - 1 + 2 * halo_cols)

    sends = []
    locals_ = []
    for half in range(n_halves):
        for t in range(1, GROUP):
            b = (j + t) % GROUP
            cp = pltpu.make_async_remote_copy(
                src_ref=chunks_ref.at[b, half], dst_ref=held.at[half, 0, j],
                send_sem=send_e.at[half, b], recv_sem=recv_e.at[half, j],
                device_id=devg(b), device_id_type=MESH)
            cp.start()
            sends.append(cp)
        cp = pltpu.make_async_copy(chunks_ref.at[j, half], held.at[half, 0, j], own_sem.at[half])
        cp.start()
        locals_.append(cp)
    for half in range(n_halves):
        locals_[half].wait()
        for t in range(1, GROUP):
            b = (j + t) % GROUP
            pltpu.make_async_remote_copy(
                src_ref=chunks_ref.at[b, half], dst_ref=held.at[half, 0, b],
                send_sem=send_e.at[half, b], recv_sem=recv_e.at[half, b],
                device_id=devg(b), device_id_type=MESH).wait_recv()
        for h in range(halo_cols, 0, -1):
            cp = pltpu.make_async_remote_copy(
                src_ref=held.at[half, 0], dst_ref=held.at[half, h],
                send_sem=send_h.at[half, h], recv_sem=recv_h.at[half, h],
                device_id=devh(h, -1), device_id_type=MESH)
            cp.start()
            sends.append(cp)
    for half in range(n_halves):
        for h in range(1, halo_cols + 1):
            pltpu.make_async_remote_copy(
                src_ref=held.at[half, 0], dst_ref=held.at[half, h],
                send_sem=send_h.at[half, h], recv_sem=recv_h.at[half, h],
                device_id=devh(h, 1), device_id_type=MESH).wait_recv()
    for cp in sends:
        cp.wait_send()
    out_ref[...] = held[...]


def gather_columns(payload, halo_cols, n_halves):
    fl, two, rows, bw = payload.shape
    q = fl // GROUP // n_halves
    chunks = payload.reshape(GROUP, n_halves, q, two, rows, bw)
    shape = (n_halves, 1 + halo_cols, GROUP, q, two, rows, bw)
    vmem = pl.BlockSpec(memory_space=pltpu.VMEM)
    held = pl.pallas_call(
        functools.partial(head_kernel, n_halves, halo_cols),
        out_shape=jax.ShapeDtypeStruct(shape, payload.dtype),
        in_specs=[vmem],
        out_specs=vmem,
        scratch_shapes=[
            pltpu.VMEM(shape, payload.dtype),
            pltpu.SemaphoreType.DMA((n_halves, GROUP)),
            pltpu.SemaphoreType.DMA((n_halves, GROUP)),
            pltpu.SemaphoreType.DMA((n_halves, 1 + halo_cols)),
            pltpu.SemaphoreType.DMA((n_halves, 1 + halo_cols)),
            pltpu.SemaphoreType.DMA((n_halves,)),
        ],
        compiler_params=pltpu.CompilerParams(collective_id=1, has_side_effects=True),
    )(chunks)
    held = jnp.transpose(held, (0, 3, 1, 2, 4, 5, 6))
    return held.reshape(n_halves * q, (1 + halo_cols) * GROUP, two, rows, bw)


def tail_kernel(n_col, n_f, blocks_ref, val_ref, out_ref, sum_ref,
                got, slots1, slots2, stage, send_o, recv_o, send1, recv1, send2, recv2):
    c = lax.axis_index("chan")
    f = lax.axis_index("freq")
    k = c // GROUP
    j = c % GROUP
    g1 = GROUP * n_f
    me1 = j * n_f + f

    def dev1(slot):
        return (k * GROUP + slot // n_f, slot % n_f)

    def dev2(col):
        return (col * GROUP + j, f)

    def devg(b):
        return (k * GROUP + b, f)

    barrier = pltpu.get_barrier_semaphore()
    for t in range(1, g1):
        pl.semaphore_signal(barrier, 1, device_id=dev1((me1 + t) % g1), device_id_type=MESH)
    for t in range(1, n_col):
        pl.semaphore_signal(barrier, 1, device_id=dev2((k + t) % n_col), device_id_type=MESH)
    pl.semaphore_wait(barrier, g1 - 1 + n_col - 1)

    def start_gather(src, slots, sends, recvs, count, mine, dev):
        out = []
        for t in range(1, count):
            peer = (mine + t) % count
            cp = pltpu.make_async_remote_copy(
                src_ref=src, dst_ref=slots.at[mine], send_sem=sends.at[peer],
                recv_sem=recvs.at[mine], device_id=dev(peer), device_id_type=MESH)
            cp.start()
            out.append(cp)
        return out

    def finish_gather(src, slots, sends, recvs, count, mine, dev, started):
        slots[mine] = src[...]
        for t in range(1, count):
            peer = (mine + t) % count
            pltpu.make_async_remote_copy(
                src_ref=src, dst_ref=slots.at[peer], send_sem=sends.at[peer],
                recv_sem=recvs.at[peer], device_id=dev(peer), device_id_type=MESH).wait_recv()
        for cp in started:
            cp.wait_send()
        acc = slots[0]
        for s in range(1, count):
            acc = acc + slots[s]
        return acc

    first = start_gather(val_ref, slots1, send1, recv1, g1, me1, dev1)
    outgoing = []
    for t in range(1, GROUP):
        b = (j + t) % GROUP
        cp = pltpu.make_async_remote_copy(
            src_ref=blocks_ref.at[b], dst_ref=got.at[j], send_sem=send_o.at[b],
            recv_sem=recv_o.at[j], device_id=devg(b), device_id_type=MESH)
        cp.start()
        outgoing.append(cp)
    stage[...] = finish_gather(val_ref, slots1, send1, recv1, g1, me1, dev1, first)
    second = start_gather(stage, slots2, send2, recv2, n_col, k, dev2)
    sum_ref[...] = finish_gather(stage, slots2, send2, recv2, n_col, k, dev2, second)
    got[j] = blocks_ref[j]
    for t in range(1, GROUP):
        b = (j + t) % GROUP
        pltpu.make_async_remote_copy(
            src_ref=blocks_ref.at[b], dst_ref=got.at[b], send_sem=send_o.at[b],
            recv_sem=recv_o.at[b], device_id=devg(b), device_id_type=MESH).wait_recv()
    for cp in outgoing:
        cp.wait_send()
    out_ref[...] = got[...]


def finish(blocks, v, mesh_shape):
    n_col = mesh_shape["chan"] // GROUP
    n_f = mesh_shape["freq"]
    g1 = GROUP * n_f
    tile = jnp.full((8, 128), v, jnp.float32)
    vmem = pl.BlockSpec(memory_space=pltpu.VMEM)
    out, total = pl.pallas_call(
        functools.partial(tail_kernel, n_col, n_f),
        out_shape=(jax.ShapeDtypeStruct(blocks.shape, blocks.dtype),
                   jax.ShapeDtypeStruct((8, 128), jnp.float32)),
        in_specs=[vmem, vmem],
        out_specs=(vmem, vmem),
        scratch_shapes=[
            pltpu.VMEM(blocks.shape, blocks.dtype),
            pltpu.VMEM((g1, 8, 128), jnp.float32),
            pltpu.VMEM((n_col, 8, 128), jnp.float32),
            pltpu.VMEM((8, 128), jnp.float32),
            pltpu.SemaphoreType.DMA((GROUP,)),
            pltpu.SemaphoreType.DMA((GROUP,)),
            pltpu.SemaphoreType.DMA((g1,)),
            pltpu.SemaphoreType.DMA((g1,)),
            pltpu.SemaphoreType.DMA((n_col,)),
            pltpu.SemaphoreType.DMA((n_col,)),
        ],
        compiler_params=pltpu.CompilerParams(collective_id=0, has_side_effects=True),
    )(blocks, tile)
    return out, total[0, 0]


def shards(spectra, model, channel_ok, limits, mesh_shape):
    payload = jnp.concatenate([spectra, model], axis=2)
    fl, _, rows, bw = payload.shape
    peers = lax.axis_size("chan")
    me = lax.axis_index("chan")
    j = me % GROUP
    column = me // GROUP
    sub = fl // GROUP
    band_blocks = BAND // bw
    halo_cols = -(-band_blocks // GROUP)
    nblk = GROUP * (1 + halo_cols)

    ext = gather_columns(payload, halo_cols, HALVES)

    ok_all = channel_ok.astype(jnp.float32)
    ok_wide = jnp.concatenate([ok_all, ok_all[: nblk * bw]])
    ok_ext = lax.dynamic_slice_in_dim(ok_wide, column * GROUP * bw, nblk * bw).reshape(nblk, bw)
    lim = lax.dynamic_slice_in_dim(limits, column * GROUP, GROUP)

    first = ext[:, :GROUP]
    ok_first = ok_ext[:GROUP]
    misfit_part = jnp.zeros((8, bw), jnp.float32)
    near_acc = jnp.zeros((sub, GROUP, 2, W, bw), jnp.float32)
    far_acc = [jnp.zeros((sub, 2, W, bw), jnp.float32) for _ in range(nblk)]
    sent = []
    for s in range(band_blocks, -1, -1):
        second = ext[:, s : s + GROUP]
        piece_loss, near_terms, far_terms = pair_terms(
            first, second, ok_first, ok_ext[s : s + GROUP], lim, s
        )
        misfit_part = misfit_part + piece_loss
        near_acc = near_acc + near_terms
        for bb in range(GROUP):
            far_acc[s + bb] = far_acc[s + bb] + far_terms[:, bb]
        for h in range(1, halo_cols + 1):
            if s == max(GROUP * h - GROUP + 1, 0) and h * GROUP < nblk:
                done = jnp.stack(far_acc[h * GROUP : (h + 1) * GROUP], axis=1)
                done, ext = lax.optimization_barrier((done, ext))
                first = ext[:, :GROUP]
                sent.append(permute(done, shift_pairs(peers, GROUP * h)))
    misfit_sum = 0.5 * jnp.sum(misfit_part)
    adj = near_acc + jnp.stack(far_acc[:GROUP], axis=1)
    for part in sent:
        adj = adj + part

    blocks = jnp.transpose(adj, (1, 0, 2, 3, 4))
    back, misfit_total = finish(blocks, misfit_sum, mesh_shape)
    adjoint = back.reshape(fl, 2, W, bw) * (1.0 / W)

    misfit = misfit_total / float(F * bw * peers * BAND)
    return adjoint, misfit


def solution(mesh):
    mesh_shape = dict(mesh.shape)
    return jax.shard_map(
        lambda *a: shards(*a, mesh_shape),
        mesh=mesh,
        in_specs=(P("freq", None, None, "chan"), P("freq", None, None, "chan"), P(), P()),
        out_specs=(P("freq", None, None, "chan"), P()),
        check_vma=False,
    )
```
